256 devices in a mesh: gx: 16 (over z, x_hi), gy: 16 (over x_lo, y, core).
Axes of the slice: x: 4 (x_hi: 2, x_lo: 2; x = x_hi * 2 + x_lo), y: 4, z: 8, core: 2. Of those that a mesh axis runs over, the one named last changes fastest.
Arguments:
- fine_e: float32 [3, 16, 96, 6144], P(None, None, 'gx', 'gy'), may hold values from -6 to 6
- fine_h: float32 [3, 16, 96, 6144], P(None, None, 'gx', 'gy'), may hold values from -6 to 6
- drude_current: float32 [3, 16, 96, 6144], P(None, None, 'gx', 'gy'), may hold values from -4 to 4
- lorentz_pol: float32 [3, 16, 96, 6144], P(None, None, 'gx', 'gy'), may hold values from -4 to 4
- lorentz_rate: float32 [3, 16, 96, 6144], P(None, None, 'gx', 'gy'), may hold values from -4 to 4
- material: int32 [16, 96, 6144], P(None, 'gx', 'gy'), may hold values from 0 to 7
- permittivity: float32 [8], replicated, may hold values from 1 to 4
- plasma: float32 [8], replicated, may hold values from 0.2 to 1.5
- damping: float32 [8], replicated, may hold values from 0.05 to 1
- strength: float32 [8], replicated, may hold values from 0.5 to 4
- resonance: float32 [8], replicated, may hold values from 0.3 to 1.2
- linewidth: float32 [8], replicated, may hold values from 0.05 to 0.5
- coarse_e: float32 [3, 16, 32, 2048], P(None, None, 'gx', 'gy'), may hold values from -6 to 6
- coarse_h: float32 [3, 16, 32, 2048], P(None, None, 'gx', 'gy'), may hold values from -6 to 6
- coarse_material: int32 [16, 32, 2048], P(None, 'gx', 'gy'), may hold values from 0 to 7
- coarse_prior: float32 [2, 32, 2048], P(None, 'gx', 'gy'), may hold values from -6 to 6
Outputs:
- fine_e_out: float32 [3, 16, 96, 6144], P(None, None, 'gx', 'gy')
- fine_h_out: float32 [3, 16, 96, 6144], P(None, None, 'gx', 'gy')
- current_out: float32 [3, 16, 96, 6144], P(None, None, 'gx', 'gy')
- pol_out: float32 [3, 16, 96, 6144], P(None, None, 'gx', 'gy')
- rate_out: float32 [3, 16, 96, 6144], P(None, None, 'gx', 'gy')
- coarse_e_out: float32 [3, 16, 32, 2048], P(None, None, 'gx', 'gy')
- coarse_h_out: float32 [3, 16, 32, 2048], P(None, None, 'gx', 'gy')
The draws below stay inside these ranges and needn't reach their ends.
All inputs are finite; a program needn't handle non-finite values.
Results may differ from the reference program's by a relative error of at most 0.0001.
Values sent between devices are 32-bit elements; how exact they have to be, the bound alone decides.
No kernel may reach another device: no remote copies, remote signals or barrier semaphores. Data moves between devices by JAX's collectives and lax.ppermute only.
A program may use at most 128 MiB of HBM per device.

```python
import math
import jax
import jax.numpy as jnp

NZ = 16
NZC = 16
RATIO = 3
STEPS = 3
M = 8
NX = 96
NY = 6144
XC = 32
YC = 2048


def with_ends(entries, stream_key, smallest, high):
    dims = entries.shape
    place = [jax.random.randint(jax.random.fold_in(stream_key, axis), (), 0, dims[axis]) for axis in range(len(dims))]
    entries = entries.at[tuple(place)].set(smallest)
    longest = dims.index(max(dims))
    place[longest] = (place[longest] + 1) % dims[longest]
    return entries.at[tuple(place)].set(high)


def block_scale(rng, shape, split, smallest, top_value):
    factor_of, own = 1.0, jax.random.fold_in(rng, 6)
    for position, blocks in split:
        steps = jnp.exp(jax.random.uniform(jax.random.fold_in(own, position), (blocks,), jnp.float32, smallest / len(split), top_value / len(split)))
        factor_of = factor_of * jnp.repeat(steps, shape[position] // blocks).reshape([-1 if axis == position else 1 for axis in range(len(shape))])
    return factor_of


def gaussian(own_key, extent, width, bound, cuts=(), dtype=jnp.bfloat16):
    entries = jax.random.normal(own_key, extent, jnp.float32) * width
    if len(cuts) > 0:
        entries = block_scale(own_key, extent, cuts, -0.22, 0.18) * entries
    return jnp.clip(entries, min=-bound, max=bound).astype(dtype)


def setup_inputs(seed: int = 0) -> dict:
    key_of = jax.random.split(jax.random.key(seed), 17)
    return {
        "fine_e": gaussian(key_of[0], (3, NZ, NX, NY), 1.0, 6.0, ((2, 16), (3, 16)), jnp.float32),
        "fine_h": gaussian(key_of[1], (3, NZ, NX, NY), 1.0, 6.0, ((2, 16), (3, 16)), jnp.float32),
        "drude_current": gaussian(key_of[2], (3, NZ, NX, NY), 0.5, 4.0, ((2, 16), (3, 16)), jnp.float32),
        "lorentz_pol": gaussian(key_of[3], (3, NZ, NX, NY), 0.5, 4.0, ((2, 16), (3, 16)), jnp.float32),
        "lorentz_rate": gaussian(key_of[4], (3, NZ, NX, NY), 0.5, 4.0, ((2, 16), (3, 16)), jnp.float32),
        "material": with_ends(jax.random.randint(key_of[5], (NZ, NX, NY), 0, M), jax.random.fold_in(key_of[5], 1), 0, M - 1).astype(jnp.int32),
        "permittivity": jnp.clip(jax.random.uniform(key_of[6], (M,), jnp.float32, 1.0, 4.0), 1.0, 4.0),
        "plasma": jnp.clip(jnp.exp(jax.random.uniform(key_of[7], (M,), jnp.float32, math.log(0.2), math.log(1.5))), 0.2, 1.5),
        "damping": jnp.clip(jnp.exp(jax.random.uniform(key_of[8], (M,), jnp.float32, math.log(0.05), math.log(1.0))), 0.05, 1.0),
        "strength": jnp.clip(jnp.exp(jax.random.uniform(key_of[9], (M,), jnp.float32, math.log(0.5), math.log(4.0))), 0.5, 4.0),
        "resonance": jnp.clip(jnp.exp(jax.random.uniform(key_of[10], (M,), jnp.float32, math.log(0.3), math.log(1.2))), 0.3, 1.2),
        "linewidth": jnp.clip(jnp.exp(jax.random.uniform(key_of[11], (M,), jnp.float32, math.log(0.05), math.log(0.5))), 0.05, 0.5),
        "coarse_e": gaussian(key_of[12], (3, NZC, XC, YC), 1.0, 6.0, ((2, 16), (3, 16)), jnp.float32),
        "coarse_h": gaussian(key_of[13], (3, NZC, XC, YC), 1.0, 6.0, ((2, 16), (3, 16)), jnp.float32),
        "coarse_material": with_ends(jax.random.randint(key_of[14], (NZC, XC, YC), 0, M), jax.random.fold_in(key_of[14], 1), 0, M - 1).astype(jnp.int32),
        "coarse_prior": gaussian(key_of[15], (2, XC, YC), 1.0, 6.0, ((1, 16), (2, 16)), jnp.float32),
    }


COURANT = 0.5
TIMESTEP = 0.5


def coefficients(permittivity, plasma, damping, strength, resonance, linewidth):
    half_step = 0.5 * TIMESTEP
    return jnp.stack([
        TIMESTEP / permittivity,
        (1.0 - damping * half_step) / (1.0 + damping * half_step),
        plasma * plasma * TIMESTEP / (1.0 + damping * half_step),
        (1.0 - linewidth * half_step) / (1.0 + linewidth * half_step),
        TIMESTEP * resonance * resonance / (1.0 + linewidth * half_step),
        strength,
    ])


def roll_forward(field):
    return jnp.roll(field[1:3], -1, 2), jnp.roll(field[0::2], -1, 3)


def roll_backward(field):
    return jnp.roll(field[1:3], 1, 2), jnp.roll(field[0::2], 1, 3)


def curl_of_e(field, above_top, forward):
    upper_x, upper_y = forward(field)
    higher = jnp.concatenate([field[0:2, 1:], above_top[:, None]], 1)
    curl_x = (upper_y[1] - field[2]) - (higher[1] - field[1])
    curl_y = (higher[0] - field[0]) - (upper_x[1] - field[2])
    curl_z = (upper_x[0] - field[1]) - (upper_y[0] - field[0])
    return jnp.stack([curl_x, curl_y, curl_z])


def curl_of_h(field, below_bottom, backward):
    lower_x, lower_y = backward(field)
    deeper = jnp.concatenate([below_bottom[:, None], field[0:2, :-1]], 1)
    curl_x = (field[2] - lower_y[1]) - (field[1] - deeper[1])
    curl_y = (field[0] - deeper[0]) - (field[2] - lower_x[1])
    curl_z = (field[1] - lower_x[0]) - (field[0] - lower_y[0])
    return jnp.stack([curl_x, curl_y, curl_z])


def prolong(plane):
    count, rows_c, cols_c = plane.shape
    spread = jnp.broadcast_to(plane[:, :, None, :, None], (count, rows_c, RATIO, cols_c, RATIO))
    return spread.reshape(count, rows_c * RATIO, cols_c * RATIO)


def restrict(plane):
    count, rows_f, cols_f = plane.shape
    blocks = plane.reshape(count, rows_f // RATIO, RATIO, cols_f // RATIO, RATIO)
    return jnp.sum(blocks, axis=(2, 4)) / float(RATIO * RATIO * RATIO)


def dispersive(electric, magnetic, current, polarization, velocity, coefficient, backward):
    below_bottom = jnp.zeros((2,) + electric.shape[2:], jnp.float32)
    curl = curl_of_h(magnetic, below_bottom, backward)
    velocity = coefficient[3] * velocity + coefficient[4] * (coefficient[5] * electric - polarization)
    current = coefficient[1] * current + coefficient[2] * electric
    polarization = polarization + TIMESTEP * velocity
    electric = electric + coefficient[0] * (curl - current - velocity)
    return electric, current, polarization, velocity


def reference(fine_e, fine_h, drude_current, lorentz_pol, lorentz_rate, material, permittivity, plasma, damping, strength, resonance, linewidth, coarse_e, coarse_h, coarse_material, coarse_prior):
    material_table = coefficients(permittivity, plasma, damping, strength, resonance, linewidth)
    coefficient = material_table[:, material]
    inverse = (COURANT / permittivity)[coarse_material]
    electric, magnetic = fine_e, fine_h
    current, polarization, velocity = drude_current, lorentz_pol, lorentz_rate
    previous = coarse_prior
    for coarse_step in range(STEPS):
        interface = coarse_e[0:2, 0]
        increment = (interface - previous) / RATIO
        coarse_h = coarse_h - COURANT * curl_of_e(coarse_e, jnp.zeros_like(interface), roll_forward)
        summed = jnp.zeros((2,) + material.shape[1:], jnp.float32)
        for substep in range(RATIO):
            above_top = prolong(interface + substep * increment)
            magnetic = magnetic - COURANT * curl_of_e(electric, above_top, roll_forward)
            summed = summed + magnetic[0:2, -1]
            electric, current, polarization, velocity = dispersive(electric, magnetic, current, polarization, velocity, coefficient, roll_backward)
        coarse_e = coarse_e + inverse * curl_of_h(coarse_h, restrict(summed), roll_backward)
        previous = interface
    return electric, magnetic, current, polarization, velocity, coarse_e, coarse_h
```

```python
import functools

import jax
import jax.numpy as jnp
from jax import lax
from jax.experimental import pallas as pl
from jax.experimental.pallas import tpu as pltpu
from jax.sharding import PartitionSpec as P

RATIO = 3
STEPS = 3
COURANT = 0.5
TIMESTEP = 0.5

Z = 16
ROWS = 6
OWN = 384
W = 256
CROWS = 2
CW = 128
GHOST = 9
CGHOST = 3
TILES = ((0, 1), (1, 2))
F32 = jnp.float32


def rolled(value, shift, axis):
    shift %= value.shape[axis]
    return value if shift == 0 else pltpu.roll(value, shift, axis)


def lanes(shape):
    return lax.broadcasted_iota(jnp.int32, shape, len(shape) - 1)


def right(value):
    return rolled(value, -1, 1)


def left(value):
    return rolled(value, 1, 1)


def above(value, top):
    sublane = lax.broadcasted_iota(jnp.int32, value.shape, 0)
    return jnp.where(sublane == Z - 1, top, rolled(value, -1, 0))


def below(value, bottom):
    sublane = lax.broadcasted_iota(jnp.int32, value.shape, 0)
    return jnp.where(sublane == 0, bottom, rolled(value, 1, 0))


def minus(first, second):
    if first is None:
        return None if second is None else -second
    return first if second is None else first - second


def h_row(h, e, following, top, wanted=(0, 1, 2)):
    ex, ey, ez = e
    next_y, next_z = following
    out = [None, None, None]
    if 0 in wanted:
        out[0] = h[0] - COURANT * ((right(ez) - ez) - (above(ey, top[1]) - ey))
    if 1 in wanted:
        out[1] = h[1] - COURANT * ((above(ex, top[0]) - ex) - minus(next_z, ez))
    if 2 in wanted:
        out[2] = h[2] - COURANT * (minus(next_y, ey) - (right(ex) - ex))
    return out


def curl_h(h, preceding, bottom, wanted=(0, 1, 2)):
    hx, hy, hz = h
    prev_y, prev_z = preceding
    out = [None, None, None]
    if 0 in wanted:
        out[0] = (hz - left(hz)) - (hy - below(hy, bottom[1]))
    if 1 in wanted:
        out[1] = (hx - below(hx, bottom[0])) - minus(hz, prev_z)
    if 2 in wanted:
        out[2] = minus(hy, prev_y) - (hx - left(hx))
    return out


def e_row(e, h, preceding, j, p, v, c, wanted=(0, 1, 2)):
    curl = curl_h(h, preceding, (0.0, 0.0), wanted)
    e2, j2, p2, v2 = [None] * 3, [None] * 3, [None] * 3, [None] * 3
    for k in wanted:
        v2[k] = c[3] * v[k] + c[4] * (c[5] * e[k] - p[k])
        j2[k] = c[1] * j[k] + c[2] * e[k]
        p2[k] = p[k] + TIMESTEP * v2[k]
        e2[k] = e[k] + c[0] * (curl[k] - j2[k] - v2[k])
    return e2, j2, p2, v2


def y_slots():
    entries = [("f", a, k, x, GHOST) for a in range(5) for k in range(3) for x in range(ROWS)]
    entries += [("m", 0, 0, x, GHOST) for x in range(ROWS)]
    entries += [("c", a, k, r, CGHOST) for a in range(2) for k in range(3) for r in range(CROWS)]
    entries += [("cm", 0, 0, r, CGHOST) for r in range(CROWS)]
    entries += [("prior", 0, 0, 0, CGHOST)]
    slots, plane, offset = {}, 0, 0
    for *key, width in entries:
        if offset + width > 128:
            plane, offset = plane + 1, 0
        slots[tuple(key)] = (plane, offset, width)
        offset += width
    return slots, plane + 1


Y_SLOTS, Y_PLANES = y_slots()


def coarse_row(ref, k, r):
    return ref[k, pl.ds(r, Z, stride=CROWS), :]


def pack_y_kernel(*refs):
    fields, (material, ce_in, ch_in, cmat_in, prior_in) = refs[0:5], refs[5:10]
    to_left, to_right, ce, ch, cmat, prior = refs[10:16]
    firsts, lasts, mats, sems = refs[16:20]
    pairs = []
    for a in range(5):
        pairs.append((fields[a].at[:, :, :, 0:128], firsts.at[a]))
        pairs.append((fields[a].at[:, :, :, OWN - 128 : OWN], lasts.at[a]))
    pairs.append((material.at[:, :, 0:128], mats.at[0]))
    pairs.append((material.at[:, :, OWN - 128 : OWN], mats.at[1]))
    pairs += [(ce_in, ce), (ch_in, ch), (cmat_in, cmat), (prior_in, prior)]
    copies = [pltpu.make_async_copy(src, dst, sems.at[i]) for i, (src, dst) in enumerate(pairs)]
    for copy in copies:
        copy.start()
    for copy in copies:
        copy.wait()
    lane = lanes((Z, 128))
    built = {}
    for key, (plane, offset, width) in Y_SLOTS.items():
        kind, a, k, x = key
        if kind == "f":
            first, last = firsts[a, k, x], lasts[a, k, x]
        elif kind == "m":
            first, last = mats[0, x].astype(F32), mats[1, x].astype(F32)
        elif kind == "c":
            first = last = coarse_row((ce, ch)[a], k, x)
        elif kind == "cm":
            first = last = cmat[pl.ds(x, Z, stride=CROWS), :].astype(F32)
        else:
            first = last = jnp.concatenate([prior[...]] * (Z // 4), 0)
        pair = (rolled(first, offset, 1), rolled(last, offset + width, 1))
        if plane in built:
            keep = lane < offset
            pair = tuple(jnp.where(keep, old, new) for old, new in zip(built[plane], pair))
        built[plane] = pair
    for plane, (one, other) in built.items():
        to_left[plane] = one
        to_right[plane] = other


def with_ghosts(half, message, key, tile):
    plane, offset, width = Y_SLOTS[key]
    lane = lanes((Z, 128))
    if half == 0:
        return jnp.where(lane < 96, tile, rolled(message[plane], -offset - width, 1))
    return jnp.where(lane < 32, rolled(message[plane], -offset, 1), tile)


def load_kernel(*refs):
    own, material_in, tab = refs[0:5], refs[5], refs[6]
    states = (refs[7:12], refs[12:17])
    c_halves, mat_halves = refs[17:19], refs[19:21]
    material, sems = refs[21:23]
    first = pltpu.make_async_copy(material_in, material, sems.at[10])
    first.start()
    copies = []
    for half in range(2):
        for a in range(5):
            source = own[a].at[:, :, :, 128 * half : 128 * half + W]
            copies.append(pltpu.make_async_copy(source, states[half][a], sems.at[5 * half + a]))
            copies[-1].start()
    first.wait()
    for x in range(ROWS):
        for half in range(2):
            mat_halves[half][x] = material[x, :, 128 * half : 128 * half + W].astype(F32)
        for tile in range(3):
            index = material[x, :, 128 * tile : 128 * (tile + 1)]
            for k in range(6):
                value = lookup(tab, k, index)
                for half in range(2):
                    if tile in TILES[half]:
                        local_tile = TILES[half].index(tile)
                        c_halves[half][k, x, :, 128 * local_tile : 128 * (local_tile + 1)] = value
    for copy in copies:
        copy.wait()


E_ITEMS = [(("e", t, k), 9 - t, 8 - t, True) for t in range(RATIO) for k in (1, 2)]
H_ITEMS = [(("h", t, k), 8 - t, 8 - t, True) for t in range(RATIO) for k in (1, 2)]
COARSE_ITEMS = [(("c", 0, k), CGHOST, CGHOST, False) for k in (1, 2)]
MATERIAL_ITEM = [(("m", 0, 0), 8, 8, True)]


def x_places(half, items):
    places, half_slots, plane, offset = {}, [], 1, 0
    for name, lefts, rights, fine in items:
        mixed = (1 - half) if fine else 0
        segments = []
        if fine:
            segments.append((half, 0, plane, 0, 128))
            plane += 1
        if not half_slots:
            half_slots = [(plane, 0), (plane, 64)]
            plane += 1
        own_lane = 64 * half
        segments.append((mixed, own_lane, *half_slots.pop(0), 64))
        left_lane = 64 - lefts if half else 128 - lefts
        right_lane = 0 if half else 64
        for lane, length in ((left_lane, lefts), (right_lane, rights)):
            segments.append((mixed, lane, 0, offset, length))
            offset += length
        places[name] = segments
    assert offset <= 128
    return places, plane


def write_x(half, items, values):
    places, planes = x_places(half, items)
    lane = lanes((Z, 128))
    built_planes = []
    for plane in range(planes):
        parts = sorted(
            (there, name, tile, start)
            for name, segments in places.items()
            for tile, start, where, there, _ in segments
            if where == plane
        )
        built = None
        for there, name, tile, start in parts:
            value = rolled(values[name][:, 128 * tile : 128 * (tile + 1)], there - start, 1)
            built = value if built is None else jnp.where(lane < there, built, value)
        built_planes.append(built)
    return built_planes


def read_x(ref, half, items, name):
    lane = lanes((Z, 128))
    built = {}
    for tile, start, plane, there, _ in sorted(x_places(half, items)[0][name]):
        value = rolled(ref[plane], start - there, 1)
        built[tile] = value if tile not in built else jnp.where(lane < start, built[tile], value)
    return jnp.concatenate([built[tile] for tile in sorted(built)], 1)


def x_items(first):
    extra = MATERIAL_ITEM if first else []
    return E_ITEMS + COARSE_ITEMS + extra, H_ITEMS + COARSE_ITEMS + extra


def gather(value, index):
    return jnp.take_along_axis(value, index, axis=1, mode="promise_in_bounds")


def prolong_lanes(half, value):
    lane = lanes((8, 128))
    third = lambda number: (number * 21846) >> 16
    if half == 0:
        indices = [third(lane), jnp.where(lane < 96, third(lane + 128), 128 - third(130 - lane))]
    else:
        indices = [jnp.where(lane < 32, third(lane), third(lane + 128)), third(lane + 256)]
    return jnp.concatenate([gather(value, index) for index in indices], 1)


def restrict_lanes(half, value):
    three = value + rolled(value, -1, 1) + rolled(value, -2, 1)
    lane = lanes((8, 128))
    index = (lane * RATIO) & 127
    tiles = [gather(three[:, 128 * tile : 128 * (tile + 1)], index) for tile in range(2)]
    in_first = lane * RATIO < (128 if half == 0 else 256)
    return jnp.where(in_first, tiles[0], tiles[1]) * (1.0 / RATIO**3)


def sort_messages(received, sorted_refs):
    even = lax.rem(lax.axis_index("gx"), 2) == 0
    first, second = received
    from_left, from_right = sorted_refs
    for plane in range(first.shape[0]):
        from_left[plane] = jnp.where(even, second[plane], first[plane])
        from_right[plane] = jnp.where(even, first[plane], second[plane])
    return from_left, from_right


def interface_rows(ce):
    return jnp.concatenate([ce[k, r][0:1] for k in range(2) for r in range(CROWS)], 0)


def top_plane(pl_ref, x, t):
    r = x // RATIO
    out = []
    for k in range(2):
        row = 2 * k + r
        value = pl_ref[row : row + 1, :]
        if t:
            value = value + float(t) * pl_ref[4 + row : 5 + row, :]
        out.append(value)
    return out


def lookup(tab, row, index):
    entry = jnp.broadcast_to(tab[row : row + 1, :], (8, 128))
    rows = []
    for z in range(0, Z, 8):
        rows.append(
            jnp.concatenate(
                [
                    gather(entry, index[z : z + 8, lane : lane + 128])
                    for lane in range(0, index.shape[1], 128)
                ],
                1,
            )
        )
    return jnp.concatenate(rows, 0)


def row_of(ref, x):
    return [ref[k, x] for k in range(3)]


def send_edges(half, first, fields, c, ce, ch, pl_ref, mat, to_first, to_second):
    fe, fh, fj, fp, fv = fields
    none = (None, None)
    e_items, h_items = x_items(first)
    coef = lambda x: [c[k, x] for k in range(6)]
    states = lambda x: (row_of(fj, x), row_of(fp, x), row_of(fv, x))
    e0 = {x: row_of(fe, x) for x in range(ROWS)}
    low, high = {}, {}

    for k in (1, 2):
        low["e", 0, k] = e0[0][k]
    h1 = {x: h_row(row_of(fh, x), e0[x], e0[x + 1][1:], top_plane(pl_ref, x, 0)) for x in (0, 1)}
    e1, s1 = {}, {}
    e1[0], *s1[0] = e_row(e0[0], h1[0], none, *states(0), coef(0))
    e1[1], *s1[1] = e_row(e0[1], h1[1], h1[0][1:], *states(1), coef(1), (1, 2))
    h2 = h_row(h1[0], e1[0], e1[1][1:], top_plane(pl_ref, 0, 1))
    e2 = e_row(e1[0], h2, none, *s1[0], coef(0), (1, 2))[0]
    for k in (1, 2):
        low["e", 1, k] = e1[0][k]
        low["e", 2, k] = e2[k]
        low["c", 0, k] = ce[k, 0]

    a, b, d = ROWS - 3, ROWS - 2, ROWS - 1
    h1 = {
        a: h_row(row_of(fh, a), e0[a], e0[b][1:], top_plane(pl_ref, a, 0), (1, 2)),
        b: h_row(row_of(fh, b), e0[b], e0[d][1:], top_plane(pl_ref, b, 0)),
        d: h_row(row_of(fh, d), e0[d], none, top_plane(pl_ref, d, 0)),
    }
    e1, s1 = {}, {}
    e1[b], *s1[b] = e_row(e0[b], h1[b], h1[a][1:], *states(b), coef(b))
    e1[d], *s1[d] = e_row(e0[d], h1[d], h1[b][1:], *states(d), coef(d))
    h2 = {
        b: h_row(h1[b], e1[b], e1[d][1:], top_plane(pl_ref, b, 1), (1, 2)),
        d: h_row(h1[d], e1[d], none, top_plane(pl_ref, d, 1)),
    }
    e2 = e_row(e1[d], h2[d], h2[b][1:], *s1[d], coef(d))[0]
    h3 = h_row(h2[d], e2, none, top_plane(pl_ref, d, 2), (1, 2))
    ch_last = h_row(row_of(ch, CROWS - 1), row_of(ce, CROWS - 1), none, (0.0, 0.0), (1, 2))
    for k in (1, 2):
        high["h", 0, k] = h1[d][k]
        high["h", 1, k] = h2[d][k]
        high["h", 2, k] = h3[k]
        high["c", 0, k] = ch_last[k]
    if first:
        low["m", 0, 0] = mat[0]
        high["m", 0, 0] = mat[ROWS - 1]
    even = lax.rem(lax.axis_index("gx"), 2) == 0
    for first_part, second_part, plane in zip(write_x(half, h_items, high), write_x(half, e_items, low), range(99)):
        to_first[plane] = jnp.where(even, first_part, second_part)
        to_second[plane] = jnp.where(even, second_part, first_part)


def start_kernel(half, *refs):
    fields_in, (c_in, mat_in, ce_in, ch_in, cmat, prior, tab, message) = refs[0:5], refs[5:13]
    fields, (c, ce, ch, inv, pl_ref, to_first, to_second, mat) = refs[13:18], refs[18:26]
    outer = slice(128, 256) if half == 0 else slice(0, 128)
    inner = slice(0, 128) if half == 0 else slice(128, 256)
    for x in range(ROWS):
        value = with_ghosts(half, message, ("m", 0, 0, x), mat_in[x, :, outer])
        index = jnp.clip(value.astype(jnp.int32), 0, 127)
        if x in (0, ROWS - 1):
            mat[x, :, outer] = value
            mat[x, :, inner] = mat_in[x, :, inner]
        for k in range(6):
            c[k, x, :, outer] = lookup(tab, k, index)
    for a in range(5):
        for k in range(3):
            for x in range(ROWS):
                fields[a][k, x, :, outer] = with_ghosts(
                    half, message, ("f", a, k, x), fields_in[a][k, x, :, outer]
                )
    for a, (source, target) in enumerate(((ce_in, ce), (ch_in, ch))):
        for k in range(3):
            for r in range(CROWS):
                target[k, r] = with_ghosts(half, message, ("c", a, k, r), coarse_row(source, k, r))
    for r in range(CROWS):
        value = cmat[pl.ds(r, Z, stride=CROWS), :].astype(F32)
        index = with_ghosts(half, message, ("cm", 0, 0, r), value).astype(jnp.int32)
        inv[r] = lookup(tab, 7, jnp.clip(index, 0, 127))
    before = jnp.concatenate([prior[...]] * (Z // 4), 0)
    before = with_ghosts(half, message, ("prior", 0, 0, 0), before)[0:4]
    interface = interface_rows(ce)
    increment = (interface - before) * (1.0 / RATIO)
    pl_ref[...] = prolong_lanes(half, jnp.concatenate([interface, increment], 0))
    send_edges(half, True, fields, c, ce, ch, pl_ref, mat, to_first, to_second)


def coarse_step(half, first, olds, news, c, ghost, olds_c, news_c, inv, pl_ref, from_left, from_right):
    e_items, h_items = x_items(first)
    zero = jnp.zeros((Z, W), F32)
    flat = (0.0, 0.0)
    (ce0, ch0), (ce, ch) = olds_c, news_c
    coarse_e0 = [row_of(ce0, r) for r in range(CROWS)]
    up = [read_x(from_right, half, e_items, ("c", 0, k)) for k in (1, 2)]
    down = [read_x(from_left, half, h_items, ("c", 0, k)) for k in (1, 2)]
    down = [down[0] + COURANT * coarse_e0[0][2], down[1] - COURANT * coarse_e0[0][1]]
    coarse_h = []
    for r in range(CROWS):
        following = coarse_e0[r + 1][1:] if r + 1 < CROWS else up
        coarse_h.append(h_row(row_of(ch0, r), coarse_e0[r], following, flat))
        for k in range(3):
            ch[k, r] = coarse_h[r][k]

    ge = gh = he = hh = None
    summed = [[None] * CROWS for _ in range(2)]
    for t in range(RATIO):
        fe, fh, fj, fp, fv = olds if t == 0 else news
        e_first = row_of(fe, 0)
        following = [read_x(from_right, half, e_items, ("e", t, k)) for k in (1, 2)]
        if t:
            following = [base + more for base, more in zip(following, he[1:])]
        far = [None, None]
        if t == 0:
            gh = [None, COURANT * e_first[2], -COURANT * e_first[1]]
        else:
            far = [COURANT * ge[2], -COURANT * ge[1]]
            old = [zero if value is None else value for value in gh]
            gh = h_row(old, ge, e_first[1:], flat, (0, 1, 2) if t < RATIO - 1 else (1, 2))
        preceding = [read_x(from_left, half, h_items, ("h", t, k)) + gh[k] for k in (1, 2)]
        current = e_first
        for x in range(ROWS):
            upper = row_of(fe, x + 1) if x + 1 < ROWS else None
            h = h_row(
                row_of(fh, x), current, upper[1:] if upper else following, top_plane(pl_ref, x, t)
            )
            e2, j2, p2, v2 = e_row(
                current, h, preceding, row_of(fj, x), row_of(fp, x), row_of(fv, x), [c[k, x] for k in range(6)]
            )
            for k in range(3):
                news[0][k, x] = e2[k]
                news[1][k, x] = h[k]
                news[2][k, x] = j2[k]
                news[3][k, x] = p2[k]
                news[4][k, x] = v2[k]
            for k in range(2):
                part = h[k][8:Z]
                have = summed[k][x // RATIO]
                summed[k][x // RATIO] = part if have is None else have + part
            preceding = h[1:]
            current = upper
        if t == 0:
            (a, b), (a2, b2) = [[ghost[k, side] for k in range(2)] for side in range(2)]
            ge = [
                a * ((gh[2] - left(gh[2])) - (gh[1] - below(gh[1], 0.0))),
                -a * gh[2],
                a * gh[1],
            ]
            he = [zero, a2 * preceding[1], -a2 * preceding[0]]
        elif t == 1:
            curl = curl_h(gh, far, flat)
            ge = [ge[k] + a * (curl[k] - b * ge[k]) for k in range(3)]
            hh = h_row([zero] * 3, he, (None, None), flat)
            curl = curl_h(hh, preceding, flat, (1, 2))
            he = [None] + [he[k] + a2 * (curl[k] - b2 * he[k]) for k in (1, 2)]

    rows = [summed[k][r][7:8] for k in range(2) for r in range(CROWS)]
    bottoms = restrict_lanes(half, jnp.concatenate(rows + rows, 0))
    preceding = down
    for r in range(CROWS):
        bottom = [bottoms[2 * k + r : 2 * k + r + 1, :] for k in range(2)]
        curl = curl_h(coarse_h[r], preceding, bottom)
        for k in range(3):
            ce[k, r] = coarse_e0[r][k] + inv[r] * curl[k]
        preceding = coarse_h[r][1:]


def ghost_coefficients(half, ghost, tab, from_left, from_right):
    e_items, h_items = x_items(True)
    for side, (ref, items) in enumerate(((from_left, h_items), (from_right, e_items))):
        index = jnp.clip(read_x(ref, half, items, ("m", 0, 0)).astype(jnp.int32), 0, 127)
        ghost[0, side] = lookup(tab, 0, index)
        ghost[1, side] = lookup(tab, 6, index)


def step_kernel(half, first, *refs):
    olds, rest = refs[0:5], refs[5:]
    c, ce0, ch0, inv, pl0, ghost_in = rest[0:6]
    from_left, from_right = sort_messages(rest[6:8], rest[-2:])
    news, rest = rest[8:13], rest[13:-2]
    if first:
        ce, ch, pl_ref, to_first, to_second, ghost = rest
        ghost_coefficients(half, ghost, ghost_in, from_left, from_right)
    else:
        ce, ch, pl_ref, to_first, to_second = rest
        ghost = ghost_in
    coarse_step(half, first, olds, news, c, ghost, (ce0, ch0), (ce, ch), inv, pl0, from_left, from_right)
    interface = interface_rows(ce)
    increment = (interface - interface_rows(ce0)) * (1.0 / RATIO)
    pl_ref[...] = prolong_lanes(half, jnp.concatenate([interface, increment], 0))
    send_edges(half, False, news, c, ce, ch, pl_ref, None, to_first, to_second)


def final_kernel(half, *refs):
    olds, rest = refs[0:5], refs[5:]
    c, ce0, ch0, inv, pl0, ghost = rest[0:6]
    from_left, from_right = sort_messages(rest[6:8], rest[-2:])
    if half == 0:
        news, (ce, ch) = rest[8:13], rest[13:15]
    else:
        others, others_c = rest[8:13], rest[13:15]
        outs, outs_c = rest[15:20], rest[20:22]
        news, (ce, ch) = rest[22:27], rest[27:29]
    coarse_step(half, False, olds, news, c, ghost, (ce0, ch0), (ce, ch), inv, pl0, from_left, from_right)
    if half == 0:
        return
    first = lanes((Z, 128)) < 64
    for a in range(5):
        for k in range(3):
            for x in range(ROWS):
                outs[a][k, x, :, 0:128] = others[a][k, x, :, 0:128]
                outs[a][k, x, :, 128:256] = jnp.where(
                    first, others[a][k, x, :, 128:256], news[a][k, x, :, 0:128]
                )
                outs[a][k, x, :, 256:384] = news[a][k, x, :, 128:256]
    for other, source, target in zip(others_c, (ce, ch), outs_c):
        for k in range(3):
            for r in range(CROWS):
                target[k, pl.ds(r, Z, stride=CROWS), :] = jnp.where(first, other[k, r], source[k, r])


def shifted(value, axis, steps):
    count = lax.axis_size(axis)
    return lax.ppermute(value, axis, [(source, (source + steps) % count) for source in range(count)])


FULL = pl.BlockSpec(memory_space=pltpu.VMEM)
RAW = pl.BlockSpec(memory_space=pltpu.HBM)
COST = pl.CostEstimate(flops=4_000_000, transcendentals=0, bytes_accessed=8_000_000)
FIELD = (3, ROWS, Z, W)
COEF = (6, ROWS, Z, W)
COARSE = (3, CROWS, Z, CW)
PLANES = (8, W)


def call(kernel, outs, args, specs=None, scratch=(), aliases=None, vmem=16):
    outs = [dims if isinstance(dims, jax.ShapeDtypeStruct) else jax.ShapeDtypeStruct(dims, F32) for dims in outs]
    return pl.pallas_call(
        kernel,
        out_shape=outs,
        in_specs=specs or [FULL] * len(args),
        out_specs=[FULL] * len(outs),
        scratch_shapes=list(scratch),
        input_output_aliases=aliases or {},
        compiler_params=pltpu.CompilerParams(vmem_limit_bytes=vmem * 1024 * 1024),
        cost_estimate=COST,
    )(*args)


def table(permittivity, plasma, damping, strength, resonance, linewidth):
    half_step = 0.5 * TIMESTEP
    c2 = plasma * plasma * TIMESTEP / (1.0 + damping * half_step)
    c4 = TIMESTEP * resonance * resonance / (1.0 + linewidth * half_step)
    rows = jnp.stack(
        [
            TIMESTEP / permittivity,
            (1.0 - damping * half_step) / (1.0 + damping * half_step),
            c2,
            (1.0 - linewidth * half_step) / (1.0 + linewidth * half_step),
            c4,
            strength,
            c2 + c4 * strength,
            COURANT / permittivity,
        ]
    )
    return jnp.pad(rows, ((0, 0), (0, 120)))


def message_shapes(half, first):
    return [(x_places(half, items)[1], Z, 128) for items in x_items(first)]


def exchanged(messages):
    count = lax.axis_size("gx")
    swapped = []
    for message, first in zip(messages, (0, 1)):
        pairs = [((first + i) % count, (first + (i ^ 1)) % count) for i in range(count)]
        swapped.append(lax.ppermute(message, "gx", pairs))
    return swapped


def local(
    fine_e,
    fine_h,
    drude_current,
    lorentz_pol,
    lorentz_rate,
    material,
    permittivity,
    plasma,
    damping,
    strength,
    resonance,
    linewidth,
    coarse_e,
    coarse_h,
    coarse_material,
    coarse_prior,
):
    fields = [
        jnp.transpose(value, (0, 2, 1, 3))
        for value in (fine_e, fine_h, drude_current, lorentz_pol, lorentz_rate)
    ]
    mat = jnp.transpose(material, (1, 0, 2))
    ce = coarse_e.reshape(3, Z * CROWS, 128)
    ch = coarse_h.reshape(3, Z * CROWS, 128)
    cmat = coarse_material.reshape(Z * CROWS, 128)
    prior = coarse_prior.reshape(2 * CROWS, 128)
    tab = table(permittivity, plasma, damping, strength, resonance, linewidth)

    vmem = lambda *dims: pltpu.VMEM(dims, F32)
    ints = lambda *dims: jax.ShapeDtypeStruct(dims, jnp.int32)
    to_left, to_right, ce, ch, cmat, prior = call(
        pack_y_kernel,
        [(Y_PLANES, Z, 128)] * 2 + [ce.shape, ch.shape, ints(*cmat.shape), prior.shape],
        [*fields, mat, ce, ch, cmat, prior],
        [RAW] * 10,
        [
            vmem(5, 3, ROWS, Z, 128),
            vmem(5, 3, ROWS, Z, 128),
            pltpu.VMEM((2, ROWS, Z, 128), jnp.int32),
            pltpu.SemaphoreType.DMA((16,)),
        ],
        vmem=61,
    )
    from_right = shifted(to_left, "gy", -1)
    from_left = shifted(to_right, "gy", 1)
    loaded = call(
        load_kernel,
        [FIELD] * 10 + [COEF] * 2 + [(ROWS, Z, W)] * 2,
        [*fields, mat, tab],
        [RAW] * 6 + [FULL],
        [pltpu.VMEM((ROWS, Z, OWN), jnp.int32), pltpu.SemaphoreType.DMA((11,))],
    )
    parts, waiting = [None, None], [None, None]
    for half in range(2):
        state = loaded[5 * half : 5 * half + 5]
        out = call(
            functools.partial(start_kernel, half),
            [FIELD] * 5 + [COEF, COARSE, COARSE, (CROWS, Z, CW), PLANES] + message_shapes(half, True),
            [*state, loaded[10 + half], loaded[12 + half], ce, ch, cmat, prior, tab, (from_left, from_right)[half]],
            scratch=[vmem(ROWS, Z, W)],
            aliases={index: index for index in range(6)},
        )
        parts[half] = (out[0:5], out[5:10], tab)
        waiting[half] = exchanged(out[10:12])
    for step in range(STEPS - 1):
        for half in range(2):
            state, (c, ce, ch, inv, planes), ghost = parts[half]
            out = call(
                functools.partial(step_kernel, half, step == 0),
                [FIELD] * 5
                + [COARSE, COARSE, PLANES]
                + message_shapes(half, False)
                + ([(2, 2, Z, W)] if step == 0 else []),
                [*state, c, ce, ch, inv, planes, ghost, *waiting[half]],
                scratch=[vmem(*message.shape) for message in waiting[half]],
            )
            if step == 0:
                ghost = out[10]
            parts[half] = (out[0:5], (c, out[5], out[6], inv, out[7]), ghost)
            waiting[half] = exchanged(out[8:10])
    done = []
    for half in range(2):
        state, coarse, ghost = parts[half]
        done = call(
            functools.partial(final_kernel, half),
            [FIELD] * 5 + [COARSE] * 2 if half == 0 else [(3, ROWS, Z, OWN)] * 5 + [(3, Z * CROWS, 128)] * 2,
            [*state, *coarse, ghost, *waiting[half], *done],
            scratch=([vmem(*FIELD)] * 5 + [vmem(*COARSE)] * 2 if half else [])
            + [vmem(*message.shape) for message in waiting[half]],
        )
    fine = [jnp.transpose(value, (0, 2, 1, 3)) for value in done[0:5]]
    coarse = [value.reshape(3, Z, CROWS, 128) for value in done[5:7]]
    return (*fine, *coarse)


def solution(mesh):
    field = P(None, None, "gx", "gy")
    plane = P(None, "gx", "gy")
    in_specs = (field,) * 5 + (plane,) + (P(),) * 6 + (field, field, plane, plane)
    return jax.shard_map(local, mesh=mesh, in_specs=in_specs, out_specs=(field,) * 7, check_vma=False)
```

```python
import functools

import jax
import jax.numpy as jnp
from jax import lax
from jax.experimental import pallas as pl
from jax.experimental.pallas import tpu as pltpu
from jax.sharding import PartitionSpec as P

RATIO = 3
STEPS = 3
COURANT = 0.5
TIMESTEP = 0.5

Z = 16
ROWS = 6
OWN = 384
W = 256
CROWS = 2
CW = 128
GHOST = 9
CGHOST = 3
TILES = ((0, 1), (1, 2))
F32 = jnp.float32


def rolled(value, shift, axis):
    shift %= value.shape[axis]
    return value if shift == 0 else pltpu.roll(value, shift, axis)


def lanes(shape):
    return lax.broadcasted_iota(jnp.int32, shape, len(shape) - 1)


def right(value):
    return rolled(value, -1, 1)


def left(value):
    return rolled(value, 1, 1)


def above(value, top):
    sublane = lax.broadcasted_iota(jnp.int32, value.shape, 0)
    return jnp.where(sublane == Z - 1, top, rolled(value, -1, 0))


def below(value, bottom):
    sublane = lax.broadcasted_iota(jnp.int32, value.shape, 0)
    return jnp.where(sublane == 0, bottom, rolled(value, 1, 0))


def minus(first, second):
    if first is None:
        return None if second is None else -second
    return first if second is None else first - second


def h_row(h, e, following, top, wanted=(0, 1, 2)):
    ex, ey, ez = e
    next_y, next_z = following
    out = [None, None, None]
    if 0 in wanted:
        out[0] = h[0] - COURANT * ((right(ez) - ez) - (above(ey, top[1]) - ey))
    if 1 in wanted:
        out[1] = h[1] - COURANT * ((above(ex, top[0]) - ex) - minus(next_z, ez))
    if 2 in wanted:
        out[2] = h[2] - COURANT * (minus(next_y, ey) - (right(ex) - ex))
    return out


def curl_h(h, preceding, bottom, wanted=(0, 1, 2)):
    hx, hy, hz = h
    prev_y, prev_z = preceding
    out = [None, None, None]
    if 0 in wanted:
        out[0] = (hz - left(hz)) - (hy - below(hy, bottom[1]))
    if 1 in wanted:
        out[1] = (hx - below(hx, bottom[0])) - minus(hz, prev_z)
    if 2 in wanted:
        out[2] = minus(hy, prev_y) - (hx - left(hx))
    return out


def e_row(e, h, preceding, j, p, v, c, wanted=(0, 1, 2)):
    curl = curl_h(h, preceding, (0.0, 0.0), wanted)
    e2, j2, p2, v2 = [None] * 3, [None] * 3, [None] * 3, [None] * 3
    for k in wanted:
        v2[k] = c[3] * v[k] + c[4] * (c[5] * e[k] - p[k])
        j2[k] = c[1] * j[k] + c[2] * e[k]
        p2[k] = p[k] + TIMESTEP * v2[k]
        e2[k] = e[k] + c[0] * (curl[k] - j2[k] - v2[k])
    return e2, j2, p2, v2


def y_slots():
    entries = [("f", a, k, x, GHOST) for a in range(5) for k in range(3) for x in range(ROWS)]
    entries += [("m", 0, 0, x, GHOST) for x in range(ROWS)]
    entries += [("c", a, k, r, CGHOST) for a in range(2) for k in range(3) for r in range(CROWS)]
    entries += [("cm", 0, 0, r, CGHOST) for r in range(CROWS)]
    entries += [("prior", 0, 0, 0, CGHOST)]
    slots, plane, offset = {}, 0, 0
    for *key, width in entries:
        if offset + width > 128:
            plane, offset = plane + 1, 0
        slots[tuple(key)] = (plane, offset, width)
        offset += width
    return slots, plane + 1


Y_SLOTS, Y_PLANES = y_slots()


def coarse_row(ref, k, r):
    return ref[k, pl.ds(r, Z, stride=CROWS), :]


def pack_y_kernel(*refs):
    fields, (material, ce_in, ch_in, cmat_in, prior_in) = refs[0:5], refs[5:10]
    to_first, to_second, firsts, lasts, mats, ce, ch, cmat, prior, sems = refs[10:20]
    even = lax.rem(lax.axis_index("gy"), 2) == 0
    pairs = []
    for a in range(5):
        pairs.append((fields[a].at[:, :, :, 0:128], firsts.at[a]))
        pairs.append((fields[a].at[:, :, :, OWN - 128 : OWN], lasts.at[a]))
    pairs.append((material.at[:, :, 0:128], mats.at[0]))
    pairs.append((material.at[:, :, OWN - 128 : OWN], mats.at[1]))
    pairs += [(ce_in, ce), (ch_in, ch), (cmat_in, cmat), (prior_in, prior)]
    copies = [pltpu.make_async_copy(src, dst, sems.at[i]) for i, (src, dst) in enumerate(pairs)]
    for copy in copies:
        copy.start()
    for copy in copies:
        copy.wait()
    lane = lanes((Z, 128))
    built = {}
    for key, (plane, offset, width) in Y_SLOTS.items():
        kind, a, k, x = key
        if kind == "f":
            first, last = firsts[a, k, x], lasts[a, k, x]
        elif kind == "m":
            first, last = mats[0, x].astype(F32), mats[1, x].astype(F32)
        elif kind == "c":
            first = last = coarse_row((ce, ch)[a], k, x)
        elif kind == "cm":
            first = last = cmat[pl.ds(x, Z, stride=CROWS), :].astype(F32)
        else:
            first = last = jnp.concatenate([prior[...]] * (Z // 4), 0)
        pair = (rolled(first, offset, 1), rolled(last, offset + width, 1))
        if plane in built:
            keep = lane < offset
            pair = tuple(jnp.where(keep, old, new) for old, new in zip(built[plane], pair))
        built[plane] = pair
    for plane, (one, other) in built.items():
        to_first[plane] = jnp.where(even, other, one)
        to_second[plane] = jnp.where(even, one, other)


def with_ghosts(half, message, key, tile):
    plane, offset, width = Y_SLOTS[key]
    lane = lanes((Z, 128))
    if half == 0:
        return jnp.where(lane < 96, tile, rolled(message[plane], -offset - width, 1))
    return jnp.where(lane < 32, rolled(message[plane], -offset, 1), tile)


def load_kernel(*refs):
    own, material_in, coarse_in, tab = refs[0:5], refs[5], refs[6:10], refs[10]
    states = (refs[11:16], refs[16:21])
    c_halves, mat_halves, coarse = refs[21:23], refs[23:25], refs[25:29]
    material, sems = refs[29:31]
    first = pltpu.make_async_copy(material_in, material, sems.at[10])
    first.start()
    copies = []
    for half in range(2):
        for a in range(5):
            source = own[a].at[:, :, :, 128 * half : 128 * half + W]
            copies.append(pltpu.make_async_copy(source, states[half][a], sems.at[5 * half + a]))
            copies[-1].start()
    for i, (source, target) in enumerate(zip(coarse_in, coarse)):
        copies.append(pltpu.make_async_copy(source, target, sems.at[11 + i]))
        copies[-1].start()
    first.wait()
    for x in range(ROWS):
        for half in range(2):
            mat_halves[half][x] = material[x, :, 128 * half : 128 * half + W].astype(F32)
        for tile in range(3):
            index = material[x, :, 128 * tile : 128 * (tile + 1)]
            for k in range(6):
                value = lookup(tab, k, index)
                for half in range(2):
                    if tile in TILES[half]:
                        local_tile = TILES[half].index(tile)
                        c_halves[half][k, x, :, 128 * local_tile : 128 * (local_tile + 1)] = value
    for copy in copies:
        copy.wait()


E_ITEMS = [(("e", t, k), 9 - t, 8 - t, True) for t in range(RATIO) for k in (1, 2)]
H_ITEMS = [(("h", t, k), 8 - t, 8 - t, True) for t in range(RATIO) for k in (1, 2)]
COARSE_ITEMS = [(("c", 0, k), CGHOST, CGHOST, False) for k in (1, 2)]
MATERIAL_ITEM = [(("m", 0, 0), 8, 8, True)]


def x_places(half, items):
    places, half_slots, plane, offset = {}, [], 1, 0
    for name, lefts, rights, fine in items:
        mixed = (1 - half) if fine else 0
        segments = []
        if fine:
            segments.append((half, 0, plane, 0, 128))
            plane += 1
        if not half_slots:
            half_slots = [(plane, 0), (plane, 64)]
            plane += 1
        own_lane = 64 * half
        segments.append((mixed, own_lane, *half_slots.pop(0), 64))
        left_lane = 64 - lefts if half else 128 - lefts
        right_lane = 0 if half else 64
        for lane, length in ((left_lane, lefts), (right_lane, rights)):
            segments.append((mixed, lane, 0, offset, length))
            offset += length
        places[name] = segments
    assert offset <= 128
    return places, plane


def write_x(half, items, values):
    places, planes = x_places(half, items)
    lane = lanes((Z, 128))
    built_planes = []
    for plane in range(planes):
        parts = sorted(
            (there, name, tile, start)
            for name, segments in places.items()
            for tile, start, where, there, _ in segments
            if where == plane
        )
        built = None
        for there, name, tile, start in parts:
            value = rolled(values[name][:, 128 * tile : 128 * (tile + 1)], there - start, 1)
            built = value if built is None else jnp.where(lane < there, built, value)
        built_planes.append(built)
    return built_planes


def read_x(ref, half, items, name):
    lane = lanes((Z, 128))
    built = {}
    for tile, start, plane, there, _ in sorted(x_places(half, items)[0][name]):
        value = rolled(ref[plane], start - there, 1)
        built[tile] = value if tile not in built else jnp.where(lane < start, built[tile], value)
    return jnp.concatenate([built[tile] for tile in sorted(built)], 1)


def x_items(first):
    extra = MATERIAL_ITEM if first else []
    return E_ITEMS + COARSE_ITEMS + extra, H_ITEMS + COARSE_ITEMS + extra


def gather(value, index):
    return jnp.take_along_axis(value, index, axis=1, mode="promise_in_bounds")


def prolong_lanes(half, value):
    lane = lanes((8, 128))
    third = lambda number: (number * 21846) >> 16
    if half == 0:
        indices = [third(lane), jnp.where(lane < 96, third(lane + 128), 128 - third(130 - lane))]
    else:
        indices = [jnp.where(lane < 32, third(lane), third(lane + 128)), third(lane + 256)]
    return jnp.concatenate([gather(value, index) for index in indices], 1)


def restrict_lanes(half, value):
    three = value + rolled(value, -1, 1) + rolled(value, -2, 1)
    lane = lanes((8, 128))
    index = (lane * RATIO) & 127
    tiles = [gather(three[:, 128 * tile : 128 * (tile + 1)], index) for tile in range(2)]
    in_first = lane * RATIO < (128 if half == 0 else 256)
    return jnp.where(in_first, tiles[0], tiles[1]) * (1.0 / RATIO**3)


def sort_messages(received, sorted_refs):
    even = lax.rem(lax.axis_index("gx"), 2) == 0
    first, second = received
    from_left, from_right = sorted_refs
    for plane in range(first.shape[0]):
        from_left[plane] = jnp.where(even, second[plane], first[plane])
        from_right[plane] = jnp.where(even, first[plane], second[plane])
    return from_left, from_right


def interface_rows(ce):
    return jnp.concatenate([ce[k, r][0:1] for k in range(2) for r in range(CROWS)], 0)


def top_plane(pl_ref, x, t):
    r = x // RATIO
    out = []
    for k in range(2):
        row = 2 * k + r
        value = pl_ref[row : row + 1, :]
        if t:
            value = value + float(t) * pl_ref[4 + row : 5 + row, :]
        out.append(value)
    return out


def lookup(tab, row, index):
    entry = jnp.broadcast_to(tab[row : row + 1, :], (8, 128))
    rows = []
    for z in range(0, Z, 8):
        rows.append(
            jnp.concatenate(
                [
                    gather(entry, index[z : z + 8, lane : lane + 128])
                    for lane in range(0, index.shape[1], 128)
                ],
                1,
            )
        )
    return jnp.concatenate(rows, 0)


def row_of(ref, x):
    return [ref[k, x] for k in range(3)]


def send_edges(half, first, fields, c, ce, ch, pl_ref, mat, to_first, to_second):
    fe, fh, fj, fp, fv = fields
    none = (None, None)
    e_items, h_items = x_items(first)
    coef = lambda x: [c[k, x] for k in range(6)]
    states = lambda x: (row_of(fj, x), row_of(fp, x), row_of(fv, x))
    e0 = {x: row_of(fe, x) for x in range(ROWS)}
    low, high = {}, {}

    for k in (1, 2):
        low["e", 0, k] = e0[0][k]
    h1 = {x: h_row(row_of(fh, x), e0[x], e0[x + 1][1:], top_plane(pl_ref, x, 0)) for x in (0, 1)}
    e1, s1 = {}, {}
    e1[0], *s1[0] = e_row(e0[0], h1[0], none, *states(0), coef(0))
    e1[1], *s1[1] = e_row(e0[1], h1[1], h1[0][1:], *states(1), coef(1), (1, 2))
    h2 = h_row(h1[0], e1[0], e1[1][1:], top_plane(pl_ref, 0, 1))
    e2 = e_row(e1[0], h2, none, *s1[0], coef(0), (1, 2))[0]
    for k in (1, 2):
        low["e", 1, k] = e1[0][k]
        low["e", 2, k] = e2[k]
        low["c", 0, k] = ce[k, 0]

    a, b, d = ROWS - 3, ROWS - 2, ROWS - 1
    h1 = {
        a: h_row(row_of(fh, a), e0[a], e0[b][1:], top_plane(pl_ref, a, 0), (1, 2)),
        b: h_row(row_of(fh, b), e0[b], e0[d][1:], top_plane(pl_ref, b, 0)),
        d: h_row(row_of(fh, d), e0[d], none, top_plane(pl_ref, d, 0)),
    }
    e1, s1 = {}, {}
    e1[b], *s1[b] = e_row(e0[b], h1[b], h1[a][1:], *states(b), coef(b))
    e1[d], *s1[d] = e_row(e0[d], h1[d], h1[b][1:], *states(d), coef(d))
    h2 = {
        b: h_row(h1[b], e1[b], e1[d][1:], top_plane(pl_ref, b, 1), (1, 2)),
        d: h_row(h1[d], e1[d], none, top_plane(pl_ref, d, 1)),
    }
    e2 = e_row(e1[d], h2[d], h2[b][1:], *s1[d], coef(d))[0]
    h3 = h_row(h2[d], e2, none, top_plane(pl_ref, d, 2), (1, 2))
    ch_last = h_row(row_of(ch, CROWS - 1), row_of(ce, CROWS - 1), none, (0.0, 0.0), (1, 2))
    for k in (1, 2):
        high["h", 0, k] = h1[d][k]
        high["h", 1, k] = h2[d][k]
        high["h", 2, k] = h3[k]
        high["c", 0, k] = ch_last[k]
    if first:
        low["m", 0, 0] = mat[0]
        high["m", 0, 0] = mat[ROWS - 1]
    even = lax.rem(lax.axis_index("gx"), 2) == 0
    for first_part, second_part, plane in zip(write_x(half, h_items, high), write_x(half, e_items, low), range(99)):
        to_first[plane] = jnp.where(even, first_part, second_part)
        to_second[plane] = jnp.where(even, second_part, first_part)


def start_kernel(half, *refs):
    fields_in, (c_in, mat_in, ce_in, ch_in, cmat, prior, tab) = refs[0:5], refs[5:12]
    received, fields = refs[12:14], refs[14:19]
    c, ce, ch, inv, pl_ref, to_first, to_second, mat, message = refs[19:28]
    even = lax.rem(lax.axis_index("gy"), 2) == 0
    swap = even if half == 0 else jnp.logical_not(even)
    for plane in range(Y_PLANES):
        message[plane] = jnp.where(swap, received[1][plane], received[0][plane])
    outer = slice(128, 256) if half == 0 else slice(0, 128)
    inner = slice(0, 128) if half == 0 else slice(128, 256)
    for x in range(ROWS):
        value = with_ghosts(half, message, ("m", 0, 0, x), mat_in[x, :, outer])
        index = jnp.clip(value.astype(jnp.int32), 0, 127)
        if x in (0, ROWS - 1):
            mat[x, :, outer] = value
            mat[x, :, inner] = mat_in[x, :, inner]
        for k in range(6):
            c[k, x, :, outer] = lookup(tab, k, index)
    for a in range(5):
        for k in range(3):
            for x in range(ROWS):
                fields[a][k, x, :, outer] = with_ghosts(
                    half, message, ("f", a, k, x), fields_in[a][k, x, :, outer]
                )
    for a, (source, target) in enumerate(((ce_in, ce), (ch_in, ch))):
        for k in range(3):
            for r in range(CROWS):
                target[k, r] = with_ghosts(half, message, ("c", a, k, r), coarse_row(source, k, r))
    for r in range(CROWS):
        value = cmat[pl.ds(r, Z, stride=CROWS), :].astype(F32)
        index = with_ghosts(half, message, ("cm", 0, 0, r), value).astype(jnp.int32)
        inv[r] = lookup(tab, 7, jnp.clip(index, 0, 127))
    before = jnp.concatenate([prior[...]] * (Z // 4), 0)
    before = with_ghosts(half, message, ("prior", 0, 0, 0), before)[0:4]
    interface = interface_rows(ce)
    increment = (interface - before) * (1.0 / RATIO)
    pl_ref[...] = prolong_lanes(half, jnp.concatenate([interface, increment], 0))
    send_edges(half, True, fields, c, ce, ch, pl_ref, mat, to_first, to_second)


def coarse_step(half, first, olds, news, c, ghost, olds_c, news_c, inv, pl_ref, from_left, from_right, finished=None):
    e_items, h_items = x_items(first)
    zero = jnp.zeros((Z, W), F32)
    flat = (0.0, 0.0)
    (ce0, ch0), (ce, ch) = olds_c, news_c
    coarse_e0 = [row_of(ce0, r) for r in range(CROWS)]
    up = [read_x(from_right, half, e_items, ("c", 0, k)) for k in (1, 2)]
    down = [read_x(from_left, half, h_items, ("c", 0, k)) for k in (1, 2)]
    down = [down[0] + COURANT * coarse_e0[0][2], down[1] - COURANT * coarse_e0[0][1]]
    coarse_h = []
    for r in range(CROWS):
        following = coarse_e0[r + 1][1:] if r + 1 < CROWS else up
        coarse_h.append(h_row(row_of(ch0, r), coarse_e0[r], following, flat))
        for k in range(3):
            ch[k, r] = coarse_h[r][k]
    if finished:
        finished(-2)

    ge = gh = he = hh = None
    summed = [[None] * CROWS for _ in range(2)]
    for t in range(RATIO):
        fe, fh, fj, fp, fv = olds if t == 0 else news
        e_first = row_of(fe, 0)
        following = [read_x(from_right, half, e_items, ("e", t, k)) for k in (1, 2)]
        if t:
            following = [base + more for base, more in zip(following, he[1:])]
        far = [None, None]
        if t == 0:
            gh = [None, COURANT * e_first[2], -COURANT * e_first[1]]
        else:
            far = [COURANT * ge[2], -COURANT * ge[1]]
            old = [zero if value is None else value for value in gh]
            gh = h_row(old, ge, e_first[1:], flat, (0, 1, 2) if t < RATIO - 1 else (1, 2))
        preceding = [read_x(from_left, half, h_items, ("h", t, k)) + gh[k] for k in (1, 2)]
        current = e_first
        for x in range(ROWS):
            upper = row_of(fe, x + 1) if x + 1 < ROWS else None
            h = h_row(
                row_of(fh, x), current, upper[1:] if upper else following, top_plane(pl_ref, x, t)
            )
            e2, j2, p2, v2 = e_row(
                current, h, preceding, row_of(fj, x), row_of(fp, x), row_of(fv, x), [c[k, x] for k in range(6)]
            )
            for k in range(3):
                news[0][k, x] = e2[k]
                news[1][k, x] = h[k]
                news[2][k, x] = j2[k]
                news[3][k, x] = p2[k]
                news[4][k, x] = v2[k]
            for k in range(2):
                part = h[k][8:Z]
                have = summed[k][x // RATIO]
                summed[k][x // RATIO] = part if have is None else have + part
            preceding = h[1:]
            current = upper
            if finished and t == RATIO - 1:
                finished(x)
        if t == 0:
            (a, b), (a2, b2) = [[ghost[k, side] for k in range(2)] for side in range(2)]
            ge = [
                a * ((gh[2] - left(gh[2])) - (gh[1] - below(gh[1], 0.0))),
                -a * gh[2],
                a * gh[1],
            ]
            he = [zero, a2 * preceding[1], -a2 * preceding[0]]
        elif t == 1:
            curl = curl_h(gh, far, flat)
            ge = [ge[k] + a * (curl[k] - b * ge[k]) for k in range(3)]
            hh = h_row([zero] * 3, he, (None, None), flat)
            curl = curl_h(hh, preceding, flat, (1, 2))
            he = [None] + [he[k] + a2 * (curl[k] - b2 * he[k]) for k in (1, 2)]

    rows = [summed[k][r][7:8] for k in range(2) for r in range(CROWS)]
    bottoms = restrict_lanes(half, jnp.concatenate(rows + rows, 0))
    preceding = down
    for r in range(CROWS):
        bottom = [bottoms[2 * k + r : 2 * k + r + 1, :] for k in range(2)]
        curl = curl_h(coarse_h[r], preceding, bottom)
        for k in range(3):
            ce[k, r] = coarse_e0[r][k] + inv[r] * curl[k]
        preceding = coarse_h[r][1:]
    if finished:
        finished(-1)


def ghost_coefficients(half, ghost, tab, from_left, from_right):
    e_items, h_items = x_items(True)
    for side, (ref, items) in enumerate(((from_left, h_items), (from_right, e_items))):
        index = jnp.clip(read_x(ref, half, items, ("m", 0, 0)).astype(jnp.int32), 0, 127)
        ghost[0, side] = lookup(tab, 0, index)
        ghost[1, side] = lookup(tab, 6, index)


def step_kernel(half, first, *refs):
    olds, rest = refs[0:5], refs[5:]
    c, ce0, ch0, inv, pl0, ghost_in = rest[0:6]
    from_left, from_right = sort_messages(rest[6:8], rest[-2:])
    news, rest = rest[8:13], rest[13:-2]
    if first:
        ce, ch, pl_ref, to_first, to_second, ghost = rest
        ghost_coefficients(half, ghost, ghost_in, from_left, from_right)
    else:
        ce, ch, pl_ref, to_first, to_second = rest
        ghost = ghost_in
    coarse_step(half, first, olds, news, c, ghost, (ce0, ch0), (ce, ch), inv, pl0, from_left, from_right)
    interface = interface_rows(ce)
    increment = (interface - interface_rows(ce0)) * (1.0 / RATIO)
    pl_ref[...] = prolong_lanes(half, jnp.concatenate([interface, increment], 0))
    send_edges(half, False, news, c, ce, ch, pl_ref, None, to_first, to_second)


def final_kernel(half, *refs):
    olds, rest = refs[0:5], refs[5:]
    c, ce0, ch0, inv, pl0, ghost = rest[0:6]
    received, rest = rest[6:8], rest[8:]
    if half == 0:
        outs, news, ce, ch = rest[0:5], rest[5:10], rest[10], rest[11]
        rest = rest[12:]
    else:
        others, others_c = rest[5:10], rest[10:12]
        outs, outs_c, news, ce, ch = rest[12:17], rest[17:19], rest[19:24], rest[24], rest[25]
        coarse_parts = rest[26:28]
        rest = rest[28:]
    sorted_refs, sems = rest[0:2], rest[2]
    from_left, from_right = sort_messages(received, sorted_refs)
    first = lanes((Z, 128)) < 64
    copies = []

    def coarse_finished(a):
        if half == 0:
            return
        for k in range(3):
            for r in range(CROWS):
                value = jnp.where(first, others_c[a][k, r], (ce, ch)[a][k, r])
                coarse_parts[a][k, pl.ds(r, Z, stride=CROWS), :] = value
        copies.append(pltpu.make_async_copy(coarse_parts[a], outs_c[a], sems.at[ROWS, a]))
        copies[-1].start()

    def finished(x):
        if x < 0:
            return coarse_finished(-x - 1)
        for a in range(5):
            if half == 0:
                source = news[a].at[:, x, :, 0:128]
                target = outs[a].at[:, x, :, 0:128]
            else:
                for k in range(3):
                    news[a][k, x, :, 0:128] = jnp.where(
                        first, others[a][k, x, :, 128:256], news[a][k, x, :, 0:128]
                    )
                source = news[a].at[:, x]
                target = outs[a].at[:, x, :, 128:384]
            copies.append(pltpu.make_async_copy(source, target, sems.at[x, a]))
            copies[-1].start()

    coarse_step(
        half, False, olds, news, c, ghost, (ce0, ch0), (ce, ch), inv, pl0, from_left, from_right, finished
    )
    for copy in copies:
        copy.wait()


FULL = pl.BlockSpec(memory_space=pltpu.VMEM)
RAW = pl.BlockSpec(memory_space=pltpu.HBM)
COST = pl.CostEstimate(flops=4_000_000, transcendentals=0, bytes_accessed=8_000_000)
FIELD = (3, ROWS, Z, W)
COEF = (6, ROWS, Z, W)
COARSE = (3, CROWS, Z, CW)
PLANES = (8, W)


def call(kernel, outs, args, specs=None, scratch=(), aliases=None, vmem=16, out_specs=None):
    outs = [dims if isinstance(dims, jax.ShapeDtypeStruct) else jax.ShapeDtypeStruct(dims, F32) for dims in outs]
    return pl.pallas_call(
        kernel,
        out_shape=outs,
        in_specs=specs or [FULL] * len(args),
        out_specs=out_specs or [FULL] * len(outs),
        scratch_shapes=list(scratch),
        input_output_aliases=aliases or {},
        compiler_params=pltpu.CompilerParams(vmem_limit_bytes=vmem * 1024 * 1024),
        cost_estimate=COST,
    )(*args)


def table(permittivity, plasma, damping, strength, resonance, linewidth):
    half_step = 0.5 * TIMESTEP
    c2 = plasma * plasma * TIMESTEP / (1.0 + damping * half_step)
    c4 = TIMESTEP * resonance * resonance / (1.0 + linewidth * half_step)
    rows = jnp.stack(
        [
            TIMESTEP / permittivity,
            (1.0 - damping * half_step) / (1.0 + damping * half_step),
            c2,
            (1.0 - linewidth * half_step) / (1.0 + linewidth * half_step),
            c4,
            strength,
            c2 + c4 * strength,
            COURANT / permittivity,
        ]
    )
    return jnp.pad(rows, ((0, 0), (0, 120)))


def message_shapes(half, first):
    return [(x_places(half, items)[1], Z, 128) for items in x_items(first)]


def exchanged(messages, axis):
    count = lax.axis_size(axis)
    swapped = []
    for message, first in zip(messages, (0, 1)):
        pairs = [((first + i) % count, (first + (i ^ 1)) % count) for i in range(count)]
        swapped.append(lax.ppermute(message, axis, pairs))
    return swapped


def local(
    fine_e,
    fine_h,
    drude_current,
    lorentz_pol,
    lorentz_rate,
    material,
    permittivity,
    plasma,
    damping,
    strength,
    resonance,
    linewidth,
    coarse_e,
    coarse_h,
    coarse_material,
    coarse_prior,
):
    fields = [
        jnp.transpose(value, (0, 2, 1, 3))
        for value in (fine_e, fine_h, drude_current, lorentz_pol, lorentz_rate)
    ]
    mat = jnp.transpose(material, (1, 0, 2))
    ce = coarse_e.reshape(3, Z * CROWS, 128)
    ch = coarse_h.reshape(3, Z * CROWS, 128)
    cmat = coarse_material.reshape(Z * CROWS, 128)
    prior = coarse_prior.reshape(2 * CROWS, 128)
    in_hbm = lambda values: [pltpu.with_memory_space_constraint(value, pltpu.HBM) for value in values]
    fields, coarse = in_hbm(fields), in_hbm([ce, ch, cmat, prior])
    (mat,) = in_hbm([mat])
    tab = table(permittivity, plasma, damping, strength, resonance, linewidth)

    vmem = lambda *dims: pltpu.VMEM(dims, F32)
    packed = call(
        pack_y_kernel,
        [(Y_PLANES, Z, 128)] * 2,
        [*fields, mat, *coarse],
        [RAW] * 10,
        [
            vmem(5, 3, ROWS, Z, 128),
            vmem(5, 3, ROWS, Z, 128),
            pltpu.VMEM((2, ROWS, Z, 128), jnp.int32),
            vmem(*ce.shape),
            vmem(*ch.shape),
            pltpu.VMEM(cmat.shape, jnp.int32),
            vmem(*prior.shape),
            pltpu.SemaphoreType.DMA((16,)),
        ],
        vmem=16,
    )
    received = exchanged(packed, "gy")
    loaded = call(
        load_kernel,
        [FIELD] * 10
        + [COEF] * 2
        + [(ROWS, Z, W)] * 2
        + [jax.ShapeDtypeStruct(value.shape, value.dtype) for value in coarse],
        [*fields, mat, *coarse, tab],
        [RAW] * 10 + [FULL],
        [pltpu.VMEM((ROWS, Z, OWN), jnp.int32), pltpu.SemaphoreType.DMA((15,))],
    )
    parts, waiting = [None, None], [None, None]
    for half in range(2):
        state = loaded[5 * half : 5 * half + 5]
        out = call(
            functools.partial(start_kernel, half),
            [FIELD] * 5 + [COEF, COARSE, COARSE, (CROWS, Z, CW), PLANES] + message_shapes(half, True),
            [*state, loaded[10 + half], loaded[12 + half], *loaded[14:18], tab, *received],
            scratch=[vmem(ROWS, Z, W), vmem(Y_PLANES, Z, 128)],
            aliases={index: index for index in range(6)},
        )
        parts[half] = (out[0:5], out[5:10], tab)
        waiting[half] = exchanged(out[10:12], "gx")
    for step in range(STEPS - 1):
        for half in range(2):
            state, (c, ce, ch, inv, planes), ghost = parts[half]
            out = call(
                functools.partial(step_kernel, half, step == 0),
                [FIELD] * 5
                + [COARSE, COARSE, PLANES]
                + message_shapes(half, False)
                + ([(2, 2, Z, W)] if step == 0 else []),
                [*state, c, ce, ch, inv, planes, ghost, *waiting[half]],
                scratch=[vmem(*message.shape) for message in waiting[half]],
            )
            if step == 0:
                ghost = out[10]
            parts[half] = (out[0:5], (c, out[5], out[6], inv, out[7]), ghost)
            waiting[half] = exchanged(out[8:10], "gx")
    whole = [(3, ROWS, Z, OWN)] * 5
    done = []
    for half in range(2):
        state, coarse, ghost = parts[half]
        args = [*state, *coarse, ghost, *waiting[half], *done]
        done = call(
            functools.partial(final_kernel, half),
            whole + ([(3, Z * CROWS, 128)] * 2 if half else [FIELD] * 5 + [COARSE] * 2),
            args,
            specs=[RAW if 13 <= i < 18 else FULL for i in range(len(args))],
            out_specs=[RAW] * 7 if half else [RAW] * 5 + [FULL] * 7,
            scratch=([vmem(*FIELD)] * 5 + [vmem(*COARSE)] * 2 + [vmem(3, Z * CROWS, 128)] * 2 if half else [])
            + [vmem(*message.shape) for message in waiting[half]]
            + [pltpu.SemaphoreType.DMA((ROWS + 1, 5))],
            aliases={13 + i: i for i in range(5)} if half else None,
        )
    fine = [jnp.transpose(value, (0, 2, 1, 3)) for value in done[0:5]]
    coarse = [value.reshape(3, Z, CROWS, 128) for value in done[5:7]]
    return (*fine, *coarse)


def solution(mesh):
    field = P(None, None, "gx", "gy")
    plane = P(None, "gx", "gy")
    in_specs = (field,) * 5 + (plane,) + (P(),) * 6 + (field, field, plane, plane)
    return jax.shard_map(local, mesh=mesh, in_specs=in_specs, out_specs=(field,) * 7, check_vma=False)
```

```python
import functools

import jax
import jax.numpy as jnp
from jax import lax
from jax.experimental import pallas as pl
from jax.experimental.pallas import tpu as pltpu
from jax.sharding import PartitionSpec as P

RATIO = 3
STEPS = 3
COURANT = 0.5
TIMESTEP = 0.5

Z = 16
ROWS = 6
OWN = 384
W = 256
CROWS = 2
CW = 128
GHOST = 9
CGHOST = 3
TILES = ((0, 1), (1, 2))
F32 = jnp.float32


def rolled(value, shift, axis):
    shift %= value.shape[axis]
    return value if shift == 0 else pltpu.roll(value, shift, axis)


def lanes(shape):
    return lax.broadcasted_iota(jnp.int32, shape, len(shape) - 1)


def right(value):
    return rolled(value, -1, 1)


def left(value):
    return rolled(value, 1, 1)


def above(value, top):
    sublane = lax.broadcasted_iota(jnp.int32, value.shape, 0)
    return jnp.where(sublane == Z - 1, top, rolled(value, -1, 0))


def below(value, bottom):
    sublane = lax.broadcasted_iota(jnp.int32, value.shape, 0)
    return jnp.where(sublane == 0, bottom, rolled(value, 1, 0))


def minus(first, second):
    if first is None:
        return None if second is None else -second
    return first if second is None else first - second


def h_row(h, e, following, top, wanted=(0, 1, 2)):
    ex, ey, ez = e
    next_y, next_z = following
    out = [None, None, None]
    if 0 in wanted:
        out[0] = h[0] - COURANT * ((right(ez) - ez) - (above(ey, top[1]) - ey))
    if 1 in wanted:
        out[1] = h[1] - COURANT * ((above(ex, top[0]) - ex) - minus(next_z, ez))
    if 2 in wanted:
        out[2] = h[2] - COURANT * (minus(next_y, ey) - (right(ex) - ex))
    return out


def curl_h(h, preceding, bottom, wanted=(0, 1, 2)):
    hx, hy, hz = h
    prev_y, prev_z = preceding
    out = [None, None, None]
    if 0 in wanted:
        out[0] = (hz - left(hz)) - (hy - below(hy, bottom[1]))
    if 1 in wanted:
        out[1] = (hx - below(hx, bottom[0])) - minus(hz, prev_z)
    if 2 in wanted:
        out[2] = minus(hy, prev_y) - (hx - left(hx))
    return out


def e_row(e, h, preceding, j, p, v, c, wanted=(0, 1, 2)):
    curl = curl_h(h, preceding, (0.0, 0.0), wanted)
    e2, j2, p2, v2 = [None] * 3, [None] * 3, [None] * 3, [None] * 3
    for k in wanted:
        v2[k] = c[3] * v[k] + c[4] * (c[5] * e[k] - p[k])
        j2[k] = c[1] * j[k] + c[2] * e[k]
        p2[k] = p[k] + TIMESTEP * v2[k]
        e2[k] = e[k] + c[0] * (curl[k] - j2[k] - v2[k])
    return e2, j2, p2, v2


def y_slots():
    entries = [("f", a, k, x, GHOST) for a in range(5) for k in range(3) for x in range(ROWS)]
    entries += [("m", 0, 0, x, GHOST) for x in range(ROWS)]
    entries += [("c", a, k, r, CGHOST) for a in range(2) for k in range(3) for r in range(CROWS)]
    entries += [("cm", 0, 0, r, CGHOST) for r in range(CROWS)]
    entries += [("prior", 0, 0, 0, CGHOST)]
    slots, plane, offset = {}, 0, 0
    for *key, width in entries:
        if offset + width > 128:
            plane, offset = plane + 1, 0
        slots[tuple(key)] = (plane, offset, width)
        offset += width
    return slots, plane + 1


Y_SLOTS, Y_PLANES = y_slots()


def coarse_row(ref, k, r):
    return ref[k, pl.ds(r, Z, stride=CROWS), :]


def pack_y_kernel(*refs):
    fields, (material, ce_in, ch_in, cmat_in, prior_in) = refs[0:5], refs[5:10]
    to_first, to_second, firsts, lasts, mats, ce, ch, cmat, prior, sems = refs[10:20]
    even = lax.rem(lax.axis_index("gy"), 2) == 0
    pairs = []
    for a in range(5):
        pairs.append((fields[a].at[:, :, :, 0:128], firsts.at[a]))
        pairs.append((fields[a].at[:, :, :, OWN - 128 : OWN], lasts.at[a]))
    pairs.append((material.at[:, :, 0:128], mats.at[0]))
    pairs.append((material.at[:, :, OWN - 128 : OWN], mats.at[1]))
    pairs += [(ce_in, ce), (ch_in, ch), (cmat_in, cmat), (prior_in, prior)]
    copies = [pltpu.make_async_copy(src, dst, sems.at[i]) for i, (src, dst) in enumerate(pairs)]
    for copy in copies:
        copy.start()
    needs = {("f", a): [2 * a, 2 * a + 1] for a in range(5)}
    needs.update({("m", 0): [10, 11], ("c", 0): [12], ("c", 1): [13], ("cm", 0): [14], ("prior", 0): [15]})
    lane = lanes((Z, 128))
    built = {}
    for key, (plane, offset, width) in Y_SLOTS.items():
        kind, a, k, x = key
        for needed in needs.pop((kind, a), []):
            copies[needed].wait()
        if kind == "f":
            first, last = firsts[a, k, x], lasts[a, k, x]
        elif kind == "m":
            first, last = mats[0, x].astype(F32), mats[1, x].astype(F32)
        elif kind == "c":
            first = last = coarse_row((ce, ch)[a], k, x)
        elif kind == "cm":
            first = last = cmat[pl.ds(x, Z, stride=CROWS), :].astype(F32)
        else:
            first = last = jnp.concatenate([prior[...]] * (Z // 4), 0)
        pair = (rolled(first, offset, 1), rolled(last, offset + width, 1))
        if plane in built:
            keep = lane < offset
            pair = tuple(jnp.where(keep, old, new) for old, new in zip(built[plane], pair))
        built[plane] = pair
    for plane, (one, other) in built.items():
        to_first[plane] = jnp.where(even, other, one)
        to_second[plane] = jnp.where(even, one, other)


def with_ghosts(half, message, key, tile):
    plane, offset, width = Y_SLOTS[key]
    lane = lanes((Z, 128))
    if half == 0:
        return jnp.where(lane < 96, tile, rolled(message[plane], -offset - width, 1))
    return jnp.where(lane < 32, rolled(message[plane], -offset, 1), tile)


def load_kernel(*refs):
    own, material_in, coarse_in, tab = refs[0:5], refs[5], refs[6:10], refs[10]
    states = (refs[11:16], refs[16:21])
    c_halves, mat_halves, coarse = refs[21:23], refs[23:25], refs[25:29]
    material, sems = refs[29:31]
    first = pltpu.make_async_copy(material_in, material, sems.at[10])
    first.start()
    copies = []
    for half in range(2):
        for a in range(5):
            source = own[a].at[:, :, :, 128 * half : 128 * half + W]
            copies.append(pltpu.make_async_copy(source, states[half][a], sems.at[5 * half + a]))
            copies[-1].start()
    for i, (source, target) in enumerate(zip(coarse_in, coarse)):
        copies.append(pltpu.make_async_copy(source, target, sems.at[11 + i]))
        copies[-1].start()
    first.wait()
    for x in range(ROWS):
        for half in range(2):
            mat_halves[half][x] = material[x, :, 128 * half : 128 * half + W].astype(F32)
        for tile in range(3):
            index = material[x, :, 128 * tile : 128 * (tile + 1)]
            for k in range(6):
                value = lookup(tab, k, index)
                for half in range(2):
                    if tile in TILES[half]:
                        local_tile = TILES[half].index(tile)
                        c_halves[half][k, x, :, 128 * local_tile : 128 * (local_tile + 1)] = value
    for copy in copies:
        copy.wait()


E_ITEMS = [(("e", t, k), 9 - t, 8 - t, True) for t in range(RATIO) for k in (1, 2)]
H_ITEMS = [(("h", t, k), 8 - t, 8 - t, True) for t in range(RATIO) for k in (1, 2)]
COARSE_ITEMS = [(("c", 0, k), CGHOST, CGHOST, False) for k in (1, 2)]
MATERIAL_ITEM = [(("m", 0, 0), 8, 8, True)]


def x_places(half, items):
    places, half_slots, plane, offset = {}, [], 1, 0
    for name, lefts, rights, fine in items:
        mixed = (1 - half) if fine else 0
        segments = []
        if fine:
            segments.append((half, 0, plane, 0, 128))
            plane += 1
        if not half_slots:
            half_slots = [(plane, 0), (plane, 64)]
            plane += 1
        own_lane = 64 * half
        segments.append((mixed, own_lane, *half_slots.pop(0), 64))
        left_lane = 64 - lefts if half else 128 - lefts
        right_lane = 0 if half else 64
        for lane, length in ((left_lane, lefts), (right_lane, rights)):
            segments.append((mixed, lane, 0, offset, length))
            offset += length
        places[name] = segments
    assert offset <= 128
    return places, plane


def write_x(half, items, values):
    places, planes = x_places(half, items)
    lane = lanes((Z, 128))
    built_planes = []
    for plane in range(planes):
        parts = sorted(
            (there, name, tile, start)
            for name, segments in places.items()
            for tile, start, where, there, _ in segments
            if where == plane
        )
        built = None
        for there, name, tile, start in parts:
            value = rolled(values[name][:, 128 * tile : 128 * (tile + 1)], there - start, 1)
            built = value if built is None else jnp.where(lane < there, built, value)
        built_planes.append(built)
    return built_planes


def read_x(ref, half, items, name):
    lane = lanes((Z, 128))
    built = {}
    for tile, start, plane, there, _ in sorted(x_places(half, items)[0][name]):
        value = rolled(ref[plane], start - there, 1)
        built[tile] = value if tile not in built else jnp.where(lane < start, built[tile], value)
    return jnp.concatenate([built[tile] for tile in sorted(built)], 1)


def x_items(first):
    extra = MATERIAL_ITEM if first else []
    return E_ITEMS + COARSE_ITEMS + extra, H_ITEMS + COARSE_ITEMS + extra


def gather(value, index):
    return jnp.take_along_axis(value, index, axis=1, mode="promise_in_bounds")


def prolong_lanes(half, value):
    lane = lanes((8, 128))
    third = lambda number: (number * 21846) >> 16
    if half == 0:
        indices = [third(lane), jnp.where(lane < 96, third(lane + 128), 128 - third(130 - lane))]
    else:
        indices = [jnp.where(lane < 32, third(lane), third(lane + 128)), third(lane + 256)]
    return jnp.concatenate([gather(value, index) for index in indices], 1)


def restrict_lanes(half, value):
    three = value + rolled(value, -1, 1) + rolled(value, -2, 1)
    lane = lanes((8, 128))
    index = (lane * RATIO) & 127
    tiles = [gather(three[:, 128 * tile : 128 * (tile + 1)], index) for tile in range(2)]
    in_first = lane * RATIO < (128 if half == 0 else 256)
    return jnp.where(in_first, tiles[0], tiles[1]) * (1.0 / RATIO**3)


def sort_messages(received, sorted_refs):
    even = lax.rem(lax.axis_index("gx"), 2) == 0
    first, second = received
    from_left, from_right = sorted_refs
    for plane in range(first.shape[0]):
        from_left[plane] = jnp.where(even, second[plane], first[plane])
        from_right[plane] = jnp.where(even, first[plane], second[plane])
    return from_left, from_right


def interface_rows(ce):
    return jnp.concatenate([ce[k, r][0:1] for k in range(2) for r in range(CROWS)], 0)


def top_plane(pl_ref, x, t):
    r = x // RATIO
    out = []
    for k in range(2):
        row = 2 * k + r
        value = pl_ref[row : row + 1, :]
        if t:
            value = value + float(t) * pl_ref[4 + row : 5 + row, :]
        out.append(value)
    return out


def lookup(tab, row, index):
    entry = jnp.broadcast_to(tab[row : row + 1, :], (8, 128))
    rows = []
    for z in range(0, Z, 8):
        rows.append(
            jnp.concatenate(
                [
                    gather(entry, index[z : z + 8, lane : lane + 128])
                    for lane in range(0, index.shape[1], 128)
                ],
                1,
            )
        )
    return jnp.concatenate(rows, 0)


def row_of(ref, x):
    return [ref[k, x] for k in range(3)]


def send_edges(half, first, fields, c, ce, ch, pl_ref, mat, to_first, to_second):
    fe, fh, fj, fp, fv = fields
    none = (None, None)
    e_items, h_items = x_items(first)
    coef = lambda x: [c[k, x] for k in range(6)]
    states = lambda x: (row_of(fj, x), row_of(fp, x), row_of(fv, x))
    e0 = {x: row_of(fe, x) for x in range(ROWS)}
    low, high = {}, {}

    for k in (1, 2):
        low["e", 0, k] = e0[0][k]
    h1 = {x: h_row(row_of(fh, x), e0[x], e0[x + 1][1:], top_plane(pl_ref, x, 0)) for x in (0, 1)}
    e1, s1 = {}, {}
    e1[0], *s1[0] = e_row(e0[0], h1[0], none, *states(0), coef(0))
    e1[1], *s1[1] = e_row(e0[1], h1[1], h1[0][1:], *states(1), coef(1), (1, 2))
    h2 = h_row(h1[0], e1[0], e1[1][1:], top_plane(pl_ref, 0, 1))
    e2 = e_row(e1[0], h2, none, *s1[0], coef(0), (1, 2))[0]
    for k in (1, 2):
        low["e", 1, k] = e1[0][k]
        low["e", 2, k] = e2[k]
        low["c", 0, k] = ce[k, 0]

    a, b, d = ROWS - 3, ROWS - 2, ROWS - 1
    h1 = {
        a: h_row(row_of(fh, a), e0[a], e0[b][1:], top_plane(pl_ref, a, 0), (1, 2)),
        b: h_row(row_of(fh, b), e0[b], e0[d][1:], top_plane(pl_ref, b, 0)),
        d: h_row(row_of(fh, d), e0[d], none, top_plane(pl_ref, d, 0)),
    }
    e1, s1 = {}, {}
    e1[b], *s1[b] = e_row(e0[b], h1[b], h1[a][1:], *states(b), coef(b))
    e1[d], *s1[d] = e_row(e0[d], h1[d], h1[b][1:], *states(d), coef(d))
    h2 = {
        b: h_row(h1[b], e1[b], e1[d][1:], top_plane(pl_ref, b, 1), (1, 2)),
        d: h_row(h1[d], e1[d], none, top_plane(pl_ref, d, 1)),
    }
    e2 = e_row(e1[d], h2[d], h2[b][1:], *s1[d], coef(d))[0]
    h3 = h_row(h2[d], e2, none, top_plane(pl_ref, d, 2), (1, 2))
    ch_last = h_row(row_of(ch, CROWS - 1), row_of(ce, CROWS - 1), none, (0.0, 0.0), (1, 2))
    for k in (1, 2):
        high["h", 0, k] = h1[d][k]
        high["h", 1, k] = h2[d][k]
        high["h", 2, k] = h3[k]
        high["c", 0, k] = ch_last[k]
    if first:
        low["m", 0, 0] = mat[0]
        high["m", 0, 0] = mat[ROWS - 1]
    even = lax.rem(lax.axis_index("gx"), 2) == 0
    for first_part, second_part, plane in zip(write_x(half, h_items, high), write_x(half, e_items, low), range(99)):
        to_first[plane] = jnp.where(even, first_part, second_part)
        to_second[plane] = jnp.where(even, second_part, first_part)


def start_kernel(half, *refs):
    fields_in, (c_in, mat_in, ce_in, ch_in, cmat, prior, tab) = refs[0:5], refs[5:12]
    received, fields = refs[12:14], refs[14:19]
    c, ce, ch, inv, pl_ref, to_first, to_second, mat, message = refs[19:28]
    even = lax.rem(lax.axis_index("gy"), 2) == 0
    swap = even if half == 0 else jnp.logical_not(even)
    for plane in range(Y_PLANES):
        message[plane] = jnp.where(swap, received[1][plane], received[0][plane])
    outer = slice(128, 256) if half == 0 else slice(0, 128)
    inner = slice(0, 128) if half == 0 else slice(128, 256)
    for x in range(ROWS):
        value = with_ghosts(half, message, ("m", 0, 0, x), mat_in[x, :, outer])
        index = jnp.clip(value.astype(jnp.int32), 0, 127)
        if x in (0, ROWS - 1):
            mat[x, :, outer] = value
            mat[x, :, inner] = mat_in[x, :, inner]
        for k in range(6):
            c[k, x, :, outer] = lookup(tab, k, index)
    for a in range(5):
        for k in range(3):
            for x in range(ROWS):
                fields[a][k, x, :, outer] = with_ghosts(
                    half, message, ("f", a, k, x), fields_in[a][k, x, :, outer]
                )
    for a, (source, target) in enumerate(((ce_in, ce), (ch_in, ch))):
        for k in range(3):
            for r in range(CROWS):
                target[k, r] = with_ghosts(half, message, ("c", a, k, r), coarse_row(source, k, r))
    for r in range(CROWS):
        value = cmat[pl.ds(r, Z, stride=CROWS), :].astype(F32)
        index = with_ghosts(half, message, ("cm", 0, 0, r), value).astype(jnp.int32)
        inv[r] = lookup(tab, 7, jnp.clip(index, 0, 127))
    before = jnp.concatenate([prior[...]] * (Z // 4), 0)
    before = with_ghosts(half, message, ("prior", 0, 0, 0), before)[0:4]
    interface = interface_rows(ce)
    increment = (interface - before) * (1.0 / RATIO)
    pl_ref[...] = prolong_lanes(half, jnp.concatenate([interface, increment], 0))
    send_edges(half, True, fields, c, ce, ch, pl_ref, mat, to_first, to_second)


def coarse_step(half, first, olds, news, c, ghost, olds_c, news_c, inv, pl_ref, from_left, from_right, finished=None):
    e_items, h_items = x_items(first)
    zero = jnp.zeros((Z, W), F32)
    flat = (0.0, 0.0)
    (ce0, ch0), (ce, ch) = olds_c, news_c
    coarse_e0 = [row_of(ce0, r) for r in range(CROWS)]
    up = [read_x(from_right, half, e_items, ("c", 0, k)) for k in (1, 2)]
    down = [read_x(from_left, half, h_items, ("c", 0, k)) for k in (1, 2)]
    down = [down[0] + COURANT * coarse_e0[0][2], down[1] - COURANT * coarse_e0[0][1]]
    coarse_h = []
    for r in range(CROWS):
        following = coarse_e0[r + 1][1:] if r + 1 < CROWS else up
        coarse_h.append(h_row(row_of(ch0, r), coarse_e0[r], following, flat))
        for k in range(3):
            ch[k, r] = coarse_h[r][k]
    if finished:
        finished(-2)

    ge = gh = he = hh = None
    summed = [[None] * CROWS for _ in range(2)]
    for t in range(RATIO):
        fe, fh, fj, fp, fv = olds if t == 0 else news
        e_first = row_of(fe, 0)
        following = [read_x(from_right, half, e_items, ("e", t, k)) for k in (1, 2)]
        if t:
            following = [base + more for base, more in zip(following, he[1:])]
        far = [None, None]
        if t == 0:
            gh = [None, COURANT * e_first[2], -COURANT * e_first[1]]
        else:
            far = [COURANT * ge[2], -COURANT * ge[1]]
            old = [zero if value is None else value for value in gh]
            gh = h_row(old, ge, e_first[1:], flat, (0, 1, 2) if t < RATIO - 1 else (1, 2))
        preceding = [read_x(from_left, half, h_items, ("h", t, k)) + gh[k] for k in (1, 2)]
        current = e_first
        for x in range(ROWS):
            upper = row_of(fe, x + 1) if x + 1 < ROWS else None
            h = h_row(
                row_of(fh, x), row_of(fe, x), upper[1:] if upper else following, top_plane(pl_ref, x, t)
            )
            for k in range(3):
                news[1][k, x] = h[k]
            for k in range(2):
                part = h[k][8:Z]
                have = summed[k][x // RATIO]
                summed[k][x // RATIO] = part if have is None else have + part
        for x in range(ROWS):
            h = row_of(news[1], x)
            e2, j2, p2, v2 = e_row(
                row_of(fe, x), h, preceding, row_of(fj, x), row_of(fp, x), row_of(fv, x), [c[k, x] for k in range(6)]
            )
            for k in range(3):
                news[0][k, x] = e2[k]
                news[2][k, x] = j2[k]
                news[3][k, x] = p2[k]
                news[4][k, x] = v2[k]
            preceding = h[1:]
            if finished and t == RATIO - 1:
                finished(x)
        if t == 0:
            (a, b), (a2, b2) = [[ghost[k, side] for k in range(2)] for side in range(2)]
            ge = [
                a * ((gh[2] - left(gh[2])) - (gh[1] - below(gh[1], 0.0))),
                -a * gh[2],
                a * gh[1],
            ]
            he = [zero, a2 * preceding[1], -a2 * preceding[0]]
        elif t == 1:
            curl = curl_h(gh, far, flat)
            ge = [ge[k] + a * (curl[k] - b * ge[k]) for k in range(3)]
            hh = h_row([zero] * 3, he, (None, None), flat)
            curl = curl_h(hh, preceding, flat, (1, 2))
            he = [None] + [he[k] + a2 * (curl[k] - b2 * he[k]) for k in (1, 2)]

    rows = [summed[k][r][7:8] for k in range(2) for r in range(CROWS)]
    bottoms = restrict_lanes(half, jnp.concatenate(rows + rows, 0))
    preceding = down
    for r in range(CROWS):
        bottom = [bottoms[2 * k + r : 2 * k + r + 1, :] for k in range(2)]
        curl = curl_h(coarse_h[r], preceding, bottom)
        for k in range(3):
            ce[k, r] = coarse_e0[r][k] + inv[r] * curl[k]
        preceding = coarse_h[r][1:]
    if finished:
        finished(-1)


def ghost_coefficients(half, ghost, tab, from_left, from_right):
    e_items, h_items = x_items(True)
    for side, (ref, items) in enumerate(((from_left, h_items), (from_right, e_items))):
        index = jnp.clip(read_x(ref, half, items, ("m", 0, 0)).astype(jnp.int32), 0, 127)
        ghost[0, side] = lookup(tab, 0, index)
        ghost[1, side] = lookup(tab, 6, index)


def step_kernel(half, first, *refs):
    olds, rest = refs[0:5], refs[5:]
    c, ce0, ch0, inv, pl0, ghost_in = rest[0:6]
    from_left, from_right = sort_messages(rest[6:8], rest[-2:])
    news, rest = rest[8:13], rest[13:-2]
    if first:
        ce, ch, pl_ref, to_first, to_second, ghost = rest
        ghost_coefficients(half, ghost, ghost_in, from_left, from_right)
    else:
        ce, ch, pl_ref, to_first, to_second = rest
        ghost = ghost_in
    coarse_step(half, first, olds, news, c, ghost, (ce0, ch0), (ce, ch), inv, pl0, from_left, from_right)
    interface = interface_rows(ce)
    increment = (interface - interface_rows(ce0)) * (1.0 / RATIO)
    pl_ref[...] = prolong_lanes(half, jnp.concatenate([interface, increment], 0))
    send_edges(half, False, news, c, ce, ch, pl_ref, None, to_first, to_second)


def final_kernel(half, *refs):
    olds, rest = refs[0:5], refs[5:]
    c, ce0, ch0, inv, pl0, ghost = rest[0:6]
    received, rest = rest[6:8], rest[8:]
    if half == 0:
        outs, news, ce, ch = rest[0:5], rest[5:10], rest[10], rest[11]
        rest = rest[12:]
    else:
        others, others_c = rest[5:10], rest[10:12]
        outs, outs_c, news, ce, ch = rest[12:17], rest[17:19], rest[19:24], rest[24], rest[25]
        coarse_parts = rest[26:28]
        rest = rest[28:]
    sorted_refs, sems = rest[0:2], rest[2]
    from_left, from_right = sort_messages(received, sorted_refs)
    first = lanes((Z, 128)) < 64
    copies = []

    def coarse_finished(a):
        if half == 0:
            return
        for k in range(3):
            for r in range(CROWS):
                value = jnp.where(first, others_c[a][k, r], (ce, ch)[a][k, r])
                coarse_parts[a][k, pl.ds(r, Z, stride=CROWS), :] = value
        copies.append(pltpu.make_async_copy(coarse_parts[a], outs_c[a], sems.at[ROWS, a]))
        copies[-1].start()

    def finished(x):
        if x < 0:
            return coarse_finished(-x - 1)
        for a in range(5):
            if half == 0:
                source = news[a].at[:, x, :, 0:128]
                target = outs[a].at[:, x, :, 0:128]
            else:
                for k in range(3):
                    news[a][k, x, :, 0:128] = jnp.where(
                        first, others[a][k, x, :, 128:256], news[a][k, x, :, 0:128]
                    )
                source = news[a].at[:, x]
                target = outs[a].at[:, x, :, 128:384]
            copies.append(pltpu.make_async_copy(source, target, sems.at[x, a]))
            copies[-1].start()

    coarse_step(
        half, False, olds, news, c, ghost, (ce0, ch0), (ce, ch), inv, pl0, from_left, from_right, finished
    )
    for copy in copies:
        copy.wait()


FULL = pl.BlockSpec(memory_space=pltpu.VMEM)
RAW = pl.BlockSpec(memory_space=pltpu.HBM)
COST = pl.CostEstimate(flops=4_000_000, transcendentals=0, bytes_accessed=8_000_000)
FIELD = (3, ROWS, Z, W)
COEF = (6, ROWS, Z, W)
COARSE = (3, CROWS, Z, CW)
PLANES = (8, W)


def call(kernel, outs, args, specs=None, scratch=(), aliases=None, vmem=16, out_specs=None):
    outs = [dims if isinstance(dims, jax.ShapeDtypeStruct) else jax.ShapeDtypeStruct(dims, F32) for dims in outs]
    return pl.pallas_call(
        kernel,
        out_shape=outs,
        in_specs=specs or [FULL] * len(args),
        out_specs=out_specs or [FULL] * len(outs),
        scratch_shapes=list(scratch),
        input_output_aliases=aliases or {},
        compiler_params=pltpu.CompilerParams(vmem_limit_bytes=vmem * 1024 * 1024),
        cost_estimate=COST,
    )(*args)


def table(permittivity, plasma, damping, strength, resonance, linewidth):
    half_step = 0.5 * TIMESTEP
    c2 = plasma * plasma * TIMESTEP / (1.0 + damping * half_step)
    c4 = TIMESTEP * resonance * resonance / (1.0 + linewidth * half_step)
    rows = jnp.stack(
        [
            TIMESTEP / permittivity,
            (1.0 - damping * half_step) / (1.0 + damping * half_step),
            c2,
            (1.0 - linewidth * half_step) / (1.0 + linewidth * half_step),
            c4,
            strength,
            c2 + c4 * strength,
            COURANT / permittivity,
        ]
    )
    return jnp.pad(rows, ((0, 0), (0, 120)))


def message_shapes(half, first):
    return [(x_places(half, items)[1], Z, 128) for items in x_items(first)]


def exchanged(messages, axis):
    count = lax.axis_size(axis)
    swapped = []
    for message, first in zip(messages, (0, 1)):
        pairs = [((first + i) % count, (first + (i ^ 1)) % count) for i in range(count)]
        swapped.append(lax.ppermute(message, axis, pairs))
    return swapped


def local(
    fine_e,
    fine_h,
    drude_current,
    lorentz_pol,
    lorentz_rate,
    material,
    permittivity,
    plasma,
    damping,
    strength,
    resonance,
    linewidth,
    coarse_e,
    coarse_h,
    coarse_material,
    coarse_prior,
):
    fields = [
        jnp.transpose(value, (0, 2, 1, 3))
        for value in (fine_e, fine_h, drude_current, lorentz_pol, lorentz_rate)
    ]
    mat = jnp.transpose(material, (1, 0, 2))
    ce = coarse_e.reshape(3, Z * CROWS, 128)
    ch = coarse_h.reshape(3, Z * CROWS, 128)
    cmat = coarse_material.reshape(Z * CROWS, 128)
    prior = coarse_prior.reshape(2 * CROWS, 128)
    in_hbm = lambda values: [pltpu.with_memory_space_constraint(value, pltpu.HBM) for value in values]
    fields, coarse = in_hbm(fields), in_hbm([ce, ch, cmat, prior])
    (mat,) = in_hbm([mat])
    tab = table(permittivity, plasma, damping, strength, resonance, linewidth)

    vmem = lambda *dims: pltpu.VMEM(dims, F32)
    packed = call(
        pack_y_kernel,
        [(Y_PLANES, Z, 128)] * 2,
        [*fields, mat, *coarse],
        [RAW] * 10,
        [
            vmem(5, 3, ROWS, Z, 128),
            vmem(5, 3, ROWS, Z, 128),
            pltpu.VMEM((2, ROWS, Z, 128), jnp.int32),
            vmem(*ce.shape),
            vmem(*ch.shape),
            pltpu.VMEM(cmat.shape, jnp.int32),
            vmem(*prior.shape),
            pltpu.SemaphoreType.DMA((16,)),
        ],
        vmem=16,
    )
    received = exchanged(packed, "gy")
    loaded = call(
        load_kernel,
        [FIELD] * 10
        + [COEF] * 2
        + [(ROWS, Z, W)] * 2
        + [jax.ShapeDtypeStruct(value.shape, value.dtype) for value in coarse],
        [*fields, mat, *coarse, tab],
        [RAW] * 10 + [FULL],
        [pltpu.VMEM((ROWS, Z, OWN), jnp.int32), pltpu.SemaphoreType.DMA((15,))],
    )
    parts, waiting = [None, None], [None, None]
    for half in range(2):
        state = loaded[5 * half : 5 * half + 5]
        out = call(
            functools.partial(start_kernel, half),
            [FIELD] * 5 + [COEF, COARSE, COARSE, (CROWS, Z, CW), PLANES] + message_shapes(half, True),
            [*state, loaded[10 + half], loaded[12 + half], *loaded[14:18], tab, *received],
            scratch=[vmem(ROWS, Z, W), vmem(Y_PLANES, Z, 128)],
            aliases={index: index for index in range(6)},
        )
        parts[half] = (out[0:5], out[5:10], tab)
        waiting[half] = exchanged(out[10:12], "gx")
    for step in range(STEPS - 1):
        for half in range(2):
            state, (c, ce, ch, inv, planes), ghost = parts[half]
            out = call(
                functools.partial(step_kernel, half, step == 0),
                [FIELD] * 5
                + [COARSE, COARSE, PLANES]
                + message_shapes(half, False)
                + ([(2, 2, Z, W)] if step == 0 else []),
                [*state, c, ce, ch, inv, planes, ghost, *waiting[half]],
                scratch=[vmem(*message.shape) for message in waiting[half]],
            )
            if step == 0:
                ghost = out[10]
            parts[half] = (out[0:5], (c, out[5], out[6], inv, out[7]), ghost)
            waiting[half] = exchanged(out[8:10], "gx")
    whole = [(3, ROWS, Z, OWN)] * 5
    done = []
    for half in range(2):
        state, coarse, ghost = parts[half]
        args = [*state, *coarse, ghost, *waiting[half], *done]
        done = call(
            functools.partial(final_kernel, half),
            whole + ([(3, Z * CROWS, 128)] * 2 if half else [FIELD] * 5 + [COARSE] * 2),
            args,
            specs=[RAW if 13 <= i < 18 else FULL for i in range(len(args))],
            out_specs=[RAW] * 7 if half else [RAW] * 5 + [FULL] * 7,
            scratch=([vmem(*FIELD)] * 5 + [vmem(*COARSE)] * 2 + [vmem(3, Z * CROWS, 128)] * 2 if half else [])
            + [vmem(*message.shape) for message in waiting[half]]
            + [pltpu.SemaphoreType.DMA((ROWS + 1, 5))],
            aliases={13 + i: i for i in range(5)} if half else None,
        )
    fine = [jnp.transpose(value, (0, 2, 1, 3)) for value in done[0:5]]
    coarse = [value.reshape(3, Z, CROWS, 128) for value in done[5:7]]
    return (*fine, *coarse)


def solution(mesh):
    field = P(None, None, "gx", "gy")
    plane = P(None, "gx", "gy")
    in_specs = (field,) * 5 + (plane,) + (P(),) * 6 + (field, field, plane, plane)
    return jax.shard_map(local, mesh=mesh, in_specs=in_specs, out_specs=(field,) * 7, check_vma=False)
```

```python
import functools

import jax
import jax.numpy as jnp
from jax import lax
from jax.experimental import pallas as pl
from jax.experimental.pallas import tpu as pltpu
from jax.sharding import PartitionSpec as P

RATIO = 3
STEPS = 3
COURANT = 0.5
TIMESTEP = 0.5

Z = 16
ROWS = 6
OWN = 384
W = 256
CROWS = 2
CW = 128
GHOST = 9
CGHOST = 3
TILES = ((0, 1), (1, 2))
F32 = jnp.float32


def rolled(value, shift, axis):
    shift %= value.shape[axis]
    return value if shift == 0 else pltpu.roll(value, shift, axis)


def lanes(shape):
    return lax.broadcasted_iota(jnp.int32, shape, len(shape) - 1)


def right(value):
    return rolled(value, -1, 1)


def left(value):
    return rolled(value, 1, 1)


def above(value, top):
    sublane = lax.broadcasted_iota(jnp.int32, value.shape, 0)
    return jnp.where(sublane == Z - 1, top, rolled(value, -1, 0))


def below(value, bottom):
    sublane = lax.broadcasted_iota(jnp.int32, value.shape, 0)
    return jnp.where(sublane == 0, bottom, rolled(value, 1, 0))


def minus(first, second):
    if first is None:
        return None if second is None else -second
    return first if second is None else first - second


def h_row(h, e, following, top, wanted=(0, 1, 2)):
    ex, ey, ez = e
    next_y, next_z = following
    out = [None, None, None]
    if 0 in wanted:
        out[0] = h[0] - COURANT * ((right(ez) - ez) - (above(ey, top[1]) - ey))
    if 1 in wanted:
        out[1] = h[1] - COURANT * ((above(ex, top[0]) - ex) - minus(next_z, ez))
    if 2 in wanted:
        out[2] = h[2] - COURANT * (minus(next_y, ey) - (right(ex) - ex))
    return out


def curl_h(h, preceding, bottom, wanted=(0, 1, 2)):
    hx, hy, hz = h
    prev_y, prev_z = preceding
    out = [None, None, None]
    if 0 in wanted:
        out[0] = (hz - left(hz)) - (hy - below(hy, bottom[1]))
    if 1 in wanted:
        out[1] = (hx - below(hx, bottom[0])) - minus(hz, prev_z)
    if 2 in wanted:
        out[2] = minus(hy, prev_y) - (hx - left(hx))
    return out


def e_row(e, h, preceding, j, p, v, c, wanted=(0, 1, 2)):
    curl = curl_h(h, preceding, (0.0, 0.0), wanted)
    e2, j2, p2, v2 = [None] * 3, [None] * 3, [None] * 3, [None] * 3
    for k in wanted:
        v2[k] = c[3] * v[k] + c[4] * (c[5] * e[k] - p[k])
        j2[k] = c[1] * j[k] + c[2] * e[k]
        p2[k] = p[k] + TIMESTEP * v2[k]
        e2[k] = e[k] + c[0] * (curl[k] - j2[k] - v2[k])
    return e2, j2, p2, v2


def y_slots():
    entries = [("f", a, k, x, GHOST) for a in range(5) for k in range(3) for x in range(ROWS)]
    entries += [("m", 0, 0, x, GHOST) for x in range(ROWS)]
    entries += [("c", a, k, r, CGHOST) for a in range(2) for k in range(3) for r in range(CROWS)]
    entries += [("cm", 0, 0, r, CGHOST) for r in range(CROWS)]
    entries += [("prior", 0, 0, 0, CGHOST)]
    slots, plane, offset = {}, 0, 0
    for *key, width in entries:
        if offset + width > 128:
            plane, offset = plane + 1, 0
        slots[tuple(key)] = (plane, offset, width)
        offset += width
    return slots, plane + 1


Y_SLOTS, Y_PLANES = y_slots()


def coarse_row(ref, k, r):
    return ref[k, pl.ds(r, Z, stride=CROWS), :]


def pack_y_kernel(*refs):
    fields, (material, ce_in, ch_in, cmat_in, prior_in) = refs[0:5], refs[5:10]
    to_first, to_second, firsts, lasts, mats, ce, ch, cmat, prior, sems = refs[10:20]
    even = lax.rem(lax.axis_index("gy"), 2) == 0
    pairs = []
    for a in range(5):
        pairs.append((fields[a].at[:, :, :, 0:128], firsts.at[a]))
        pairs.append((fields[a].at[:, :, :, OWN - 128 : OWN], lasts.at[a]))
    pairs.append((material.at[:, :, 0:128], mats.at[0]))
    pairs.append((material.at[:, :, OWN - 128 : OWN], mats.at[1]))
    pairs += [(ce_in, ce), (ch_in, ch), (cmat_in, cmat), (prior_in, prior)]
    copies = [pltpu.make_async_copy(src, dst, sems.at[i]) for i, (src, dst) in enumerate(pairs)]
    for copy in copies:
        copy.start()
    for copy in copies:
        copy.wait()
    lane = lanes((Z, 128))
    built = {}
    for key, (plane, offset, width) in Y_SLOTS.items():
        kind, a, k, x = key
        if kind == "f":
            first, last = firsts[a, k, x], lasts[a, k, x]
        elif kind == "m":
            first, last = mats[0, x].astype(F32), mats[1, x].astype(F32)
        elif kind == "c":
            first = last = coarse_row((ce, ch)[a], k, x)
        elif kind == "cm":
            first = last = cmat[pl.ds(x, Z, stride=CROWS), :].astype(F32)
        else:
            first = last = jnp.concatenate([prior[...]] * (Z // 4), 0)
        pair = (rolled(first, offset, 1), rolled(last, offset + width, 1))
        if plane in built:
            keep = lane < offset
            pair = tuple(jnp.where(keep, old, new) for old, new in zip(built[plane], pair))
        built[plane] = pair
    for plane, (one, other) in built.items():
        to_first[plane] = jnp.where(even, other, one)
        to_second[plane] = jnp.where(even, one, other)


def with_ghosts(half, message, key, tile):
    plane, offset, width = Y_SLOTS[key]
    lane = lanes((Z, 128))
    if half == 0:
        return jnp.where(lane < 96, tile, rolled(message[plane], -offset - width, 1))
    return jnp.where(lane < 32, rolled(message[plane], -offset, 1), tile)


def load_kernel(*refs):
    own, material_in, coarse_in, tab = refs[0:5], refs[5], refs[6:10], refs[10]
    states = (refs[11:16], refs[16:21])
    c_halves, mat_halves, coarse = refs[21:23], refs[23:25], refs[25:29]
    material, sems = refs[29:31]
    first = pltpu.make_async_copy(material_in, material, sems.at[10])
    first.start()
    copies = []
    for half in range(2):
        for a in range(5):
            source = own[a].at[:, :, :, 128 * half : 128 * half + W]
            copies.append(pltpu.make_async_copy(source, states[half][a], sems.at[5 * half + a]))
            copies[-1].start()
    for i, (source, target) in enumerate(zip(coarse_in, coarse)):
        copies.append(pltpu.make_async_copy(source, target, sems.at[11 + i]))
        copies[-1].start()
    first.wait()
    for x in range(ROWS):
        for half in range(2):
            mat_halves[half][x] = material[x, :, 128 * half : 128 * half + W].astype(F32)
        for tile in range(3):
            index = material[x, :, 128 * tile : 128 * (tile + 1)]
            for k in range(6):
                value = lookup(tab, k, index)
                for half in range(2):
                    if tile in TILES[half]:
                        local_tile = TILES[half].index(tile)
                        c_halves[half][k, x, :, 128 * local_tile : 128 * (local_tile + 1)] = value
    for copy in copies:
        copy.wait()


E_ITEMS = [(("e", t, k), 9 - t, 8 - t, True) for t in range(RATIO) for k in (1, 2)]
H_ITEMS = [(("h", t, k), 8 - t, 8 - t, True) for t in range(RATIO) for k in (1, 2)]
COARSE_ITEMS = [(("c", 0, k), CGHOST, CGHOST, False) for k in (1, 2)]
MATERIAL_ITEM = [(("m", 0, 0), 8, 8, True)]


def x_places(half, items):
    places, half_slots, plane, offset = {}, [], 1, 0
    for name, lefts, rights, fine in items:
        mixed = (1 - half) if fine else 0
        segments = []
        if fine:
            segments.append((half, 0, plane, 0, 128))
            plane += 1
        if not half_slots:
            half_slots = [(plane, 0), (plane, 64)]
            plane += 1
        own_lane = 64 * half
        segments.append((mixed, own_lane, *half_slots.pop(0), 64))
        left_lane = 64 - lefts if half else 128 - lefts
        right_lane = 0 if half else 64
        for lane, length in ((left_lane, lefts), (right_lane, rights)):
            segments.append((mixed, lane, 0, offset, length))
            offset += length
        places[name] = segments
    assert offset <= 128
    return places, plane


def write_x(half, items, values):
    places, planes = x_places(half, items)
    lane = lanes((Z, 128))
    built_planes = []
    for plane in range(planes):
        parts = sorted(
            (there, name, tile, start)
            for name, segments in places.items()
            for tile, start, where, there, _ in segments
            if where == plane
        )
        built = None
        for there, name, tile, start in parts:
            value = rolled(values[name][:, 128 * tile : 128 * (tile + 1)], there - start, 1)
            built = value if built is None else jnp.where(lane < there, built, value)
        built_planes.append(built)
    return built_planes


def read_x(ref, half, items, name):
    lane = lanes((Z, 128))
    built = {}
    for tile, start, plane, there, _ in sorted(x_places(half, items)[0][name]):
        value = rolled(ref[plane], start - there, 1)
        built[tile] = value if tile not in built else jnp.where(lane < start, built[tile], value)
    return jnp.concatenate([built[tile] for tile in sorted(built)], 1)


def x_items(first):
    extra = MATERIAL_ITEM if first else []
    return E_ITEMS + COARSE_ITEMS + extra, H_ITEMS + COARSE_ITEMS + extra


def gather(value, index):
    return jnp.take_along_axis(value, index, axis=1, mode="promise_in_bounds")


def prolong_lanes(half, value):
    lane = lanes((8, 128))
    third = lambda number: (number * 21846) >> 16
    if half == 0:
        indices = [third(lane), jnp.where(lane < 96, third(lane + 128), 128 - third(130 - lane))]
    else:
        indices = [jnp.where(lane < 32, third(lane), third(lane + 128)), third(lane + 256)]
    return jnp.concatenate([gather(value, index) for index in indices], 1)


def restrict_lanes(half, value):
    three = value + rolled(value, -1, 1) + rolled(value, -2, 1)
    lane = lanes((8, 128))
    index = (lane * RATIO) & 127
    tiles = [gather(three[:, 128 * tile : 128 * (tile + 1)], index) for tile in range(2)]
    in_first = lane * RATIO < (128 if half == 0 else 256)
    return jnp.where(in_first, tiles[0], tiles[1]) * (1.0 / RATIO**3)


def sort_messages(received, sorted_refs):
    even = lax.rem(lax.axis_index("gx"), 2) == 0
    first, second = received
    from_left, from_right = sorted_refs
    for plane in range(first.shape[0]):
        from_left[plane] = jnp.where(even, second[plane], first[plane])
        from_right[plane] = jnp.where(even, first[plane], second[plane])
    return from_left, from_right


def interface_rows(ce):
    return jnp.concatenate([ce[k, r][0:1] for k in range(2) for r in range(CROWS)], 0)


def top_plane(pl_ref, x, t):
    r = x // RATIO
    out = []
    for k in range(2):
        row = 2 * k + r
        value = pl_ref[row : row + 1, :]
        if t:
            value = value + float(t) * pl_ref[4 + row : 5 + row, :]
        out.append(value)
    return out


def lookup(tab, row, index):
    entry = jnp.broadcast_to(tab[row : row + 1, :], (8, 128))
    rows = []
    for z in range(0, Z, 8):
        rows.append(
            jnp.concatenate(
                [
                    gather(entry, index[z : z + 8, lane : lane + 128])
                    for lane in range(0, index.shape[1], 128)
                ],
                1,
            )
        )
    return jnp.concatenate(rows, 0)


def row_of(ref, x):
    return [ref[k, x] for k in range(3)]


def send_edges(half, first, fields, c, ce, ch, pl_ref, mat, to_first, to_second):
    fe, fh, fj, fp, fv = fields
    none = (None, None)
    e_items, h_items = x_items(first)
    coef = lambda x: [c[k, x] for k in range(6)]
    states = lambda x: (row_of(fj, x), row_of(fp, x), row_of(fv, x))
    e0 = {x: row_of(fe, x) for x in range(ROWS)}
    low, high = {}, {}

    for k in (1, 2):
        low["e", 0, k] = e0[0][k]
    h1 = {x: h_row(row_of(fh, x), e0[x], e0[x + 1][1:], top_plane(pl_ref, x, 0)) for x in (0, 1)}
    e1, s1 = {}, {}
    e1[0], *s1[0] = e_row(e0[0], h1[0], none, *states(0), coef(0))
    e1[1], *s1[1] = e_row(e0[1], h1[1], h1[0][1:], *states(1), coef(1), (1, 2))
    h2 = h_row(h1[0], e1[0], e1[1][1:], top_plane(pl_ref, 0, 1))
    e2 = e_row(e1[0], h2, none, *s1[0], coef(0), (1, 2))[0]
    for k in (1, 2):
        low["e", 1, k] = e1[0][k]
        low["e", 2, k] = e2[k]
        low["c", 0, k] = ce[k, 0]

    a, b, d = ROWS - 3, ROWS - 2, ROWS - 1
    h1 = {
        a: h_row(row_of(fh, a), e0[a], e0[b][1:], top_plane(pl_ref, a, 0), (1, 2)),
        b: h_row(row_of(fh, b), e0[b], e0[d][1:], top_plane(pl_ref, b, 0)),
        d: h_row(row_of(fh, d), e0[d], none, top_plane(pl_ref, d, 0)),
    }
    e1, s1 = {}, {}
    e1[b], *s1[b] = e_row(e0[b], h1[b], h1[a][1:], *states(b), coef(b))
    e1[d], *s1[d] = e_row(e0[d], h1[d], h1[b][1:], *states(d), coef(d))
    h2 = {
        b: h_row(h1[b], e1[b], e1[d][1:], top_plane(pl_ref, b, 1), (1, 2)),
        d: h_row(h1[d], e1[d], none, top_plane(pl_ref, d, 1)),
    }
    e2 = e_row(e1[d], h2[d], h2[b][1:], *s1[d], coef(d))[0]
    h3 = h_row(h2[d], e2, none, top_plane(pl_ref, d, 2), (1, 2))
    ch_last = h_row(row_of(ch, CROWS - 1), row_of(ce, CROWS - 1), none, (0.0, 0.0), (1, 2))
    for k in (1, 2):
        high["h", 0, k] = h1[d][k]
        high["h", 1, k] = h2[d][k]
        high["h", 2, k] = h3[k]
        high["c", 0, k] = ch_last[k]
    if first:
        low["m", 0, 0] = mat[0]
        high["m", 0, 0] = mat[ROWS - 1]
    even = lax.rem(lax.axis_index("gx"), 2) == 0
    for first_part, second_part, plane in zip(write_x(half, h_items, high), write_x(half, e_items, low), range(99)):
        to_first[plane] = jnp.where(even, first_part, second_part)
        to_second[plane] = jnp.where(even, second_part, first_part)


def start_kernel(half, *refs):
    fields_in, (c_in, mat_in, ce_in, ch_in, cmat, prior, tab) = refs[0:5], refs[5:12]
    received, fields = refs[12:14], refs[14:19]
    c, ce, ch, inv, pl_ref, to_first, to_second, mat, message = refs[19:28]
    even = lax.rem(lax.axis_index("gy"), 2) == 0
    swap = even if half == 0 else jnp.logical_not(even)
    for plane in range(Y_PLANES):
        message[plane] = jnp.where(swap, received[1][plane], received[0][plane])
    outer = slice(128, 256) if half == 0 else slice(0, 128)
    inner = slice(0, 128) if half == 0 else slice(128, 256)
    for x in (0, ROWS - 1):
        mat[x, :, outer] = with_ghosts(half, message, ("m", 0, 0, x), mat_in[x, :, outer])
        mat[x, :, inner] = mat_in[x, :, inner]
    (packed_plane,) = {Y_SLOTS["m", 0, 0, x][0] for x in range(ROWS)}
    index = jnp.clip(message[packed_plane].astype(jnp.int32), 0, 127)
    for k in range(6):
        packed = {packed_plane: lookup(tab, k, index)}
        for x in range(ROWS):
            c[k, x, :, outer] = with_ghosts(half, packed, ("m", 0, 0, x), c_in[k, x, :, outer])
    for a in range(5):
        for k in range(3):
            for x in range(ROWS):
                fields[a][k, x, :, outer] = with_ghosts(
                    half, message, ("f", a, k, x), fields_in[a][k, x, :, outer]
                )
    for a, (source, target) in enumerate(((ce_in, ce), (ch_in, ch))):
        for k in range(3):
            for r in range(CROWS):
                target[k, r] = with_ghosts(half, message, ("c", a, k, r), coarse_row(source, k, r))
    for r in range(CROWS):
        value = cmat[pl.ds(r, Z, stride=CROWS), :].astype(F32)
        index = with_ghosts(half, message, ("cm", 0, 0, r), value).astype(jnp.int32)
        inv[r] = lookup(tab, 7, jnp.clip(index, 0, 127))
    before = jnp.concatenate([prior[...]] * (Z // 4), 0)
    before = with_ghosts(half, message, ("prior", 0, 0, 0), before)[0:4]
    interface = interface_rows(ce)
    increment = (interface - before) * (1.0 / RATIO)
    pl_ref[...] = prolong_lanes(half, jnp.concatenate([interface, increment], 0))
    send_edges(half, True, fields, c, ce, ch, pl_ref, mat, to_first, to_second)


def coarse_step(half, first, olds, news, c, ghost, olds_c, news_c, inv, pl_ref, from_left, from_right, finished=None):
    e_items, h_items = x_items(first)
    zero = jnp.zeros((Z, W), F32)
    flat = (0.0, 0.0)
    (ce0, ch0), (ce, ch) = olds_c, news_c
    coarse_e0 = [row_of(ce0, r) for r in range(CROWS)]
    up = [read_x(from_right, half, e_items, ("c", 0, k)) for k in (1, 2)]
    down = [read_x(from_left, half, h_items, ("c", 0, k)) for k in (1, 2)]
    down = [down[0] + COURANT * coarse_e0[0][2], down[1] - COURANT * coarse_e0[0][1]]
    coarse_h = []
    for r in range(CROWS):
        following = coarse_e0[r + 1][1:] if r + 1 < CROWS else up
        coarse_h.append(h_row(row_of(ch0, r), coarse_e0[r], following, flat))
        for k in range(3):
            ch[k, r] = coarse_h[r][k]
    if finished:
        finished((6,))

    ge = gh = he = hh = None
    summed = [[None] * CROWS for _ in range(2)]
    for t in range(RATIO):
        fe, fh, fj, fp, fv = olds if t == 0 else news
        e_first = row_of(fe, 0)
        following = [read_x(from_right, half, e_items, ("e", t, k)) for k in (1, 2)]
        if t:
            following = [base + more for base, more in zip(following, he[1:])]
        far = [None, None]
        if t == 0:
            gh = [None, COURANT * e_first[2], -COURANT * e_first[1]]
        else:
            far = [COURANT * ge[2], -COURANT * ge[1]]
            old = [zero if value is None else value for value in gh]
            gh = h_row(old, ge, e_first[1:], flat, (0, 1, 2) if t < RATIO - 1 else (1, 2))
        preceding = [read_x(from_left, half, h_items, ("h", t, k)) + gh[k] for k in (1, 2)]
        current = e_first
        last = finished is not None and t == RATIO - 1
        if last:
            for x in range(ROWS):
                for k in range(3):
                    v2 = c[3, x] * fv[k, x] + c[4, x] * (c[5, x] * fe[k, x] - fp[k, x])
                    news[2][k, x] = c[1, x] * fj[k, x] + c[2, x] * fe[k, x]
                    news[3][k, x] = fp[k, x] + TIMESTEP * v2
                    news[4][k, x] = v2
            finished((2, 3, 4))
        for x in range(ROWS):
            upper = row_of(fe, x + 1) if x + 1 < ROWS else None
            h = h_row(
                row_of(fh, x), row_of(fe, x), upper[1:] if upper else following, top_plane(pl_ref, x, t)
            )
            for k in range(3):
                news[1][k, x] = h[k]
            for k in range(2):
                part = h[k][8:Z]
                have = summed[k][x // RATIO]
                summed[k][x // RATIO] = part if have is None else have + part
        if last:
            finished((1,))
        for x in range(ROWS):
            h = row_of(news[1], x)
            if last:
                curl = curl_h(h, preceding, flat)
                for k in range(3):
                    news[0][k, x] = fe[k, x] + c[0, x] * (curl[k] - fj[k, x] - fv[k, x])
                preceding = h[1:]
                continue
            e2, j2, p2, v2 = e_row(
                row_of(fe, x), h, preceding, row_of(fj, x), row_of(fp, x), row_of(fv, x), [c[k, x] for k in range(6)]
            )
            for k in range(3):
                news[0][k, x] = e2[k]
                news[2][k, x] = j2[k]
                news[3][k, x] = p2[k]
                news[4][k, x] = v2[k]
            preceding = h[1:]
        if last:
            finished((0,))
        if t == 0:
            (a, b), (a2, b2) = [[ghost[k, side] for k in range(2)] for side in range(2)]
            ge = [
                a * ((gh[2] - left(gh[2])) - (gh[1] - below(gh[1], 0.0))),
                -a * gh[2],
                a * gh[1],
            ]
            he = [zero, a2 * preceding[1], -a2 * preceding[0]]
        elif t == 1:
            curl = curl_h(gh, far, flat)
            ge = [ge[k] + a * (curl[k] - b * ge[k]) for k in range(3)]
            hh = h_row([zero] * 3, he, (None, None), flat)
            curl = curl_h(hh, preceding, flat, (1, 2))
            he = [None] + [he[k] + a2 * (curl[k] - b2 * he[k]) for k in (1, 2)]

    rows = [summed[k][r][7:8] for k in range(2) for r in range(CROWS)]
    bottoms = restrict_lanes(half, jnp.concatenate(rows + rows, 0))
    preceding = down
    for r in range(CROWS):
        bottom = [bottoms[2 * k + r : 2 * k + r + 1, :] for k in range(2)]
        curl = curl_h(coarse_h[r], preceding, bottom)
        for k in range(3):
            ce[k, r] = coarse_e0[r][k] + inv[r] * curl[k]
        preceding = coarse_h[r][1:]
    if finished:
        finished((5,))


def ghost_coefficients(half, ghost, tab, from_left, from_right):
    e_items, h_items = x_items(True)
    for side, (ref, items) in enumerate(((from_left, h_items), (from_right, e_items))):
        index = jnp.clip(read_x(ref, half, items, ("m", 0, 0)).astype(jnp.int32), 0, 127)
        ghost[0, side] = lookup(tab, 0, index)
        ghost[1, side] = lookup(tab, 6, index)


def step_kernel(half, first, *refs):
    olds, rest = refs[0:5], refs[5:]
    c, ce0, ch0, inv, pl0, ghost_in = rest[0:6]
    from_left, from_right = sort_messages(rest[6:8], rest[-2:])
    news, rest = rest[8:13], rest[13:-2]
    if first:
        ce, ch, pl_ref, to_first, to_second, ghost = rest
        ghost_coefficients(half, ghost, ghost_in, from_left, from_right)
    else:
        ce, ch, pl_ref, to_first, to_second = rest
        ghost = ghost_in
    coarse_step(half, first, olds, news, c, ghost, (ce0, ch0), (ce, ch), inv, pl0, from_left, from_right)
    interface = interface_rows(ce)
    increment = (interface - interface_rows(ce0)) * (1.0 / RATIO)
    pl_ref[...] = prolong_lanes(half, jnp.concatenate([interface, increment], 0))
    send_edges(half, False, news, c, ce, ch, pl_ref, None, to_first, to_second)


def final_kernel(half, *refs):
    olds, rest = refs[0:5], refs[5:]
    c, ce0, ch0, inv, pl0, ghost = rest[0:6]
    received, rest = rest[6:8], rest[8:]
    if half == 0:
        outs, news, ce, ch = rest[0:5], rest[5:10], rest[10], rest[11]
        rest = rest[12:]
    else:
        others, others_c = rest[5:10], rest[10:12]
        outs, outs_c, news, ce, ch = rest[12:17], rest[17:19], rest[19:24], rest[24], rest[25]
        coarse_parts = rest[26:28]
        rest = rest[28:]
    sorted_refs, sems = rest[0:2], rest[2]
    from_left, from_right = sort_messages(received, sorted_refs)
    first = lanes((Z, 128)) < 64
    copies = []

    def coarse_finished(a):
        if half == 0:
            return
        for k in range(3):
            for r in range(CROWS):
                value = jnp.where(first, others_c[a][k, r], (ce, ch)[a][k, r])
                coarse_parts[a][k, pl.ds(r, Z, stride=CROWS), :] = value
        copies.append(pltpu.make_async_copy(coarse_parts[a], outs_c[a], sems.at[5 + a]))
        copies[-1].start()

    def finished(arrays):
        for a in arrays:
            if a >= 5:
                coarse_finished(a - 5)
                continue
            if half == 0:
                source, target = news[a].at[:, :, :, 0:128], outs[a].at[:, :, :, 0:128]
            else:
                for x in range(ROWS):
                    for k in range(3):
                        news[a][k, x, :, 0:128] = jnp.where(
                            first, others[a][k, x, :, 128:256], news[a][k, x, :, 0:128]
                        )
                source, target = news[a], outs[a].at[:, :, :, 128:384]
            copies.append(pltpu.make_async_copy(source, target, sems.at[a]))
            copies[-1].start()

    coarse_step(
        half, False, olds, news, c, ghost, (ce0, ch0), (ce, ch), inv, pl0, from_left, from_right, finished
    )
    for copy in copies:
        copy.wait()


FULL = pl.BlockSpec(memory_space=pltpu.VMEM)
RAW = pl.BlockSpec(memory_space=pltpu.HBM)
COST = pl.CostEstimate(flops=4_000_000, transcendentals=0, bytes_accessed=8_000_000)
FIELD = (3, ROWS, Z, W)
COEF = (6, ROWS, Z, W)
COARSE = (3, CROWS, Z, CW)
PLANES = (8, W)


def call(kernel, outs, args, specs=None, scratch=(), aliases=None, vmem=16, out_specs=None):
    outs = [dims if isinstance(dims, jax.ShapeDtypeStruct) else jax.ShapeDtypeStruct(dims, F32) for dims in outs]
    return pl.pallas_call(
        kernel,
        out_shape=outs,
        in_specs=specs or [FULL] * len(args),
        out_specs=out_specs or [FULL] * len(outs),
        scratch_shapes=list(scratch),
        input_output_aliases=aliases or {},
        compiler_params=pltpu.CompilerParams(vmem_limit_bytes=vmem * 1024 * 1024),
        cost_estimate=COST,
    )(*args)


def table(permittivity, plasma, damping, strength, resonance, linewidth):
    half_step = 0.5 * TIMESTEP
    c2 = plasma * plasma * TIMESTEP / (1.0 + damping * half_step)
    c4 = TIMESTEP * resonance * resonance / (1.0 + linewidth * half_step)
    rows = jnp.stack(
        [
            TIMESTEP / permittivity,
            (1.0 - damping * half_step) / (1.0 + damping * half_step),
            c2,
            (1.0 - linewidth * half_step) / (1.0 + linewidth * half_step),
            c4,
            strength,
            c2 + c4 * strength,
            COURANT / permittivity,
        ]
    )
    return jnp.pad(rows, ((0, 0), (0, 120)))


def message_shapes(half, first):
    return [(x_places(half, items)[1], Z, 128) for items in x_items(first)]


def exchanged(messages, axis):
    count = lax.axis_size(axis)
    swapped = []
    for message, first in zip(messages, (0, 1)):
        pairs = [((first + i) % count, (first + (i ^ 1)) % count) for i in range(count)]
        swapped.append(lax.ppermute(message, axis, pairs))
    return swapped


def local(
    fine_e,
    fine_h,
    drude_current,
    lorentz_pol,
    lorentz_rate,
    material,
    permittivity,
    plasma,
    damping,
    strength,
    resonance,
    linewidth,
    coarse_e,
    coarse_h,
    coarse_material,
    coarse_prior,
):
    fields = [
        jnp.transpose(value, (0, 2, 1, 3))
        for value in (fine_e, fine_h, drude_current, lorentz_pol, lorentz_rate)
    ]
    mat = jnp.transpose(material, (1, 0, 2))
    ce = coarse_e.reshape(3, Z * CROWS, 128)
    ch = coarse_h.reshape(3, Z * CROWS, 128)
    cmat = coarse_material.reshape(Z * CROWS, 128)
    prior = coarse_prior.reshape(2 * CROWS, 128)
    in_hbm = lambda values: [pltpu.with_memory_space_constraint(value, pltpu.HBM) for value in values]
    fields, coarse = in_hbm(fields), in_hbm([ce, ch, cmat, prior])
    (mat,) = in_hbm([mat])
    tab = table(permittivity, plasma, damping, strength, resonance, linewidth)

    vmem = lambda *dims: pltpu.VMEM(dims, F32)
    packed = call(
        pack_y_kernel,
        [(Y_PLANES, Z, 128)] * 2,
        [*fields, mat, *coarse],
        [RAW] * 10,
        [
            vmem(5, 3, ROWS, Z, 128),
            vmem(5, 3, ROWS, Z, 128),
            pltpu.VMEM((2, ROWS, Z, 128), jnp.int32),
            vmem(*ce.shape),
            vmem(*ch.shape),
            pltpu.VMEM(cmat.shape, jnp.int32),
            vmem(*prior.shape),
            pltpu.SemaphoreType.DMA((16,)),
        ],
        vmem=16,
    )
    received = exchanged(packed, "gy")
    loaded = call(
        load_kernel,
        [FIELD] * 10
        + [COEF] * 2
        + [(ROWS, Z, W)] * 2
        + [jax.ShapeDtypeStruct(value.shape, value.dtype) for value in coarse],
        [*fields, mat, *coarse, tab],
        [RAW] * 10 + [FULL],
        [pltpu.VMEM((ROWS, Z, OWN), jnp.int32), pltpu.SemaphoreType.DMA((15,))],
    )
    parts, waiting = [None, None], [None, None]
    for half in range(2):
        state = loaded[5 * half : 5 * half + 5]
        out = call(
            functools.partial(start_kernel, half),
            [FIELD] * 5 + [COEF, COARSE, COARSE, (CROWS, Z, CW), PLANES] + message_shapes(half, True),
            [*state, loaded[10 + half], loaded[12 + half], *loaded[14:18], tab, *received],
            scratch=[vmem(ROWS, Z, W), vmem(Y_PLANES, Z, 128)],
            aliases={index: index for index in range(6)},
        )
        parts[half] = (out[0:5], out[5:10], tab)
        waiting[half] = exchanged(out[10:12], "gx")
    for step in range(STEPS - 1):
        for half in range(2):
            state, (c, ce, ch, inv, planes), ghost = parts[half]
            out = call(
                functools.partial(step_kernel, half, step == 0),
                [FIELD] * 5
                + [COARSE, COARSE, PLANES]
                + message_shapes(half, False)
                + ([(2, 2, Z, W)] if step == 0 else []),
                [*state, c, ce, ch, inv, planes, ghost, *waiting[half]],
                scratch=[vmem(*message.shape) for message in waiting[half]],
            )
            if step == 0:
                ghost = out[10]
            parts[half] = (out[0:5], (c, out[5], out[6], inv, out[7]), ghost)
            waiting[half] = exchanged(out[8:10], "gx")
    whole = [(3, ROWS, Z, OWN)] * 5
    done = []
    for half in range(2):
        state, coarse, ghost = parts[half]
        args = [*state, *coarse, ghost, *waiting[half], *done]
        done = call(
            functools.partial(final_kernel, half),
            whole + ([(3, Z * CROWS, 128)] * 2 if half else [FIELD] * 5 + [COARSE] * 2),
            args,
            specs=[RAW if 13 <= i < 18 else FULL for i in range(len(args))],
            out_specs=[RAW] * 7 if half else [RAW] * 5 + [FULL] * 7,
            scratch=([vmem(*FIELD)] * 5 + [vmem(*COARSE)] * 2 + [vmem(3, Z * CROWS, 128)] * 2 if half else [])
            + [vmem(*message.shape) for message in waiting[half]]
            + [pltpu.SemaphoreType.DMA((7,))],
            aliases={13 + i: i for i in range(5)} if half else None,
        )
    fine = [jnp.transpose(value, (0, 2, 1, 3)) for value in done[0:5]]
    coarse = [value.reshape(3, Z, CROWS, 128) for value in done[5:7]]
    return (*fine, *coarse)


def solution(mesh):
    field = P(None, None, "gx", "gy")
    plane = P(None, "gx", "gy")
    in_specs = (field,) * 5 + (plane,) + (P(),) * 6 + (field, field, plane, plane)
    return jax.shard_map(local, mesh=mesh, in_specs=in_specs, out_specs=(field,) * 7, check_vma=False)
```

```python
import functools

import jax
import jax.numpy as jnp
from jax import lax
from jax.experimental import pallas as pl
from jax.experimental.pallas import tpu as pltpu
from jax.sharding import PartitionSpec as P

RATIO = 3
STEPS = 3
COURANT = 0.5
TIMESTEP = 0.5

Z = 16
ROWS = 6
OWN = 384
W = 256
CROWS = 2
CW = 128
GHOST = 9
CGHOST = 3
TILES = ((0, 1), (1, 2))
F32 = jnp.float32


def rolled(value, shift, axis):
    shift %= value.shape[axis]
    return value if shift == 0 else pltpu.roll(value, shift, axis)


def lanes(shape):
    return lax.broadcasted_iota(jnp.int32, shape, len(shape) - 1)


def right(value):
    return rolled(value, -1, 1)


def left(value):
    return rolled(value, 1, 1)


def above(value, top):
    sublane = lax.broadcasted_iota(jnp.int32, value.shape, 0)
    return jnp.where(sublane == Z - 1, top, rolled(value, -1, 0))


def below(value, bottom):
    sublane = lax.broadcasted_iota(jnp.int32, value.shape, 0)
    return jnp.where(sublane == 0, bottom, rolled(value, 1, 0))


def minus(first, second):
    if first is None:
        return None if second is None else -second
    return first if second is None else first - second


def h_row(h, e, following, top, wanted=(0, 1, 2)):
    ex, ey, ez = e
    next_y, next_z = following
    out = [None, None, None]
    if 0 in wanted:
        out[0] = h[0] - COURANT * ((right(ez) - ez) - (above(ey, top[1]) - ey))
    if 1 in wanted:
        out[1] = h[1] - COURANT * ((above(ex, top[0]) - ex) - minus(next_z, ez))
    if 2 in wanted:
        out[2] = h[2] - COURANT * (minus(next_y, ey) - (right(ex) - ex))
    return out


def curl_h(h, preceding, bottom, wanted=(0, 1, 2)):
    hx, hy, hz = h
    prev_y, prev_z = preceding
    out = [None, None, None]
    if 0 in wanted:
        out[0] = (hz - left(hz)) - (hy - below(hy, bottom[1]))
    if 1 in wanted:
        out[1] = (hx - below(hx, bottom[0])) - minus(hz, prev_z)
    if 2 in wanted:
        out[2] = minus(hy, prev_y) - (hx - left(hx))
    return out


def e_row(e, h, preceding, j, p, v, c, wanted=(0, 1, 2)):
    curl = curl_h(h, preceding, (0.0, 0.0), wanted)
    e2, j2, p2, v2 = [None] * 3, [None] * 3, [None] * 3, [None] * 3
    for k in wanted:
        v2[k] = c[3] * v[k] + c[4] * (c[5] * e[k] - p[k])
        j2[k] = c[1] * j[k] + c[2] * e[k]
        p2[k] = p[k] + TIMESTEP * v2[k]
        e2[k] = e[k] + c[0] * (curl[k] - j2[k] - v2[k])
    return e2, j2, p2, v2


def y_slots():
    fine = [("m", 0, 0, x) for x in range(ROWS)]
    fine += [("f", a, k, x) for a in range(5) for k in range(3) for x in range(ROWS)]
    coarse = [("c", a, k, r) for a in range(2) for k in range(3) for r in range(CROWS)]
    coarse += [("cm", 0, 0, r) for r in range(CROWS)] + [("prior", 0, 0, 0)]
    slots, plane, offset = {}, 0, 0
    for keys, width in ((fine, GHOST), (coarse, CGHOST)):
        for key in keys:
            if offset + 2 * width > 128:
                plane, offset = plane + 1, 0
            slots[key] = (plane, offset, width)
            offset += width
        offset += width
    return slots, plane + 1


Y_SLOTS, Y_PLANES = y_slots()


def coarse_row(ref, k, r):
    return ref[k, pl.ds(r, Z, stride=CROWS), :]


def pack_y_kernel(*refs):
    fields, (material, ce_in, ch_in, cmat_in, prior_in) = refs[0:5], refs[5:10]
    to_first, to_second, firsts, lasts, mats, ce, ch, cmat, prior, sems = refs[10:20]
    even = lax.rem(lax.axis_index("gy"), 2) == 0
    pairs = []
    for a in range(5):
        pairs.append((fields[a].at[:, :, :, 0:128], firsts.at[a]))
        pairs.append((fields[a].at[:, :, :, OWN - 128 : OWN], lasts.at[a]))
    pairs.append((material.at[:, :, 0:128], mats.at[0]))
    pairs.append((material.at[:, :, OWN - 128 : OWN], mats.at[1]))
    pairs += [(ce_in, ce), (ch_in, ch), (cmat_in, cmat), (prior_in, prior)]
    copies = [pltpu.make_async_copy(src, dst, sems.at[i]) for i, (src, dst) in enumerate(pairs)]
    for copy in copies:
        copy.start()
    for copy in copies:
        copy.wait()
    lane = lanes((Z, 128))
    built = {}
    for key, (plane, offset, width) in Y_SLOTS.items():
        kind, a, k, x = key
        if kind == "f":
            first, last = firsts[a, k, x], lasts[a, k, x]
        elif kind == "m":
            first, last = mats[0, x].astype(F32), mats[1, x].astype(F32)
        elif kind == "c":
            first = last = coarse_row((ce, ch)[a], k, x)
        elif kind == "cm":
            first = last = cmat[pl.ds(x, Z, stride=CROWS), :].astype(F32)
        else:
            first = last = jnp.concatenate([prior[...]] * (Z // 4), 0)
        both = rolled(first if first is last else jnp.where(lane < 64, first, last), offset + width, 1)
        pair = (both, both)
        if plane in built:
            starts = (offset + width, offset)
            pair = tuple(jnp.where(lane < start, old, both) for old, start in zip(built[plane], starts))
        built[plane] = pair
    for plane, (one, other) in built.items():
        to_first[plane] = jnp.where(even, other, one)
        to_second[plane] = jnp.where(even, one, other)


def with_ghosts(half, message, key, tile):
    plane, offset, width = Y_SLOTS[key]
    lane = lanes((Z, 128))
    if half == 0:
        return jnp.where(lane < 96, tile, rolled(message[plane], -offset - width, 1))
    return jnp.where(lane < 32, rolled(message[plane], -offset - width, 1), tile)


def load_kernel(*refs):
    own, material_in, coarse_in, tab = refs[0:5], refs[5], refs[6:10], refs[10]
    states = (refs[11:16], refs[16:21])
    c_halves, mat_halves, coarse = refs[21:23], refs[23:25], refs[25:29]
    material, sems = refs[29:31]
    first = pltpu.make_async_copy(material_in, material, sems.at[10])
    first.start()
    copies = []
    for half in range(2):
        for a in range(5):
            source = own[a].at[:, :, :, 128 * half : 128 * half + W]
            copies.append(pltpu.make_async_copy(source, states[half][a], sems.at[5 * half + a]))
            copies[-1].start()
    for i, (source, target) in enumerate(zip(coarse_in, coarse)):
        copies.append(pltpu.make_async_copy(source, target, sems.at[11 + i]))
        copies[-1].start()
    first.wait()
    for x in range(ROWS):
        for half in range(2):
            mat_halves[half][x] = material[x, :, 128 * half : 128 * half + W].astype(F32)
        for tile in range(3):
            index = material[x, :, 128 * tile : 128 * (tile + 1)]
            for k in range(6):
                value = lookup(tab, k, index)
                for half in range(2):
                    if tile in TILES[half]:
                        local_tile = TILES[half].index(tile)
                        c_halves[half][k, x, :, 128 * local_tile : 128 * (local_tile + 1)] = value
    for copy in copies:
        copy.wait()


E_ITEMS = [(("e", t, k), 9 - t, 8 - t, True) for t in range(RATIO) for k in (1, 2)]
H_ITEMS = [(("h", t, k), 8 - t, 8 - t, True) for t in range(RATIO) for k in (1, 2)]
COARSE_ITEMS = [(("c", 0, k), CGHOST, CGHOST, False) for k in (1, 2)]
MATERIAL_ITEM = [(("m", 0, 0), 8, 8, True)]


def x_places(half, items):
    places, half_slots, plane, offset = {}, [], 1, 0
    for name, lefts, rights, fine in items:
        mixed = (1 - half) if fine else 0
        segments = []
        if fine:
            segments.append((half, 0, plane, 0, 128))
            plane += 1
        if not half_slots:
            half_slots = [(plane, 0), (plane, 64)]
            plane += 1
        own_lane = 64 * half
        segments.append((mixed, own_lane, *half_slots.pop(0), 64))
        left_lane = 64 - lefts if half else 128 - lefts
        right_lane = 0 if half else 64
        for lane, length in ((left_lane, lefts), (right_lane, rights)):
            segments.append((mixed, lane, 0, offset, length))
            offset += length
        places[name] = segments
    assert offset <= 128
    return places, plane


def write_x(half, items, values):
    places, planes = x_places(half, items)
    lane = lanes((Z, 128))
    built_planes = []
    for plane in range(planes):
        parts = sorted(
            (there, name, tile, start)
            for name, segments in places.items()
            for tile, start, where, there, _ in segments
            if where == plane
        )
        built = None
        for there, name, tile, start in parts:
            value = rolled(values[name][:, 128 * tile : 128 * (tile + 1)], there - start, 1)
            built = value if built is None else jnp.where(lane < there, built, value)
        built_planes.append(built)
    return built_planes


def read_x(ref, half, items, name):
    lane = lanes((Z, 128))
    built = {}
    for tile, start, plane, there, _ in sorted(x_places(half, items)[0][name]):
        value = rolled(ref[plane], start - there, 1)
        built[tile] = value if tile not in built else jnp.where(lane < start, built[tile], value)
    return jnp.concatenate([built[tile] for tile in sorted(built)], 1)


def x_items(first):
    extra = MATERIAL_ITEM if first else []
    return E_ITEMS + COARSE_ITEMS + extra, H_ITEMS + COARSE_ITEMS + extra


def gather(value, index):
    return jnp.take_along_axis(value, index, axis=1, mode="promise_in_bounds")


def prolong_lanes(half, value):
    lane = lanes((8, 128))
    third = lambda number: (number * 21846) >> 16
    if half == 0:
        indices = [third(lane), jnp.where(lane < 96, third(lane + 128), 128 - third(130 - lane))]
    else:
        indices = [jnp.where(lane < 32, third(lane), third(lane + 128)), third(lane + 256)]
    return jnp.concatenate([gather(value, index) for index in indices], 1)


def restrict_lanes(half, value):
    three = value + rolled(value, -1, 1) + rolled(value, -2, 1)
    lane = lanes((8, 128))
    index = (lane * RATIO) & 127
    tiles = [gather(three[:, 128 * tile : 128 * (tile + 1)], index) for tile in range(2)]
    in_first = lane * RATIO < (128 if half == 0 else 256)
    return jnp.where(in_first, tiles[0], tiles[1]) * (1.0 / RATIO**3)


def sort_messages(received, sorted_refs):
    even = lax.rem(lax.axis_index("gx"), 2) == 0
    first, second = received
    from_left, from_right = sorted_refs
    for plane in range(first.shape[0]):
        from_left[plane] = jnp.where(even, second[plane], first[plane])
        from_right[plane] = jnp.where(even, first[plane], second[plane])
    return from_left, from_right


def interface_rows(ce):
    return jnp.concatenate([ce[k, r][0:1] for k in range(2) for r in range(CROWS)], 0)


def top_plane(pl_ref, x, t):
    r = x // RATIO
    out = []
    for k in range(2):
        row = 2 * k + r
        value = pl_ref[row : row + 1, :]
        if t:
            value = value + float(t) * pl_ref[4 + row : 5 + row, :]
        out.append(value)
    return out


def lookup(tab, row, index):
    entry = jnp.broadcast_to(tab[row : row + 1, :], (8, 128))
    rows = []
    for z in range(0, Z, 8):
        rows.append(
            jnp.concatenate(
                [
                    gather(entry, index[z : z + 8, lane : lane + 128])
                    for lane in range(0, index.shape[1], 128)
                ],
                1,
            )
        )
    return jnp.concatenate(rows, 0)


def row_of(ref, x):
    return [ref[k, x] for k in range(3)]


def send_edges(half, first, fields, c, ce, ch, pl_ref, mat, to_first, to_second):
    fe, fh, fj, fp, fv = fields
    none = (None, None)
    e_items, h_items = x_items(first)
    coef = lambda x: [c[k, x] for k in range(6)]
    states = lambda x: (row_of(fj, x), row_of(fp, x), row_of(fv, x))
    e0 = {x: row_of(fe, x) for x in range(ROWS)}
    low, high = {}, {}

    for k in (1, 2):
        low["e", 0, k] = e0[0][k]
    h1 = {x: h_row(row_of(fh, x), e0[x], e0[x + 1][1:], top_plane(pl_ref, x, 0)) for x in (0, 1)}
    e1, s1 = {}, {}
    e1[0], *s1[0] = e_row(e0[0], h1[0], none, *states(0), coef(0))
    e1[1], *s1[1] = e_row(e0[1], h1[1], h1[0][1:], *states(1), coef(1), (1, 2))
    h2 = h_row(h1[0], e1[0], e1[1][1:], top_plane(pl_ref, 0, 1))
    e2 = e_row(e1[0], h2, none, *s1[0], coef(0), (1, 2))[0]
    for k in (1, 2):
        low["e", 1, k] = e1[0][k]
        low["e", 2, k] = e2[k]
        low["c", 0, k] = ce[k, 0]

    a, b, d = ROWS - 3, ROWS - 2, ROWS - 1
    h1 = {
        a: h_row(row_of(fh, a), e0[a], e0[b][1:], top_plane(pl_ref, a, 0), (1, 2)),
        b: h_row(row_of(fh, b), e0[b], e0[d][1:], top_plane(pl_ref, b, 0)),
        d: h_row(row_of(fh, d), e0[d], none, top_plane(pl_ref, d, 0)),
    }
    e1, s1 = {}, {}
    e1[b], *s1[b] = e_row(e0[b], h1[b], h1[a][1:], *states(b), coef(b))
    e1[d], *s1[d] = e_row(e0[d], h1[d], h1[b][1:], *states(d), coef(d))
    h2 = {
        b: h_row(h1[b], e1[b], e1[d][1:], top_plane(pl_ref, b, 1), (1, 2)),
        d: h_row(h1[d], e1[d], none, top_plane(pl_ref, d, 1)),
    }
    e2 = e_row(e1[d], h2[d], h2[b][1:], *s1[d], coef(d))[0]
    h3 = h_row(h2[d], e2, none, top_plane(pl_ref, d, 2), (1, 2))
    ch_last = h_row(row_of(ch, CROWS - 1), row_of(ce, CROWS - 1), none, (0.0, 0.0), (1, 2))
    for k in (1, 2):
        high["h", 0, k] = h1[d][k]
        high["h", 1, k] = h2[d][k]
        high["h", 2, k] = h3[k]
        high["c", 0, k] = ch_last[k]
    if first:
        low["m", 0, 0] = mat[0]
        high["m", 0, 0] = mat[ROWS - 1]
    even = lax.rem(lax.axis_index("gx"), 2) == 0
    for first_part, second_part, plane in zip(write_x(half, h_items, high), write_x(half, e_items, low), range(99)):
        to_first[plane] = jnp.where(even, first_part, second_part)
        to_second[plane] = jnp.where(even, second_part, first_part)


def start_kernel(half, *refs):
    fields_in, (c_in, mat_in, ce_in, ch_in, cmat, prior, tab) = refs[0:5], refs[5:12]
    received, fields = refs[12:14], refs[14:19]
    c, ce, ch, inv, pl_ref, to_first, to_second, mat, message = refs[19:28]
    even = lax.rem(lax.axis_index("gy"), 2) == 0
    swap = even if half == 0 else jnp.logical_not(even)
    for plane in range(Y_PLANES):
        message[plane] = jnp.where(swap, received[1][plane], received[0][plane])
    outer = slice(128, 256) if half == 0 else slice(0, 128)
    inner = slice(0, 128) if half == 0 else slice(128, 256)
    for x in (0, ROWS - 1):
        mat[x, :, outer] = with_ghosts(half, message, ("m", 0, 0, x), mat_in[x, :, outer])
        mat[x, :, inner] = mat_in[x, :, inner]
    (packed_plane,) = {Y_SLOTS["m", 0, 0, x][0] for x in range(ROWS)}
    index = jnp.clip(message[packed_plane].astype(jnp.int32), 0, 127)
    for k in range(6):
        packed = {packed_plane: lookup(tab, k, index)}
        for x in range(ROWS):
            c[k, x, :, outer] = with_ghosts(half, packed, ("m", 0, 0, x), c_in[k, x, :, outer])
    for a in range(5):
        for k in range(3):
            for x in range(ROWS):
                fields[a][k, x, :, outer] = with_ghosts(
                    half, message, ("f", a, k, x), fields_in[a][k, x, :, outer]
                )
    for a, (source, target) in enumerate(((ce_in, ce), (ch_in, ch))):
        for k in range(3):
            for r in range(CROWS):
                target[k, r] = with_ghosts(half, message, ("c", a, k, r), coarse_row(source, k, r))
    for r in range(CROWS):
        value = cmat[pl.ds(r, Z, stride=CROWS), :].astype(F32)
        index = with_ghosts(half, message, ("cm", 0, 0, r), value).astype(jnp.int32)
        inv[r] = lookup(tab, 7, jnp.clip(index, 0, 127))
    before = jnp.concatenate([prior[...]] * (Z // 4), 0)
    before = with_ghosts(half, message, ("prior", 0, 0, 0), before)[0:4]
    interface = interface_rows(ce)
    increment = (interface - before) * (1.0 / RATIO)
    pl_ref[...] = prolong_lanes(half, jnp.concatenate([interface, increment], 0))
    send_edges(half, True, fields, c, ce, ch, pl_ref, mat, to_first, to_second)


def coarse_step(half, first, olds, news, c, ghost, olds_c, news_c, inv, pl_ref, from_left, from_right, finished=None):
    e_items, h_items = x_items(first)
    zero = jnp.zeros((Z, W), F32)
    flat = (0.0, 0.0)
    (ce0, ch0), (ce, ch) = olds_c, news_c
    coarse_e0 = [row_of(ce0, r) for r in range(CROWS)]
    up = [read_x(from_right, half, e_items, ("c", 0, k)) for k in (1, 2)]
    down = [read_x(from_left, half, h_items, ("c", 0, k)) for k in (1, 2)]
    down = [down[0] + COURANT * coarse_e0[0][2], down[1] - COURANT * coarse_e0[0][1]]
    coarse_h = []
    for r in range(CROWS):
        following = coarse_e0[r + 1][1:] if r + 1 < CROWS else up
        coarse_h.append(h_row(row_of(ch0, r), coarse_e0[r], following, flat))
        for k in range(3):
            ch[k, r] = coarse_h[r][k]
    if finished:
        finished((6,))

    ge = gh = he = hh = None
    summed = [[None] * CROWS for _ in range(2)]
    for t in range(RATIO):
        fe, fh, fj, fp, fv = olds if t == 0 else news
        e_first = row_of(fe, 0)
        following = [read_x(from_right, half, e_items, ("e", t, k)) for k in (1, 2)]
        if t:
            following = [base + more for base, more in zip(following, he[1:])]
        far = [None, None]
        if t == 0:
            gh = [None, COURANT * e_first[2], -COURANT * e_first[1]]
        else:
            far = [COURANT * ge[2], -COURANT * ge[1]]
            old = [zero if value is None else value for value in gh]
            gh = h_row(old, ge, e_first[1:], flat, (0, 1, 2) if t < RATIO - 1 else (1, 2))
        preceding = [read_x(from_left, half, h_items, ("h", t, k)) + gh[k] for k in (1, 2)]
        current = e_first
        last = finished is not None and t == RATIO - 1
        if last:
            for x in range(ROWS):
                for k in range(3):
                    v2 = c[3, x] * fv[k, x] + c[4, x] * (c[5, x] * fe[k, x] - fp[k, x])
                    news[2][k, x] = c[1, x] * fj[k, x] + c[2, x] * fe[k, x]
                    news[3][k, x] = fp[k, x] + TIMESTEP * v2
                    news[4][k, x] = v2
            finished((2, 3, 4))
        for x in range(ROWS):
            upper = row_of(fe, x + 1) if x + 1 < ROWS else None
            h = h_row(
                row_of(fh, x), row_of(fe, x), upper[1:] if upper else following, top_plane(pl_ref, x, t)
            )
            for k in range(3):
                news[1][k, x] = h[k]
            for k in range(2):
                part = h[k][8:Z]
                have = summed[k][x // RATIO]
                summed[k][x // RATIO] = part if have is None else have + part
        if last:
            finished((1,))
        for x in range(ROWS):
            h = row_of(news[1], x)
            if last:
                curl = curl_h(h, preceding, flat)
                for k in range(3):
                    news[0][k, x] = fe[k, x] + c[0, x] * (curl[k] - fj[k, x] - fv[k, x])
                preceding = h[1:]
                continue
            e2, j2, p2, v2 = e_row(
                row_of(fe, x), h, preceding, row_of(fj, x), row_of(fp, x), row_of(fv, x), [c[k, x] for k in range(6)]
            )
            for k in range(3):
                news[0][k, x] = e2[k]
                news[2][k, x] = j2[k]
                news[3][k, x] = p2[k]
                news[4][k, x] = v2[k]
            preceding = h[1:]
        if last:
            finished((0,))
        if t == 0:
            (a, b), (a2, b2) = [[ghost[k, side] for k in range(2)] for side in range(2)]
            ge = [
                a * ((gh[2] - left(gh[2])) - (gh[1] - below(gh[1], 0.0))),
                -a * gh[2],
                a * gh[1],
            ]
            he = [zero, a2 * preceding[1], -a2 * preceding[0]]
        elif t == 1:
            curl = curl_h(gh, far, flat)
            ge = [ge[k] + a * (curl[k] - b * ge[k]) for k in range(3)]
            hh = h_row([zero] * 3, he, (None, None), flat)
            curl = curl_h(hh, preceding, flat, (1, 2))
            he = [None] + [he[k] + a2 * (curl[k] - b2 * he[k]) for k in (1, 2)]

    rows = [summed[k][r][7:8] for k in range(2) for r in range(CROWS)]
    bottoms = restrict_lanes(half, jnp.concatenate(rows + rows, 0))
    preceding = down
    for r in range(CROWS):
        bottom = [bottoms[2 * k + r : 2 * k + r + 1, :] for k in range(2)]
        curl = curl_h(coarse_h[r], preceding, bottom)
        for k in range(3):
            ce[k, r] = coarse_e0[r][k] + inv[r] * curl[k]
        preceding = coarse_h[r][1:]
    if finished:
        finished((5,))


def ghost_coefficients(half, ghost, tab, from_left, from_right):
    e_items, h_items = x_items(True)
    for side, (ref, items) in enumerate(((from_left, h_items), (from_right, e_items))):
        index = jnp.clip(read_x(ref, half, items, ("m", 0, 0)).astype(jnp.int32), 0, 127)
        ghost[0, side] = lookup(tab, 0, index)
        ghost[1, side] = lookup(tab, 6, index)


def step_kernel(half, first, *refs):
    olds, rest = refs[0:5], refs[5:]
    c, ce0, ch0, inv, pl0, ghost_in = rest[0:6]
    from_left, from_right = sort_messages(rest[6:8], rest[-2:])
    news, rest = rest[8:13], rest[13:-2]
    if first:
        ce, ch, pl_ref, to_first, to_second, ghost = rest
        ghost_coefficients(half, ghost, ghost_in, from_left, from_right)
    else:
        ce, ch, pl_ref, to_first, to_second = rest
        ghost = ghost_in
    coarse_step(half, first, olds, news, c, ghost, (ce0, ch0), (ce, ch), inv, pl0, from_left, from_right)
    interface = interface_rows(ce)
    increment = (interface - interface_rows(ce0)) * (1.0 / RATIO)
    pl_ref[...] = prolong_lanes(half, jnp.concatenate([interface, increment], 0))
    send_edges(half, False, news, c, ce, ch, pl_ref, None, to_first, to_second)


def final_kernel(half, *refs):
    olds, rest = refs[0:5], refs[5:]
    c, ce0, ch0, inv, pl0, ghost = rest[0:6]
    received, rest = rest[6:8], rest[8:]
    if half == 0:
        outs, news, ce, ch = rest[0:5], rest[5:10], rest[10], rest[11]
        rest = rest[12:]
    else:
        others, others_c = rest[5:10], rest[10:12]
        outs, outs_c, news, ce, ch = rest[12:17], rest[17:19], rest[19:24], rest[24], rest[25]
        coarse_parts = rest[26:28]
        rest = rest[28:]
    sorted_refs, sems = rest[0:2], rest[2]
    from_left, from_right = sort_messages(received, sorted_refs)
    first = lanes((Z, 128)) < 64
    copies = []

    def coarse_finished(a):
        if half == 0:
            return
        for k in range(3):
            for r in range(CROWS):
                value = jnp.where(first, others_c[a][k, r], (ce, ch)[a][k, r])
                coarse_parts[a][k, pl.ds(r, Z, stride=CROWS), :] = value
        copies.append(pltpu.make_async_copy(coarse_parts[a], outs_c[a], sems.at[5 + a]))
        copies[-1].start()

    def finished(arrays):
        for a in arrays:
            if a >= 5:
                coarse_finished(a - 5)
                continue
            if half == 0:
                source, target = news[a].at[:, :, :, 0:128], outs[a].at[:, :, :, 0:128]
            else:
                for x in range(ROWS):
                    for k in range(3):
                        news[a][k, x, :, 0:128] = jnp.where(
                            first, others[a][k, x, :, 128:256], news[a][k, x, :, 0:128]
                        )
                source, target = news[a], outs[a].at[:, :, :, 128:384]
            copies.append(pltpu.make_async_copy(source, target, sems.at[a]))
            copies[-1].start()

    coarse_step(
        half, False, olds, news, c, ghost, (ce0, ch0), (ce, ch), inv, pl0, from_left, from_right, finished
    )
    for copy in copies:
        copy.wait()


FULL = pl.BlockSpec(memory_space=pltpu.VMEM)
RAW = pl.BlockSpec(memory_space=pltpu.HBM)
COST = pl.CostEstimate(flops=4_000_000, transcendentals=0, bytes_accessed=8_000_000)
FIELD = (3, ROWS, Z, W)
COEF = (6, ROWS, Z, W)
COARSE = (3, CROWS, Z, CW)
PLANES = (8, W)


def call(kernel, outs, args, specs=None, scratch=(), aliases=None, vmem=16, out_specs=None):
    outs = [dims if isinstance(dims, jax.ShapeDtypeStruct) else jax.ShapeDtypeStruct(dims, F32) for dims in outs]
    return pl.pallas_call(
        kernel,
        out_shape=outs,
        in_specs=specs or [FULL] * len(args),
        out_specs=out_specs or [FULL] * len(outs),
        scratch_shapes=list(scratch),
        input_output_aliases=aliases or {},
        compiler_params=pltpu.CompilerParams(vmem_limit_bytes=vmem * 1024 * 1024),
        cost_estimate=COST,
    )(*args)


def table(permittivity, plasma, damping, strength, resonance, linewidth):
    half_step = 0.5 * TIMESTEP
    c2 = plasma * plasma * TIMESTEP / (1.0 + damping * half_step)
    c4 = TIMESTEP * resonance * resonance / (1.0 + linewidth * half_step)
    rows = jnp.stack(
        [
            TIMESTEP / permittivity,
            (1.0 - damping * half_step) / (1.0 + damping * half_step),
            c2,
            (1.0 - linewidth * half_step) / (1.0 + linewidth * half_step),
            c4,
            strength,
            c2 + c4 * strength,
            COURANT / permittivity,
        ]
    )
    return jnp.pad(rows, ((0, 0), (0, 120)))


def message_shapes(half, first):
    return [(x_places(half, items)[1], Z, 128) for items in x_items(first)]


def exchanged(messages, axis):
    count = lax.axis_size(axis)
    swapped = []
    for message, first in zip(messages, (0, 1)):
        pairs = [((first + i) % count, (first + (i ^ 1)) % count) for i in range(count)]
        swapped.append(lax.ppermute(message, axis, pairs))
    return swapped


def local(
    fine_e,
    fine_h,
    drude_current,
    lorentz_pol,
    lorentz_rate,
    material,
    permittivity,
    plasma,
    damping,
    strength,
    resonance,
    linewidth,
    coarse_e,
    coarse_h,
    coarse_material,
    coarse_prior,
):
    fields = [
        jnp.transpose(value, (0, 2, 1, 3))
        for value in (fine_e, fine_h, drude_current, lorentz_pol, lorentz_rate)
    ]
    mat = jnp.transpose(material, (1, 0, 2))
    ce = coarse_e.reshape(3, Z * CROWS, 128)
    ch = coarse_h.reshape(3, Z * CROWS, 128)
    cmat = coarse_material.reshape(Z * CROWS, 128)
    prior = coarse_prior.reshape(2 * CROWS, 128)
    in_hbm = lambda values: [pltpu.with_memory_space_constraint(value, pltpu.HBM) for value in values]
    fields, coarse = in_hbm(fields), in_hbm([ce, ch, cmat, prior])
    (mat,) = in_hbm([mat])
    tab = table(permittivity, plasma, damping, strength, resonance, linewidth)

    vmem = lambda *dims: pltpu.VMEM(dims, F32)
    packed = call(
        pack_y_kernel,
        [(Y_PLANES, Z, 128)] * 2,
        [*fields, mat, *coarse],
        [RAW] * 10,
        [
            vmem(5, 3, ROWS, Z, 128),
            vmem(5, 3, ROWS, Z, 128),
            pltpu.VMEM((2, ROWS, Z, 128), jnp.int32),
            vmem(*ce.shape),
            vmem(*ch.shape),
            pltpu.VMEM(cmat.shape, jnp.int32),
            vmem(*prior.shape),
            pltpu.SemaphoreType.DMA((16,)),
        ],
        vmem=16,
    )
    received = exchanged(packed, "gy")
    loaded = call(
        load_kernel,
        [FIELD] * 10
        + [COEF] * 2
        + [(ROWS, Z, W)] * 2
        + [jax.ShapeDtypeStruct(value.shape, value.dtype) for value in coarse],
        [*fields, mat, *coarse, tab],
        [RAW] * 10 + [FULL],
        [pltpu.VMEM((ROWS, Z, OWN), jnp.int32), pltpu.SemaphoreType.DMA((15,))],
    )
    parts, waiting = [None, None], [None, None]
    for half in range(2):
        state = loaded[5 * half : 5 * half + 5]
        out = call(
            functools.partial(start_kernel, half),
            [FIELD] * 5 + [COEF, COARSE, COARSE, (CROWS, Z, CW), PLANES] + message_shapes(half, True),
            [*state, loaded[10 + half], loaded[12 + half], *loaded[14:18], tab, *received],
            scratch=[vmem(ROWS, Z, W), vmem(Y_PLANES, Z, 128)],
            aliases={index: index for index in range(6)},
        )
        parts[half] = (out[0:5], out[5:10], tab)
        waiting[half] = exchanged(out[10:12], "gx")
    for step in range(STEPS - 1):
        for half in range(2):
            state, (c, ce, ch, inv, planes), ghost = parts[half]
            out = call(
                functools.partial(step_kernel, half, step == 0),
                [FIELD] * 5
                + [COARSE, COARSE, PLANES]
                + message_shapes(half, False)
                + ([(2, 2, Z, W)] if step == 0 else []),
                [*state, c, ce, ch, inv, planes, ghost, *waiting[half]],
                scratch=[vmem(*message.shape) for message in waiting[half]],
            )
            if step == 0:
                ghost = out[10]
            parts[half] = (out[0:5], (c, out[5], out[6], inv, out[7]), ghost)
            waiting[half] = exchanged(out[8:10], "gx")
    whole = [(3, ROWS, Z, OWN)] * 5
    done = []
    for half in range(2):
        state, coarse, ghost = parts[half]
        args = [*state, *coarse, ghost, *waiting[half], *done]
        done = call(
            functools.partial(final_kernel, half),
            whole + ([(3, Z * CROWS, 128)] * 2 if half else [FIELD] * 5 + [COARSE] * 2),
            args,
            specs=[RAW if 13 <= i < 18 else FULL for i in range(len(args))],
            out_specs=[RAW] * 7 if half else [RAW] * 5 + [FULL] * 7,
            scratch=([vmem(*FIELD)] * 5 + [vmem(*COARSE)] * 2 + [vmem(3, Z * CROWS, 128)] * 2 if half else [])
            + [vmem(*message.shape) for message in waiting[half]]
            + [pltpu.SemaphoreType.DMA((7,))],
            aliases={13 + i: i for i in range(5)} if half else None,
        )
    fine = [jnp.transpose(value, (0, 2, 1, 3)) for value in done[0:5]]
    coarse = [value.reshape(3, Z, CROWS, 128) for value in done[5:7]]
    return (*fine, *coarse)


def solution(mesh):
    field = P(None, None, "gx", "gy")
    plane = P(None, "gx", "gy")
    in_specs = (field,) * 5 + (plane,) + (P(),) * 6 + (field, field, plane, plane)
    return jax.shard_map(local, mesh=mesh, in_specs=in_specs, out_specs=(field,) * 7, check_vma=False)
```

```python
import functools

import jax
import jax.numpy as jnp
from jax import lax
from jax.experimental import pallas as pl
from jax.experimental.pallas import tpu as pltpu
from jax.sharding import PartitionSpec as P

RATIO = 3
STEPS = 3
COURANT = 0.5
TIMESTEP = 0.5

Z = 16
ROWS = 6
OWN = 384
W = 256
CROWS = 2
CW = 128
GHOST = 9
CGHOST = 3
TILES = ((0, 1), (1, 2))
F32 = jnp.float32


def rolled(value, shift, axis):
    shift %= value.shape[axis]
    return value if shift == 0 else pltpu.roll(value, shift, axis)


def lanes(shape):
    return lax.broadcasted_iota(jnp.int32, shape, len(shape) - 1)


def right(value):
    return rolled(value, -1, 1)


def left(value):
    return rolled(value, 1, 1)


def above(value, top):
    sublane = lax.broadcasted_iota(jnp.int32, value.shape, 0)
    return jnp.where(sublane == Z - 1, top, rolled(value, -1, 0))


def below(value, bottom):
    sublane = lax.broadcasted_iota(jnp.int32, value.shape, 0)
    return jnp.where(sublane == 0, bottom, rolled(value, 1, 0))


def minus(first, second):
    if first is None:
        return None if second is None else -second
    return first if second is None else first - second


def h_row(h, e, following, top, wanted=(0, 1, 2)):
    ex, ey, ez = e
    next_y, next_z = following
    out = [None, None, None]
    if 0 in wanted:
        out[0] = h[0] - COURANT * ((right(ez) - ez) - (above(ey, top[1]) - ey))
    if 1 in wanted:
        out[1] = h[1] - COURANT * ((above(ex, top[0]) - ex) - minus(next_z, ez))
    if 2 in wanted:
        out[2] = h[2] - COURANT * (minus(next_y, ey) - (right(ex) - ex))
    return out


def curl_h(h, preceding, bottom, wanted=(0, 1, 2)):
    hx, hy, hz = h
    prev_y, prev_z = preceding
    out = [None, None, None]
    if 0 in wanted:
        out[0] = (hz - left(hz)) - (hy - below(hy, bottom[1]))
    if 1 in wanted:
        out[1] = (hx - below(hx, bottom[0])) - minus(hz, prev_z)
    if 2 in wanted:
        out[2] = minus(hy, prev_y) - (hx - left(hx))
    return out


def e_row(e, h, preceding, j, p, v, c, wanted=(0, 1, 2)):
    curl = curl_h(h, preceding, (0.0, 0.0), wanted)
    e2, j2, p2, v2 = [None] * 3, [None] * 3, [None] * 3, [None] * 3
    for k in wanted:
        v2[k] = c[3] * v[k] + c[4] * (c[5] * e[k] - p[k])
        j2[k] = c[1] * j[k] + c[2] * e[k]
        p2[k] = p[k] + TIMESTEP * v2[k]
        e2[k] = e[k] + c[0] * (curl[k] - j2[k] - v2[k])
    return e2, j2, p2, v2


def y_slots():
    fine = [("m", 0, 0, x) for x in range(ROWS)]
    fine += [("f", a, k, x) for a in range(5) for k in range(3) for x in range(ROWS)]
    coarse = [("c", a, k, r) for a in range(2) for k in range(3) for r in range(CROWS)]
    coarse += [("cm", 0, 0, r) for r in range(CROWS)] + [("prior", 0, 0, 0)]
    slots, plane, offset = {}, 0, 0
    for keys, width in ((fine, GHOST), (coarse, CGHOST)):
        for key in keys:
            if offset + 2 * width > 128:
                plane, offset = plane + 1, 0
            slots[key] = (plane, offset, width)
            offset += width
        offset += width
    return slots, plane + 1


Y_SLOTS, Y_PLANES = y_slots()


def coarse_row(ref, k, r):
    return ref[k, pl.ds(r, Z, stride=CROWS), :]


def pack_y_kernel(*refs):
    fields, (material, ce_in, ch_in, cmat_in, prior_in) = refs[0:5], refs[5:10]
    to_first, to_second, firsts, lasts, mats, ce, ch, cmat, prior, sems = refs[10:20]
    even = lax.rem(lax.axis_index("gy"), 2) == 0
    pairs = []
    for a in range(5):
        pairs.append((fields[a].at[:, :, :, 0:128], firsts.at[a]))
        pairs.append((fields[a].at[:, :, :, OWN - 128 : OWN], lasts.at[a]))
    pairs.append((material.at[:, :, 0:128], mats.at[0]))
    pairs.append((material.at[:, :, OWN - 128 : OWN], mats.at[1]))
    pairs += [(ce_in, ce), (ch_in, ch), (cmat_in, cmat), (prior_in, prior)]
    copies = [pltpu.make_async_copy(src, dst, sems.at[i]) for i, (src, dst) in enumerate(pairs)]
    early = copies[10:12] + copies[0:4]
    late = copies[4:10] + copies[12:]
    for copy in early + late:
        copy.start()
    for copy in early:
        copy.wait()
    lane = lanes((Z, 128))
    built = {}
    for key, (plane, offset, width) in Y_SLOTS.items():
        kind, a, k, x = key
        if key == ("f", 2, 0, 0):
            for copy in late:
                copy.wait()
        if kind == "f":
            first, last = firsts[a, k, x], lasts[a, k, x]
        elif kind == "m":
            first, last = mats[0, x].astype(F32), mats[1, x].astype(F32)
        elif kind == "c":
            first = last = coarse_row((ce, ch)[a], k, x)
        elif kind == "cm":
            first = last = cmat[pl.ds(x, Z, stride=CROWS), :].astype(F32)
        else:
            first = last = jnp.concatenate([prior[...]] * (Z // 4), 0)
        both = rolled(first if first is last else jnp.where(lane < 64, first, last), offset + width, 1)
        pair = (both, both)
        if plane in built:
            starts = (offset + width, offset)
            pair = tuple(jnp.where(lane < start, old, both) for old, start in zip(built[plane], starts))
        built[plane] = pair
    for plane, (one, other) in built.items():
        to_first[plane] = jnp.where(even, other, one)
        to_second[plane] = jnp.where(even, one, other)


def with_ghosts(half, message, key, tile):
    plane, offset, width = Y_SLOTS[key]
    lane = lanes((Z, 128))
    if half == 0:
        return jnp.where(lane < 96, tile, rolled(message[plane], -offset - width, 1))
    return jnp.where(lane < 32, rolled(message[plane], -offset - width, 1), tile)


def load_kernel(*refs):
    own, material_in, coarse_in, tab = refs[0:5], refs[5], refs[6:10], refs[10]
    states = (refs[11:16], refs[16:21])
    c_halves, mat_halves, coarse = refs[21:23], refs[23:25], refs[25:29]
    material, sems = refs[29:31]
    first = pltpu.make_async_copy(material_in, material, sems.at[10])
    first.start()
    copies = []
    for half in range(2):
        for a in range(5):
            source = own[a].at[:, :, :, 128 * half : 128 * half + W]
            copies.append(pltpu.make_async_copy(source, states[half][a], sems.at[5 * half + a]))
            copies[-1].start()
    for i, (source, target) in enumerate(zip(coarse_in, coarse)):
        copies.append(pltpu.make_async_copy(source, target, sems.at[11 + i]))
        copies[-1].start()
    first.wait()
    for x in range(ROWS):
        for half in range(2):
            mat_halves[half][x] = material[x, :, 128 * half : 128 * half + W].astype(F32)
        for tile in range(3):
            index = material[x, :, 128 * tile : 128 * (tile + 1)]
            for k in range(6):
                value = lookup(tab, k, index)
                for half in range(2):
                    if tile in TILES[half]:
                        local_tile = TILES[half].index(tile)
                        c_halves[half][k, x, :, 128 * local_tile : 128 * (local_tile + 1)] = value
    for copy in copies:
        copy.wait()


E_ITEMS = [(("e", t, k), 9 - t, 8 - t, True) for t in range(RATIO) for k in (1, 2)]
H_ITEMS = [(("h", t, k), 8 - t, 8 - t, True) for t in range(RATIO) for k in (1, 2)]
COARSE_ITEMS = [(("c", 0, k), CGHOST, CGHOST, False) for k in (1, 2)]
MATERIAL_ITEM = [(("m", 0, 0), 8, 8, True)]


def x_places(half, items):
    places, half_slots, plane, offset = {}, [], 1, 0
    for name, lefts, rights, fine in items:
        mixed = (1 - half) if fine else 0
        segments = []
        if fine:
            segments.append((half, 0, plane, 0, 128))
            plane += 1
        if not half_slots:
            half_slots = [(plane, 0), (plane, 64)]
            plane += 1
        own_lane = 64 * half
        segments.append((mixed, own_lane, *half_slots.pop(0), 64))
        left_lane = 64 - lefts if half else 128 - lefts
        right_lane = 0 if half else 64
        for lane, length in ((left_lane, lefts), (right_lane, rights)):
            segments.append((mixed, lane, 0, offset, length))
            offset += length
        places[name] = segments
    assert offset <= 128
    return places, plane


def write_x(half, items, values):
    places, planes = x_places(half, items)
    lane = lanes((Z, 128))
    built_planes = []
    for plane in range(planes):
        parts = sorted(
            (there, name, tile, start)
            for name, segments in places.items()
            for tile, start, where, there, _ in segments
            if where == plane
        )
        built = None
        for there, name, tile, start in parts:
            value = rolled(values[name][:, 128 * tile : 128 * (tile + 1)], there - start, 1)
            built = value if built is None else jnp.where(lane < there, built, value)
        built_planes.append(built)
    return built_planes


def read_x(ref, half, items, name):
    lane = lanes((Z, 128))
    built = {}
    for tile, start, plane, there, _ in sorted(x_places(half, items)[0][name]):
        value = rolled(ref[plane], start - there, 1)
        built[tile] = value if tile not in built else jnp.where(lane < start, built[tile], value)
    return jnp.concatenate([built[tile] for tile in sorted(built)], 1)


def x_items(first):
    extra = MATERIAL_ITEM if first else []
    return E_ITEMS + COARSE_ITEMS + extra, H_ITEMS + COARSE_ITEMS + extra


def gather(value, index):
    return jnp.take_along_axis(value, index, axis=1, mode="promise_in_bounds")


def prolong_lanes(half, value):
    lane = lanes((8, 128))
    third = lambda number: (number * 21846) >> 16
    if half == 0:
        indices = [third(lane), jnp.where(lane < 96, third(lane + 128), 128 - third(130 - lane))]
    else:
        indices = [jnp.where(lane < 32, third(lane), third(lane + 128)), third(lane + 256)]
    return jnp.concatenate([gather(value, index) for index in indices], 1)


def restrict_lanes(half, value):
    three = value + rolled(value, -1, 1) + rolled(value, -2, 1)
    lane = lanes((8, 128))
    index = (lane * RATIO) & 127
    tiles = [gather(three[:, 128 * tile : 128 * (tile + 1)], index) for tile in range(2)]
    in_first = lane * RATIO < (128 if half == 0 else 256)
    return jnp.where(in_first, tiles[0], tiles[1]) * (1.0 / RATIO**3)


def sort_messages(received, sorted_refs):
    even = lax.rem(lax.axis_index("gx"), 2) == 0
    first, second = received
    from_left, from_right = sorted_refs
    for plane in range(first.shape[0]):
        from_left[plane] = jnp.where(even, second[plane], first[plane])
        from_right[plane] = jnp.where(even, first[plane], second[plane])
    return from_left, from_right


def interface_rows(ce):
    return jnp.concatenate([ce[k, r][0:1] for k in range(2) for r in range(CROWS)], 0)


def top_plane(pl_ref, x, t):
    r = x // RATIO
    out = []
    for k in range(2):
        row = 2 * k + r
        value = pl_ref[row : row + 1, :]
        if t:
            value = value + float(t) * pl_ref[4 + row : 5 + row, :]
        out.append(value)
    return out


def lookup(tab, row, index):
    entry = jnp.broadcast_to(tab[row : row + 1, :], (8, 128))
    rows = []
    for z in range(0, Z, 8):
        rows.append(
            jnp.concatenate(
                [
                    gather(entry, index[z : z + 8, lane : lane + 128])
                    for lane in range(0, index.shape[1], 128)
                ],
                1,
            )
        )
    return jnp.concatenate(rows, 0)


def row_of(ref, x):
    return [ref[k, x] for k in range(3)]


def send_edges(half, first, fields, c, ce, ch, pl_ref, mat, to_first, to_second):
    fe, fh, fj, fp, fv = fields
    none = (None, None)
    e_items, h_items = x_items(first)
    coef = lambda x: [c[k, x] for k in range(6)]
    states = lambda x: (row_of(fj, x), row_of(fp, x), row_of(fv, x))
    e0 = {x: row_of(fe, x) for x in range(ROWS)}
    low, high = {}, {}

    for k in (1, 2):
        low["e", 0, k] = e0[0][k]
    h1 = {x: h_row(row_of(fh, x), e0[x], e0[x + 1][1:], top_plane(pl_ref, x, 0)) for x in (0, 1)}
    e1, s1 = {}, {}
    e1[0], *s1[0] = e_row(e0[0], h1[0], none, *states(0), coef(0))
    e1[1], *s1[1] = e_row(e0[1], h1[1], h1[0][1:], *states(1), coef(1), (1, 2))
    h2 = h_row(h1[0], e1[0], e1[1][1:], top_plane(pl_ref, 0, 1))
    e2 = e_row(e1[0], h2, none, *s1[0], coef(0), (1, 2))[0]
    for k in (1, 2):
        low["e", 1, k] = e1[0][k]
        low["e", 2, k] = e2[k]
        low["c", 0, k] = ce[k, 0]

    a, b, d = ROWS - 3, ROWS - 2, ROWS - 1
    h1 = {
        a: h_row(row_of(fh, a), e0[a], e0[b][1:], top_plane(pl_ref, a, 0), (1, 2)),
        b: h_row(row_of(fh, b), e0[b], e0[d][1:], top_plane(pl_ref, b, 0)),
        d: h_row(row_of(fh, d), e0[d], none, top_plane(pl_ref, d, 0)),
    }
    e1, s1 = {}, {}
    e1[b], *s1[b] = e_row(e0[b], h1[b], h1[a][1:], *states(b), coef(b))
    e1[d], *s1[d] = e_row(e0[d], h1[d], h1[b][1:], *states(d), coef(d))
    h2 = {
        b: h_row(h1[b], e1[b], e1[d][1:], top_plane(pl_ref, b, 1), (1, 2)),
        d: h_row(h1[d], e1[d], none, top_plane(pl_ref, d, 1)),
    }
    e2 = e_row(e1[d], h2[d], h2[b][1:], *s1[d], coef(d))[0]
    h3 = h_row(h2[d], e2, none, top_plane(pl_ref, d, 2), (1, 2))
    ch_last = h_row(row_of(ch, CROWS - 1), row_of(ce, CROWS - 1), none, (0.0, 0.0), (1, 2))
    for k in (1, 2):
        high["h", 0, k] = h1[d][k]
        high["h", 1, k] = h2[d][k]
        high["h", 2, k] = h3[k]
        high["c", 0, k] = ch_last[k]
    if first:
        low["m", 0, 0] = mat[0]
        high["m", 0, 0] = mat[ROWS - 1]
    even = lax.rem(lax.axis_index("gx"), 2) == 0
    for first_part, second_part, plane in zip(write_x(half, h_items, high), write_x(half, e_items, low), range(99)):
        to_first[plane] = jnp.where(even, first_part, second_part)
        to_second[plane] = jnp.where(even, second_part, first_part)


def start_kernel(half, *refs):
    fields_in, (c_in, mat_in, ce_in, ch_in, cmat, prior, tab) = refs[0:5], refs[5:12]
    received, fields = refs[12:14], refs[14:19]
    c, ce, ch, inv, pl_ref, to_first, to_second, mat, message = refs[19:28]
    even = lax.rem(lax.axis_index("gy"), 2) == 0
    swap = even if half == 0 else jnp.logical_not(even)
    for plane in range(Y_PLANES):
        message[plane] = jnp.where(swap, received[1][plane], received[0][plane])
    outer = slice(128, 256) if half == 0 else slice(0, 128)
    inner = slice(0, 128) if half == 0 else slice(128, 256)
    for x in (0, ROWS - 1):
        mat[x, :, outer] = with_ghosts(half, message, ("m", 0, 0, x), mat_in[x, :, outer])
        mat[x, :, inner] = mat_in[x, :, inner]
    (packed_plane,) = {Y_SLOTS["m", 0, 0, x][0] for x in range(ROWS)}
    index = jnp.clip(message[packed_plane].astype(jnp.int32), 0, 127)
    for k in range(6):
        packed = {packed_plane: lookup(tab, k, index)}
        for x in range(ROWS):
            c[k, x, :, outer] = with_ghosts(half, packed, ("m", 0, 0, x), c_in[k, x, :, outer])
    for a in range(5):
        for k in range(3):
            for x in range(ROWS):
                fields[a][k, x, :, outer] = with_ghosts(
                    half, message, ("f", a, k, x), fields_in[a][k, x, :, outer]
                )
    for a, (source, target) in enumerate(((ce_in, ce), (ch_in, ch))):
        for k in range(3):
            for r in range(CROWS):
                target[k, r] = with_ghosts(half, message, ("c", a, k, r), coarse_row(source, k, r))
    for r in range(CROWS):
        value = cmat[pl.ds(r, Z, stride=CROWS), :].astype(F32)
        index = with_ghosts(half, message, ("cm", 0, 0, r), value).astype(jnp.int32)
        inv[r] = lookup(tab, 7, jnp.clip(index, 0, 127))
    before = jnp.concatenate([prior[...]] * (Z // 4), 0)
    before = with_ghosts(half, message, ("prior", 0, 0, 0), before)[0:4]
    interface = interface_rows(ce)
    increment = (interface - before) * (1.0 / RATIO)
    pl_ref[...] = prolong_lanes(half, jnp.concatenate([interface, increment], 0))
    send_edges(half, True, fields, c, ce, ch, pl_ref, mat, to_first, to_second)


def coarse_step(half, first, olds, news, c, ghost, olds_c, news_c, inv, pl_ref, from_left, from_right, finished=None, merged=None):
    e_items, h_items = x_items(first)
    zero = jnp.zeros((Z, W), F32)
    flat = (0.0, 0.0)
    (ce0, ch0), (ce, ch) = olds_c, news_c
    coarse_e0 = [row_of(ce0, r) for r in range(CROWS)]
    up = [read_x(from_right, half, e_items, ("c", 0, k)) for k in (1, 2)]
    down = [read_x(from_left, half, h_items, ("c", 0, k)) for k in (1, 2)]
    down = [down[0] + COURANT * coarse_e0[0][2], down[1] - COURANT * coarse_e0[0][1]]
    coarse_h = []
    for r in range(CROWS):
        following = coarse_e0[r + 1][1:] if r + 1 < CROWS else up
        coarse_h.append(h_row(row_of(ch0, r), coarse_e0[r], following, flat))
        for k in range(3):
            ch[k, r] = coarse_h[r][k]
    if finished:
        finished((6,))

    ge = gh = he = hh = None
    summed = [[None] * CROWS for _ in range(2)]
    for t in range(RATIO):
        fe, fh, fj, fp, fv = olds if t == 0 else news
        e_first = row_of(fe, 0)
        following = [read_x(from_right, half, e_items, ("e", t, k)) for k in (1, 2)]
        if t:
            following = [base + more for base, more in zip(following, he[1:])]
        far = [None, None]
        if t == 0:
            gh = [None, COURANT * e_first[2], -COURANT * e_first[1]]
        else:
            far = [COURANT * ge[2], -COURANT * ge[1]]
            old = [zero if value is None else value for value in gh]
            gh = h_row(old, ge, e_first[1:], flat, (0, 1, 2) if t < RATIO - 1 else (1, 2))
        preceding = [read_x(from_left, half, h_items, ("h", t, k)) + gh[k] for k in (1, 2)]
        current = e_first
        last = finished is not None and t == RATIO - 1
        if last:
            for x in range(ROWS):
                for k in range(3):
                    v2 = c[3, x] * fv[k, x] + c[4, x] * (c[5, x] * fe[k, x] - fp[k, x])
                    news[2][k, x] = merged(2, k, x, c[1, x] * fj[k, x] + c[2, x] * fe[k, x])
                    news[3][k, x] = merged(3, k, x, fp[k, x] + TIMESTEP * v2)
                    news[4][k, x] = merged(4, k, x, v2)
            finished((2, 3, 4))
        for x in range(ROWS):
            upper = row_of(fe, x + 1) if x + 1 < ROWS else None
            h = h_row(
                row_of(fh, x), row_of(fe, x), upper[1:] if upper else following, top_plane(pl_ref, x, t)
            )
            for k in range(3):
                news[1][k, x] = merged(1, k, x, h[k]) if last else h[k]
            for k in range(2):
                part = h[k][8:Z]
                have = summed[k][x // RATIO]
                summed[k][x // RATIO] = part if have is None else have + part
        if last:
            finished((1,))
        for x in range(ROWS):
            h = row_of(news[1], x)
            if last:
                curl = curl_h(h, preceding, flat)
                for k in range(3):
                    e2 = fe[k, x] + c[0, x] * (curl[k] - fj[k, x] - fv[k, x])
                    news[0][k, x] = merged(0, k, x, e2)
                preceding = h[1:]
                continue
            e2, j2, p2, v2 = e_row(
                row_of(fe, x), h, preceding, row_of(fj, x), row_of(fp, x), row_of(fv, x), [c[k, x] for k in range(6)]
            )
            for k in range(3):
                news[0][k, x] = e2[k]
                news[2][k, x] = j2[k]
                news[3][k, x] = p2[k]
                news[4][k, x] = v2[k]
            preceding = h[1:]
        if last:
            finished((0,))
        if t == 0:
            (a, b), (a2, b2) = [[ghost[k, side] for k in range(2)] for side in range(2)]
            ge = [
                a * ((gh[2] - left(gh[2])) - (gh[1] - below(gh[1], 0.0))),
                -a * gh[2],
                a * gh[1],
            ]
            he = [zero, a2 * preceding[1], -a2 * preceding[0]]
        elif t == 1:
            curl = curl_h(gh, far, flat)
            ge = [ge[k] + a * (curl[k] - b * ge[k]) for k in range(3)]
            hh = h_row([zero] * 3, he, (None, None), flat)
            curl = curl_h(hh, preceding, flat, (1, 2))
            he = [None] + [he[k] + a2 * (curl[k] - b2 * he[k]) for k in (1, 2)]

    rows = [summed[k][r][7:8] for k in range(2) for r in range(CROWS)]
    bottoms = restrict_lanes(half, jnp.concatenate(rows + rows, 0))
    preceding = down
    for r in range(CROWS):
        bottom = [bottoms[2 * k + r : 2 * k + r + 1, :] for k in range(2)]
        curl = curl_h(coarse_h[r], preceding, bottom)
        for k in range(3):
            ce[k, r] = coarse_e0[r][k] + inv[r] * curl[k]
        preceding = coarse_h[r][1:]
    if finished:
        finished((5,))


def ghost_coefficients(half, ghost, tab, from_left, from_right):
    e_items, h_items = x_items(True)
    for side, (ref, items) in enumerate(((from_left, h_items), (from_right, e_items))):
        index = jnp.clip(read_x(ref, half, items, ("m", 0, 0)).astype(jnp.int32), 0, 127)
        ghost[0, side] = lookup(tab, 0, index)
        ghost[1, side] = lookup(tab, 6, index)


def step_kernel(half, first, *refs):
    olds, rest = refs[0:5], refs[5:]
    c, ce0, ch0, inv, pl0, ghost_in = rest[0:6]
    from_left, from_right = sort_messages(rest[6:8], rest[-2:])
    news, rest = rest[8:13], rest[13:-2]
    if first:
        ce, ch, pl_ref, to_first, to_second, ghost = rest
        ghost_coefficients(half, ghost, ghost_in, from_left, from_right)
    else:
        ce, ch, pl_ref, to_first, to_second = rest
        ghost = ghost_in
    coarse_step(half, first, olds, news, c, ghost, (ce0, ch0), (ce, ch), inv, pl0, from_left, from_right)
    interface = interface_rows(ce)
    increment = (interface - interface_rows(ce0)) * (1.0 / RATIO)
    pl_ref[...] = prolong_lanes(half, jnp.concatenate([interface, increment], 0))
    send_edges(half, False, news, c, ce, ch, pl_ref, None, to_first, to_second)


def final_kernel(half, *refs):
    olds, rest = refs[0:5], refs[5:]
    c, ce0, ch0, inv, pl0, ghost = rest[0:6]
    received, rest = rest[6:8], rest[8:]
    if half == 0:
        outs, news, ce, ch = rest[0:5], rest[5:10], rest[10], rest[11]
        rest = rest[12:]
    else:
        others, others_c = rest[5:10], rest[10:12]
        outs, outs_c, news, ce, ch = rest[12:17], rest[17:19], rest[19:24], rest[24], rest[25]
        coarse_parts = rest[26:28]
        rest = rest[28:]
    sorted_refs, sems = rest[0:2], rest[2]
    from_left, from_right = sort_messages(received, sorted_refs)
    first = lanes((Z, 128)) < 64
    copies = []

    def coarse_finished(a):
        if half == 0:
            return
        for k in range(3):
            for r in range(CROWS):
                value = jnp.where(first, others_c[a][k, r], (ce, ch)[a][k, r])
                coarse_parts[a][k, pl.ds(r, Z, stride=CROWS), :] = value
        copies.append(pltpu.make_async_copy(coarse_parts[a], outs_c[a], sems.at[5 + a]))
        copies[-1].start()

    def merged(a, k, x, value):
        if half == 0:
            return value
        shared = jnp.where(first, others[a][k, x, :, 128:256], value[:, 0:128])
        return jnp.concatenate([shared, value[:, 128:256]], 1)

    def finished(arrays):
        for a in arrays:
            if a >= 5:
                coarse_finished(a - 5)
                continue
            if half == 0:
                source, target = news[a].at[:, :, :, 0:128], outs[a].at[:, :, :, 0:128]
            else:
                source, target = news[a], outs[a].at[:, :, :, 128:384]
            copies.append(pltpu.make_async_copy(source, target, sems.at[a]))
            copies[-1].start()

    coarse_step(
        half, False, olds, news, c, ghost, (ce0, ch0), (ce, ch), inv, pl0, from_left, from_right, finished, merged
    )
    for copy in copies:
        copy.wait()


FULL = pl.BlockSpec(memory_space=pltpu.VMEM)
RAW = pl.BlockSpec(memory_space=pltpu.HBM)
COST = pl.CostEstimate(flops=4_000_000, transcendentals=0, bytes_accessed=8_000_000)
FIELD = (3, ROWS, Z, W)
COEF = (6, ROWS, Z, W)
COARSE = (3, CROWS, Z, CW)
PLANES = (8, W)


def call(kernel, outs, args, specs=None, scratch=(), aliases=None, vmem=16, out_specs=None):
    outs = [dims if isinstance(dims, jax.ShapeDtypeStruct) else jax.ShapeDtypeStruct(dims, F32) for dims in outs]
    return pl.pallas_call(
        kernel,
        out_shape=outs,
        in_specs=specs or [FULL] * len(args),
        out_specs=out_specs or [FULL] * len(outs),
        scratch_shapes=list(scratch),
        input_output_aliases=aliases or {},
        compiler_params=pltpu.CompilerParams(vmem_limit_bytes=vmem * 1024 * 1024),
        cost_estimate=COST,
    )(*args)


def table(permittivity, plasma, damping, strength, resonance, linewidth):
    half_step = 0.5 * TIMESTEP
    c2 = plasma * plasma * TIMESTEP / (1.0 + damping * half_step)
    c4 = TIMESTEP * resonance * resonance / (1.0 + linewidth * half_step)
    rows = jnp.stack(
        [
            TIMESTEP / permittivity,
            (1.0 - damping * half_step) / (1.0 + damping * half_step),
            c2,
            (1.0 - linewidth * half_step) / (1.0 + linewidth * half_step),
            c4,
            strength,
            c2 + c4 * strength,
            COURANT / permittivity,
        ]
    )
    return jnp.pad(rows, ((0, 0), (0, 120)))


def message_shapes(half, first):
    return [(x_places(half, items)[1], Z, 128) for items in x_items(first)]


def exchanged(messages, axis):
    count = lax.axis_size(axis)
    swapped = []
    for message, first in zip(messages, (0, 1)):
        pairs = [((first + i) % count, (first + (i ^ 1)) % count) for i in range(count)]
        swapped.append(lax.ppermute(message, axis, pairs))
    return swapped


def local(
    fine_e,
    fine_h,
    drude_current,
    lorentz_pol,
    lorentz_rate,
    material,
    permittivity,
    plasma,
    damping,
    strength,
    resonance,
    linewidth,
    coarse_e,
    coarse_h,
    coarse_material,
    coarse_prior,
):
    fields = [
        jnp.transpose(value, (0, 2, 1, 3))
        for value in (fine_e, fine_h, drude_current, lorentz_pol, lorentz_rate)
    ]
    mat = jnp.transpose(material, (1, 0, 2))
    ce = coarse_e.reshape(3, Z * CROWS, 128)
    ch = coarse_h.reshape(3, Z * CROWS, 128)
    cmat = coarse_material.reshape(Z * CROWS, 128)
    prior = coarse_prior.reshape(2 * CROWS, 128)
    in_hbm = lambda values: [pltpu.with_memory_space_constraint(value, pltpu.HBM) for value in values]
    fields, coarse = in_hbm(fields), in_hbm([ce, ch, cmat, prior])
    (mat,) = in_hbm([mat])
    tab = table(permittivity, plasma, damping, strength, resonance, linewidth)

    vmem = lambda *dims: pltpu.VMEM(dims, F32)
    packed = call(
        pack_y_kernel,
        [(Y_PLANES, Z, 128)] * 2,
        [*fields, mat, *coarse],
        [RAW] * 10,
        [
            vmem(5, 3, ROWS, Z, 128),
            vmem(5, 3, ROWS, Z, 128),
            pltpu.VMEM((2, ROWS, Z, 128), jnp.int32),
            vmem(*ce.shape),
            vmem(*ch.shape),
            pltpu.VMEM(cmat.shape, jnp.int32),
            vmem(*prior.shape),
            pltpu.SemaphoreType.DMA((16,)),
        ],
        vmem=16,
    )
    received = exchanged(packed, "gy")
    loaded = call(
        load_kernel,
        [FIELD] * 10
        + [COEF] * 2
        + [(ROWS, Z, W)] * 2
        + [jax.ShapeDtypeStruct(value.shape, value.dtype) for value in coarse],
        [*fields, mat, *coarse, tab],
        [RAW] * 10 + [FULL],
        [pltpu.VMEM((ROWS, Z, OWN), jnp.int32), pltpu.SemaphoreType.DMA((15,))],
    )
    parts, waiting = [None, None], [None, None]
    for half in range(2):
        state = loaded[5 * half : 5 * half + 5]
        out = call(
            functools.partial(start_kernel, half),
            [FIELD] * 5 + [COEF, COARSE, COARSE, (CROWS, Z, CW), PLANES] + message_shapes(half, True),
            [*state, loaded[10 + half], loaded[12 + half], *loaded[14:18], tab, *received],
            scratch=[vmem(ROWS, Z, W), vmem(Y_PLANES, Z, 128)],
            aliases={index: index for index in range(6)},
        )
        parts[half] = (out[0:5], out[5:10], tab)
        waiting[half] = exchanged(out[10:12], "gx")
    for step in range(STEPS - 1):
        for half in range(2):
            state, (c, ce, ch, inv, planes), ghost = parts[half]
            out = call(
                functools.partial(step_kernel, half, step == 0),
                [FIELD] * 5
                + [COARSE, COARSE, PLANES]
                + message_shapes(half, False)
                + ([(2, 2, Z, W)] if step == 0 else []),
                [*state, c, ce, ch, inv, planes, ghost, *waiting[half]],
                scratch=[vmem(*message.shape) for message in waiting[half]],
            )
            if step == 0:
                ghost = out[10]
            parts[half] = (out[0:5], (c, out[5], out[6], inv, out[7]), ghost)
            waiting[half] = exchanged(out[8:10], "gx")
    whole = [(3, ROWS, Z, OWN)] * 5
    done = []
    for half in range(2):
        state, coarse, ghost = parts[half]
        args = [*state, *coarse, ghost, *waiting[half], *done]
        done = call(
            functools.partial(final_kernel, half),
            whole + ([(3, Z * CROWS, 128)] * 2 if half else [FIELD] * 5 + [COARSE] * 2),
            args,
            specs=[RAW if 13 <= i < 18 else FULL for i in range(len(args))],
            out_specs=[RAW] * 7 if half else [RAW] * 5 + [FULL] * 7,
            scratch=([vmem(*FIELD)] * 5 + [vmem(*COARSE)] * 2 + [vmem(3, Z * CROWS, 128)] * 2 if half else [])
            + [vmem(*message.shape) for message in waiting[half]]
            + [pltpu.SemaphoreType.DMA((7,))],
            aliases={13 + i: i for i in range(5)} if half else None,
        )
    fine = [jnp.transpose(value, (0, 2, 1, 3)) for value in done[0:5]]
    coarse = [value.reshape(3, Z, CROWS, 128) for value in done[5:7]]
    return (*fine, *coarse)


def solution(mesh):
    field = P(None, None, "gx", "gy")
    plane = P(None, "gx", "gy")
    in_specs = (field,) * 5 + (plane,) + (P(),) * 6 + (field, field, plane, plane)
    return jax.shard_map(local, mesh=mesh, in_specs=in_specs, out_specs=(field,) * 7, check_vma=False)
```
